32 devices in a mesh: pipe: 2 (over y), dp: 8 (over z, x), tensor: 2 (over core).
Axes of the slice: x: 2, y: 2, z: 4, core: 2. Of those that a mesh axis runs over, the one named last changes fastest.
Arguments:
- boundary: bfloat16 [2, 8192, 1536], P('pipe', 'dp', 'tensor'), may hold values from -6 to 6
- norm_gain: float32 [2, 1536], P('pipe'), may hold values from 0.5 to 1.5
- in_zx: bfloat16 [2, 1536, 2, 3072], P('pipe', 'dp', None, 'tensor'), may hold values from -0.15625 to 0.15625
- in_bc: bfloat16 [2, 1536, 256], P('pipe', 'dp'), may hold values from -0.15625 to 0.15625
- in_dt: bfloat16 [2, 1536, 48], P('pipe', 'dp', 'tensor'), may hold values from -0.15625 to 0.15625
- conv_x: float32 [2, 5, 3072], P('pipe', None, 'tensor'), may hold values from -0.5 to 0.5
- conv_bc: float32 [2, 5, 256], P('pipe'), may hold values from -0.5 to 0.5
- dt_bias: float32 [2, 48], P('pipe', 'tensor'), may hold values from -5 to -2
- a_log: float32 [2, 48], P('pipe', 'tensor'), may hold values from 0 to 2.77
- d_skip: float32 [2, 48], P('pipe', 'tensor'), may hold values from 0.5 to 1.5
- gate_gain: float32 [2, 3072], P('pipe', 'tensor'), may hold values from 0.5 to 1.5
- out_w: bfloat16 [2, 3072, 1536], P('pipe', 'tensor', 'dp'), may hold values from -0.109375 to 0.109375
Outputs:
- ends: bfloat16 [2, 8192, 1536], P('pipe', 'dp', 'tensor')
- g_norm_gain: float32 [2, 1536], P('pipe')
- g_in_zx: float32 [2, 1536, 2, 3072], P('pipe', 'dp', None, 'tensor')
- g_in_bc: float32 [2, 1536, 256], P('pipe', 'dp')
- g_in_dt: float32 [2, 1536, 48], P('pipe', 'dp', 'tensor')
- g_conv_x: float32 [2, 5, 3072], P('pipe', None, 'tensor')
- g_conv_bc: float32 [2, 5, 256], P('pipe')
- g_dt_bias: float32 [2, 48], P('pipe', 'tensor')
- g_a_log: float32 [2, 48], P('pipe', 'tensor')
- g_d_skip: float32 [2, 48], P('pipe', 'tensor')
- g_gate_gain: float32 [2, 3072], P('pipe', 'tensor')
- g_out_w: float32 [2, 3072, 1536], P('pipe', 'tensor', 'dp')
The draws below stay inside these ranges and needn't reach their ends.
All inputs are finite; a program needn't handle non-finite values.
Results may differ from the reference program's by a relative error of at most 0.0173.
Values may be sent and summed in bfloat16 or wider, within the bound.
No kernel may reach another device: no remote copies, remote signals or barrier semaphores. Data moves between devices by JAX's collectives and lax.ppermute only.
A program may use at most 448 MiB of HBM per device.

```python
import jax
import jax.numpy as jnp
from jax import lax

D = 1536
NH = 48
STATE = 128
KCONV = 4
BLOCK = 256
LEN = 512
DI = 3072
SECTIONS = 2
TOKENS = 8192


def steps_of(stream_key, shape, pieces, least, largest):
    factor_of, own = 1.0, jax.random.fold_in(stream_key, 6)
    for position, shards_of in pieces:
        steps = jnp.exp(jax.random.uniform(jax.random.fold_in(own, position), (shards_of,), jnp.float32, least / len(pieces), largest / len(pieces)))
        factor_of = factor_of * jnp.repeat(steps, shape[position] // shards_of).reshape([-1 if axis == position else 1 for axis in range(len(shape))])
    return factor_of


def bell_draw(stream_key, extent, deviation, bound, pieces=(), kind=jnp.bfloat16):
    values = deviation * jax.random.normal(stream_key, extent, jnp.float32)
    if pieces:
        values = values * steps_of(stream_key, extent, pieces, -0.22, 0.18)
    return jnp.clip(values, -bound, bound).astype(kind)


def setup_inputs(seed: int = 0) -> dict:
    key_list = jax.random.split(jax.random.key(seed), 13)
    return {
        "boundary": bell_draw(key_list[0], (2, TOKENS, D), 1.0, 6.0, ((0, 2), (1, 8), (2, 2))),
        "norm_gain": jnp.clip(1.0 + 0.1 * jax.random.normal(key_list[1], (2, D), jnp.float32), 0.5, 1.5),
        "in_zx": bell_draw(key_list[2], (2, D, 2, DI), D ** -0.5, 0.15625, ((0, 2), (1, 8), (3, 2))),
        "in_bc": bell_draw(key_list[3], (2, D, 2 * STATE), D ** -0.5, 0.15625, ((0, 2), (1, 8))),
        "in_dt": bell_draw(key_list[4], (2, D, NH), D ** -0.5, 0.15625, ((0, 2), (1, 8), (2, 2))),
        "conv_x": jnp.clip(jax.random.uniform(key_list[5], (2, KCONV + 1, DI), jnp.float32, -0.5, 0.5) * steps_of(key_list[5], (2, KCONV + 1, DI), ((0, 2), (2, 2)), -0.4, 0.0), -0.5, 0.5),
        "conv_bc": jnp.clip(jax.random.uniform(key_list[6], (2, KCONV + 1, 2 * STATE), jnp.float32, -0.5, 0.5) * steps_of(key_list[6], (2, KCONV + 1, 2 * STATE), ((0, 2),), -0.4, 0.0), -0.5, 0.5),
        "dt_bias": jnp.clip(-5.0 + 3.0 * jax.random.uniform(key_list[7], (2, NH), jnp.float32) ** steps_of(key_list[7], (2, NH), ((0, 2), (1, 2)), -0.2, 0.2), -5.0, -2.0),
        "a_log": jnp.clip(2.77 * jax.random.uniform(key_list[8], (2, NH), jnp.float32) ** steps_of(key_list[8], (2, NH), ((0, 2), (1, 2)), -0.2, 0.2), 0.0, 2.77),
        "d_skip": jnp.clip(0.5 + 1.0 * jax.random.uniform(key_list[9], (2, NH), jnp.float32) ** steps_of(key_list[9], (2, NH), ((0, 2), (1, 2)), -0.2, 0.2), 0.5, 1.5),
        "gate_gain": jnp.clip(1.0 + 0.1 * jax.random.normal(key_list[10], (2, DI), jnp.float32), 0.5, 1.5),
        "out_w": bell_draw(key_list[11], (2, DI, D), DI ** -0.5, 0.109375, ((0, 2), (1, 2), (2, 8))),
    }


EPS = 1e-05
HIGH = lax.Precision.HIGHEST

@jax.custom_vjp
def low(v):
    return lax.optimization_barrier(v.astype(jnp.bfloat16)).astype(jnp.float32)

@jax.custom_vjp
def low_back(v):
    return v

def low_keep(v):
    return (low(v), None)

def low_pass(kept, grad):
    return (grad,)

def back_keep(v):
    return (v, None)

def back_low(kept, grad):
    return (low(grad),)
low.defvjp(low_keep, low_pass)
low_back.defvjp(back_keep, back_low)

def causal_conv(signal, kernel_rows):
    taps_count = kernel_rows.shape[0] - 1
    length = signal.shape[0]
    padded = jnp.pad(signal, ((taps_count - 1, 0), (0, 0)))
    running = jnp.broadcast_to(kernel_rows[taps_count], signal.shape)
    for offset in range(taps_count):
        running = running + kernel_rows[offset] * padded[offset:offset + length]
    return running

def shared_conv(signal, kernel_rows):
    return jax.nn.silu(causal_conv(signal, kernel_rows))

def ssd_scan(values, step_sizes, decay_rate, bmatrix, cmatrix, block_size):
    length, head_count, head_size = values.shape
    blocks = length // block_size
    values = values.reshape(blocks, block_size, head_count, head_size)
    step_sizes = step_sizes.reshape(blocks, block_size, head_count)
    bmatrix = bmatrix.reshape(blocks, block_size, -1)
    cmatrix = cmatrix.reshape(blocks, block_size, -1)
    cumulative = jnp.cumsum(step_sizes * decay_rate, axis=1)
    cum_heads = jnp.transpose(cumulative, (0, 2, 1))
    places = jnp.arange(block_size)
    causal = (places[:, None] >= places[None, :])[None, None, :, :]
    scores = jnp.einsum('cin,cjn->cij', cmatrix, bmatrix, precision=HIGH)
    steps_heads = jnp.transpose(step_sizes, (0, 2, 1))
    spread = jnp.where(causal, cum_heads[:, :, :, None] - cum_heads[:, :, None, :], 0.0)
    mixer = jnp.where(causal, scores[:, None, :, :] * jnp.exp(spread) * steps_heads[:, :, None, :], 0.0)
    inside = jnp.einsum('chij,cjhp->cihp', mixer, values, precision=HIGH)
    to_end = jnp.exp(cumulative[:, -1:, :] - cumulative) * step_sizes
    scaled = values * to_end[:, :, :, None]
    states = jnp.einsum('cjhp,cjn->chpn', scaled, bmatrix, precision=HIGH)
    carried = jnp.exp(cumulative[:, -1, :])

    def advance(state, step_pair):
        factor, fresh = step_pair
        return (state * factor[:, None, None] + fresh, state)
    ignored, entering = lax.scan(advance, jnp.zeros(states.shape[1:], jnp.float32), (carried, states))
    outside = jnp.einsum('cin,chpn->cihp', cmatrix, entering, precision=HIGH) * jnp.exp(cumulative)[:, :, :, None]
    return (inside + outside).reshape(length, head_count, head_size)

def mixer_core(gate_in, value_in, step_in, shared, conv_heads, bias_step, log_decay, skip_gain):
    length = value_in.shape[0]
    state_size = shared.shape[1] // 2
    head_count = bias_step.shape[0]
    convolved = jax.nn.silu(causal_conv(value_in, conv_heads))
    step_sizes = jax.nn.softplus(step_in + bias_step)
    head_rows = convolved.reshape(length, head_count, -1)
    mixed = ssd_scan(head_rows, step_sizes, -jnp.exp(log_decay), shared[:, :state_size], shared[:, state_size:], BLOCK)
    mixed = mixed + skip_gain[None, :, None] * head_rows
    return mixed.reshape(length, -1) * jax.nn.silu(gate_in)

def pre_norm(rows, gain):
    return rows * lax.rsqrt(lax.optimization_barrier(jnp.mean(rows * rows, axis=-1, keepdims=True)) + EPS) * gain

def mamba_layer(hidden, norm_gain, in_zx, in_bc, in_dt, conv_x, conv_bc, dt_bias, a_log, d_skip, gate_gain, out_w):
    inner_width = gate_gain.shape[0]
    state_cols = in_bc.shape[1]
    normed = low(pre_norm(hidden, norm_gain))
    weight_all = jnp.concatenate([in_zx.reshape(in_zx.shape[0], -1), in_bc, in_dt], axis=1)
    projected = low_back(jnp.dot(normed, weight_all, precision=HIGH, preferred_element_type=jnp.float32))
    gate_in = projected[:, :inner_width]
    value_in = projected[:, inner_width:2 * inner_width]
    shared_in = projected[:, 2 * inner_width:2 * inner_width + state_cols]
    step_in = projected[:, 2 * inner_width + state_cols:]
    shared = shared_conv(shared_in, conv_bc)
    gated = mixer_core(gate_in, value_in, step_in, shared, conv_x, dt_bias, a_log, d_skip)
    gate_norm = low(gated * lax.rsqrt(lax.optimization_barrier(jnp.mean(gated * gated, axis=-1, keepdims=True)) + EPS) * gate_gain)
    return hidden + jnp.dot(gate_norm, out_w, precision=HIGH, preferred_element_type=jnp.float32)

def forward(inputs, weights):
    hidden = inputs.reshape(-1, LEN, inputs.shape[1])
    for section_index in range(SECTIONS):
        section_weights = tuple((item[section_index] for item in weights))

        def one_sequence(sequence, chosen=section_weights):
            return mamba_layer(sequence, *chosen)
        hidden = lax.map(jax.checkpoint(one_sequence), hidden)
        if section_index + 1 < SECTIONS:
            hidden = low(low_back(hidden))
    return hidden.reshape(inputs.shape)

def reference(boundary, norm_gain, in_zx, in_bc, in_dt, conv_x, conv_bc, dt_bias, a_log, d_skip, gate_gain, out_w):
    weights = tuple((item.astype(jnp.float32) for item in (norm_gain, in_zx, in_bc, in_dt, conv_x, conv_bc, dt_bias, a_log, d_skip, gate_gain, out_w)))
    inputs = boundary[0].astype(jnp.float32)
    cotangent = boundary[1].astype(jnp.float32)
    result, pullback = jax.vjp(forward, inputs, weights)
    d_inputs, gradients = pullback(cotangent)
    ends = jnp.stack([d_inputs, result]).astype(jnp.bfloat16)
    return (ends, gradients[0], gradients[1], gradients[2], gradients[3], gradients[4], gradients[5], gradients[6], gradients[7], gradients[8], gradients[9], gradients[10])
```

```python
import functools
import jax
import jax.numpy as jnp
from jax import lax
from jax.experimental import pallas as pl
from jax.experimental.pallas import tpu as pltpu
from jax.sharding import PartitionSpec as P

LEN = 512
Q = 128
GW = 256
HS = 64
EPS = 1e-05
LOG2E = 1.4426950408889634
F32 = jnp.float32
BF16 = jnp.bfloat16
NEG = -1e30


def mm(a, b):
    return jnp.dot(a, b, preferred_element_type=F32)


def mm_nt(a, b):
    return lax.dot_general(a, b, (((1,), (1,)), ((), ())), preferred_element_type=F32)


def mm_tn(a, b):
    return lax.dot_general(a, b, (((0,), (0,)), ((), ())), preferred_element_type=F32)


def halves(a):
    high = a.astype(BF16)
    return high, (a - high.astype(F32)).astype(BF16)


def mm_split(a, b):
    high, rest = halves(a)
    return mm(high, b) + mm(rest, b)


def sigmoid(a):
    return 1.0 / (1.0 + jnp.exp2(a * (-LOG2E)))


def iota2(shape, axis):
    return lax.broadcasted_iota(jnp.int32, shape, axis)


def spread_matrix(transposed=False):
    if transposed:
        return (iota2((GW, Q), 0) // HS == iota2((GW, Q), 1)).astype(F32).astype(BF16)
    return (iota2((Q, GW), 1) // HS == iota2((Q, GW), 0)).astype(F32).astype(BF16)


def lower_ones():
    return (iota2((Q, Q), 0) >= iota2((Q, Q), 1)).astype(F32)


def shifted(ext, by):
    if by == 0:
        return ext[8:, :]
    return pltpu.roll(ext, by, 0)[8:, :]


def conv_at(pad_ref, start, taps):
    ext = pad_ref[pl.ds(pl.multiple_of(start, 8), Q + 8), :]
    out = taps[4:5, :]
    for j in range(4):
        out = out + taps[j : j + 1, :] * shifted(ext, 3 - j)
    return out


def load_pieces(pieces1, pieces2, wbuf, obuf, sem1, sem2, groups):
    inner = groups * GW
    gate, outer = [], []
    for g in range(groups):
        mine, row = [], 0
        for k, piece in enumerate(pieces1):
            rows = piece.shape[0]
            for part in range(2):
                mine.append(
                    pltpu.make_async_copy(
                        piece.at[:, pl.ds(part * inner + g * GW, GW)],
                        wbuf.at[g, pl.ds(row, rows), pl.ds(part * GW, GW)],
                        sem1.at[g, k, part],
                    )
                )
            row += rows
        gate.append(mine)
        mine, row = [], 0
        for k, piece in enumerate(pieces2):
            rows = piece.shape[0]
            mine.append(
                pltpu.make_async_copy(
                    piece.at[:, pl.ds(g * GW, GW)],
                    obuf.at[g, pl.ds(row, rows), :],
                    sem2.at[g, k],
                )
            )
            row += rows
        outer.append(mine)
    return gate, outer


def fwd_kernel(n1, n2, top, groups, *refs):
    (h_ref, ng_ref, wbc_ref, wdt_ref, cx_ref, cbc_ref, dtb_ref, rate_ref, dsk_ref, gain_ref) = refs[:10]
    refs = refs[10:]
    if top:
        dout_ref, refs = refs[0], refs[1:]
    pieces1, refs = refs[:n1], refs[n1:]
    pieces2, refs = refs[:n2], refs[n2:]
    (p_ref, ss_ref, nrm_ref, gate_ref, val_ref, y_ref, shin_ref, stin_ref, ht_ref) = refs[:9]
    refs = refs[9:]
    if top:
        dot_ref, refs = refs[0], refs[1:]
    (wbuf, obuf, vpad, bsc, csc, btsc, ssc, cum, wx, ec, cjt, gn, hst, ssum, sem1, sem2) = refs[:16]
    dsum, dgn = refs[16:] if top else (None, None)
    g = pl.program_id(0)
    rows_all = h_ref.shape[0]
    chunks = rows_all // Q
    per_seq = LEN // Q

    def each_group(copies, act):
        for k in range(groups):

            @pl.when(g == k)
            def _():
                for c in copies[k]:
                    act(c)

    gate_copies, out_copies = load_pieces(pieces1, pieces2, wbuf, obuf, sem1, sem2, groups)

    @pl.when(g == 0)
    def _():
        for k in range(groups):
            for c in gate_copies[k] + out_copies[k]:
                c.start()

        def norm_rows(c, carry):
            rows = pl.ds(pl.multiple_of(c * Q, Q), Q)
            h = h_ref[rows, :].astype(F32)
            scale = lax.rsqrt(jnp.mean(h * h, axis=-1, keepdims=True) + EPS)
            nrm_ref[rows, :] = (h * scale * ng_ref[...]).astype(BF16)
            return carry

        lax.fori_loop(0, chunks, norm_rows, 0)
        ssum[...] = jnp.zeros_like(ssum)
        if top:
            dsum[...] = jnp.zeros_like(dsum)
        wide = 8 + LEN
        for s in range(rows_all // LEN):
            rows = pl.ds(s * LEN, LEN)
            normed = nrm_ref[rows, :]
            shin = mm(normed, wbc_ref[...])
            shin_ref[rows, :] = shin
            vpad[pl.ds(s * wide, 8), :] = jnp.zeros((8, GW), F32)
            vpad[pl.ds(s * wide + 8, LEN), :] = shin
            stin_ref[rows, :] = mm(normed, wdt_ref[...])
        tri = lower_ones()
        taps = cbc_ref[...]

        def shared_rows(c, carry):
            s, cc = c // per_seq, c % per_seq
            rows = pl.ds(pl.multiple_of(c * Q, Q), Q)
            pre = conv_at(vpad, s * wide + cc * Q, taps)
            act = (pre * sigmoid(pre)).astype(BF16)
            bmat, cmat = act[:, :Q], act[:, Q:]
            bt = bmat.astype(F32).T.astype(BF16)
            btsc[c] = bt
            csc[rows, :] = cmat
            ssc[c] = mm(cmat, bt)
            pre = stin_ref[rows, :] + dtb_ref[...]
            step = jnp.maximum(pre, 0.0) + jnp.log1p(jnp.exp(-jnp.abs(pre)))
            cumulative = jnp.dot(tri, step * rate_ref[...], precision=lax.Precision.HIGHEST, preferred_element_type=F32)
            cj = cumulative - jnp.log2(step)
            cum[rows, :] = cumulative
            ec[rows, :] = jnp.exp2(cumulative)
            wx[rows, :] = jnp.exp2(cumulative[Q - 1 : Q, :] - cj)
            cjt[c] = cj.T[:16, :]
            return carry

        lax.fori_loop(0, chunks, shared_rows, 0)

    each_group(gate_copies, lambda c: c.wait())
    each_group(out_copies, lambda c: c.wait())
    wide = 8 + LEN
    for s in range(rows_all // LEN):
        rows = pl.ds(s * LEN, LEN)
        normed = nrm_ref[rows, :]
        gate_ref[rows, :] = mm(normed, wbuf[g, :, :GW])
        value = mm(normed, wbuf[g, :, GW:])
        val_ref[rows, :] = value
        vpad[pl.ds(s * wide, 8), :] = jnp.zeros((8, GW), F32)
        vpad[pl.ds(s * wide + 8, LEN), :] = value
        if top:
            dgn[rows, :] = mm(dout_ref[rows, :], obuf[g])
    taps = cx_ref[...]
    spread = spread_matrix()
    shift = lax.rem(Q - 4 * g, Q)
    causal = iota2((Q, Q), 0) >= iota2((Q, Q), 1)
    lane = iota2((Q, Q), 1)

    def chunk(c, carry):
        s, cc = c // per_seq, c % per_seq
        rows = pl.ds(pl.multiple_of(c * Q, Q), Q)

        @pl.when(cc == 0)
        def _():
            hst[...] = jnp.zeros_like(hst)

        pre = conv_at(vpad, s * wide + cc * Q, taps)
        x = pre * sigmoid(pre)
        xb = x.astype(BF16)
        here = pltpu.roll(cum[rows, :], shift, 1)
        wxe = mm_split(pltpu.roll(wx[rows, :], shift, 1), spread)
        ece = mm_split(pltpu.roll(ec[rows, :], shift, 1), spread)
        state = hst[...].astype(BF16)
        ht_ref[c] = state
        scores = ssc[c]
        outside = mm(csc[rows, :], state) * ece
        hst[...] = hst[...] * ece[Q - 1 : Q, :] + mm(btsc[c], (x * wxe).astype(BF16))
        parts = []
        for pair in range(GW // Q):
            mixers = []
            for half in range(2):
                i = 2 * pair + half
                cj = cjt[c, pl.ds(4 * g + i, 1), :]
                gap = jnp.where(causal, here[:, i : i + 1] - cj, NEG)
                mixers.append((scores * jnp.exp2(gap)).astype(BF16))
            x2 = xb[:, pair * Q : (pair + 1) * Q]
            zero = jnp.zeros_like(x2)
            stacked = jnp.concatenate([jnp.where(lane < HS, x2, zero), jnp.where(lane < HS, zero, x2)], axis=0)
            parts.append(mm(jnp.concatenate(mixers, axis=1), stacked))
        y = jnp.concatenate(parts, axis=1) + outside
        y_ref[rows, :] = y
        gate = gate_ref[rows, :]
        gated = (y + dsk_ref[...] * x) * (gate * sigmoid(gate))
        scaled = gated * gain_ref[...]
        gn[g, rows, :] = scaled.astype(BF16)
        sq = gated * gated
        ssum[rows, :] += sq[:, :Q] + sq[:, Q:]
        if top:
            prod = scaled * dgn[rows, :]
            dsum[rows, :] += prod[:, :Q] + prod[:, Q:]
        return carry

    lax.fori_loop(0, chunks, chunk, 0)

    @pl.when(g == groups - 1)
    def _():
        ones = jnp.ones((8, Q), BF16)
        high, rest = halves(ssum[...])
        ss_ref[...] = mm_nt(ones, high) + mm_nt(ones, rest)
        if top:
            high, rest = halves(dsum[...])
            dot_ref[...] = mm_nt(ones, high) + mm_nt(ones, rest)
        for s in range(rows_all // 256):
            rows = pl.ds(s * 256, 256)
            total = mm_nt(gn[0, rows, :], obuf[0])
            for k in range(1, groups):
                total = total + mm_nt(gn[k, rows, :], obuf[k])
            p_ref[rows, :] = total.astype(BF16)


def full(shape):
    zeros = (0,) * len(shape)
    return pl.BlockSpec(shape, lambda g: zeros)


def layer_forward(h, ng, wbc, wdt, cx, cbc, dtb, rate2, dsk, gain, pieces1, pieces2, dout=None, interpret=False):
    rows, width = h.shape
    inner = gain.shape[1]
    groups = inner // GW
    chunks = rows // Q
    top = dout is not None
    n1, n2 = len(pieces1), len(pieces2)
    col = lambda r: pl.BlockSpec((r, GW), lambda g: (0, g))
    anywhere = pl.BlockSpec(memory_space=pl.ANY)
    in_specs = [full(h.shape), full(ng.shape), full(wbc.shape), full(wdt.shape), col(8), full(cbc.shape), full(dtb.shape), full(rate2.shape), col(1), col(1)]
    args = [h, ng, wbc, wdt, cx, cbc, dtb, rate2, dsk, gain]
    if top:
        in_specs.append(full(dout.shape))
        args.append(dout)
    in_specs += [anywhere] * (n1 + n2)
    args += [*pieces1, *pieces2]
    sds = jax.ShapeDtypeStruct
    out_shape = [
        sds((rows, width), BF16), sds((8, rows), F32), sds((rows, width), BF16), sds((rows, inner), F32),
        sds((rows, inner), F32), sds((rows, inner), F32), sds((rows, 2 * Q), F32), sds((rows, Q), F32),
        sds((chunks, Q, inner), BF16),
    ]
    out_specs = [full((rows, width)), full((8, rows)), full((rows, width)), col(rows), col(rows), col(rows),
                 full((rows, 2 * Q)), full((rows, Q)), pl.BlockSpec((chunks, Q, GW), lambda g: (0, 0, g))]
    if top:
        out_shape.append(sds((8, rows), F32))
        out_specs.append(full((8, rows)))
    vm = pltpu.VMEM
    scratch = [
        vm((groups, width, 2 * GW), BF16), vm((groups, width, GW), BF16), vm((rows // LEN * (8 + LEN), GW), F32),
        vm((rows, Q), BF16), vm((rows, Q), BF16), vm((chunks, Q, Q), BF16), vm((chunks, Q, Q), F32),
        vm((rows, Q), F32), vm((rows, Q), F32), vm((rows, Q), F32), vm((chunks, 16, Q), F32),
        vm((groups, rows, GW), BF16), vm((Q, GW), F32), vm((rows, Q), F32),
        pltpu.SemaphoreType.DMA((groups, n1, 2)), pltpu.SemaphoreType.DMA((groups, n2)),
    ]
    if top:
        scratch += [vm((rows, Q), F32), vm((rows, GW), F32)]
    flops = 2 * rows * width * (3 * inner + 384) * (2 if top else 1)
    return pl.pallas_call(
        functools.partial(fwd_kernel, n1, n2, top, groups),
        grid=(groups,), in_specs=in_specs, out_specs=out_specs, out_shape=out_shape, scratch_shapes=scratch,
        compiler_params=pltpu.CompilerParams(dimension_semantics=("arbitrary",), vmem_limit_bytes=60 << 20),
        cost_estimate=pl.CostEstimate(flops=flops, bytes_accessed=24 << 20, transcendentals=rows * inner * 4),
        name="mixer_forward", interpret=interpret,
    )(*args)


def colsum(a):
    return jnp.sum(a, axis=0, keepdims=True)


def ahead(ext, by):
    if by == 0:
        return ext[:Q, :]
    return pltpu.roll(ext, Q + 8 - by, 0)[:Q, :]


def conv_back(dconv, after, taps):
    ext = jnp.concatenate([dconv, after], axis=0)
    out = taps[3:4, :] * dconv
    for j in range(3):
        out = out + taps[j : j + 1, :] * ahead(ext, 3 - j)
    return out


def bwd_kernel(n1, n2, groups, *refs):
    (do_ref, rq_ref, gate_ref, val_ref, y_ref, ht_ref, shin_ref, stin_ref) = refs[:8]
    (wbc_ref, wdt_ref, cx_ref, cbc_ref, dtb_ref, rate_ref, dsk_ref, gain_ref) = refs[8:16]
    refs = refs[16:]
    pieces1, refs = refs[:n1], refs[n1:]
    pieces2, refs = refs[:n2], refs[n2:]
    (dn_ref, dg_ref, dv_ref, gnorm_ref, dsh_ref, ddt_ref, gcx_ref, gcbc_ref, gdt_ref) = refs[:9]
    (wbuf, obuf, vpad, spad, bsc, csc, ctsc, ssc, cjs, wx, ec, cumt, dgn, dzx, dhst, nxt,
     dstm, dbs, dcs, dcum, xgs, sem1, sem2) = refs[9:]
    g = pl.program_id(0)
    rows_all = do_ref.shape[0]
    chunks = rows_all // Q
    per_seq = LEN // Q
    wide = 8 + LEN

    def each_group(copies, act):
        for k in range(groups):

            @pl.when(g == k)
            def _():
                for c in copies[k]:
                    act(c)

    gate_copies, out_copies = load_pieces(pieces1, pieces2, wbuf, obuf, sem1, sem2, groups)

    @pl.when(g == 0)
    def _():
        for k in range(groups):
            for c in out_copies[k]:
                c.start()
        for k in range(groups):
            for c in gate_copies[k]:
                c.start()
        for s in range(rows_all // LEN):
            spad[pl.ds(s * wide, 8), :] = jnp.zeros((8, GW), F32)
            spad[pl.ds(s * wide + 8, LEN), :] = shin_ref[pl.ds(s * LEN, LEN), :]
        tri = lower_ones()
        taps = cbc_ref[...]

        def shared_rows(c, carry):
            s, cc = c // per_seq, c % per_seq
            rows = pl.ds(pl.multiple_of(c * Q, Q), Q)
            pre = conv_at(spad, s * wide + cc * Q, taps)
            act = (pre * sigmoid(pre)).astype(BF16)
            bmat, cmat = act[:, :Q], act[:, Q:]
            ct = cmat.astype(F32).T.astype(BF16)
            bsc[rows, :] = bmat
            csc[rows, :] = cmat
            ctsc[c] = ct
            ssc[c] = mm(bmat, ct)
            pre = stin_ref[rows, :] + dtb_ref[...]
            step = jnp.maximum(pre, 0.0) + jnp.log1p(jnp.exp(-jnp.abs(pre)))
            cumulative = jnp.dot(tri, step * rate_ref[...], precision=lax.Precision.HIGHEST, preferred_element_type=F32)
            cj = cumulative - jnp.log2(step)
            cjs[rows, :] = cj
            ec[rows, :] = jnp.exp2(cumulative)
            wx[rows, :] = jnp.exp2(cumulative[Q - 1 : Q, :] - cj)
            cumt[c] = cumulative.T[:16, :]
            return carry

        lax.fori_loop(0, chunks, shared_rows, 0)
        for ref in (dstm, dbs, dcs, dcum, xgs):
            ref[...] = jnp.zeros_like(ref)

    each_group(out_copies, lambda c: c.wait())
    for s in range(rows_all // LEN):
        rows = pl.ds(s * LEN, LEN)
        dgn[rows, :] = mm(do_ref[rows, :], obuf[g])
        vpad[pl.ds(s * wide, 8), :] = jnp.zeros((8, GW), F32)
        vpad[pl.ds(s * wide + 8, LEN), :] = val_ref[rows, :]
    gcx_ref[...] = jnp.zeros_like(gcx_ref)
    taps = cx_ref[...]
    spread = spread_matrix()
    gather = spread_matrix(True)
    to_front = lax.rem(Q - 4 * g, Q)
    causal = iota2((Q, Q), 0) <= iota2((Q, Q), 1)
    lane = iota2((Q, Q), 1)
    last_row = iota2((Q, GW), 0) == Q - 1

    def chunk(back, carry):
        c = chunks - 1 - back
        s, cc = c // per_seq, c % per_seq
        rows = pl.ds(pl.multiple_of(c * Q, Q), Q)

        @pl.when(cc == per_seq - 1)
        def _():
            dhst[...] = jnp.zeros_like(dhst)
            nxt[...] = jnp.zeros_like(nxt)

        start = pl.multiple_of(s * wide + cc * Q, 8)
        ext = vpad[pl.ds(start, Q + 8), :]
        taken = [shifted(ext, 3 - j) for j in range(4)]
        pre = taps[4:5, :]
        for j in range(4):
            pre = pre + taps[j : j + 1, :] * taken[j]
        sx = sigmoid(pre)
        x = pre * sx
        xb = x.astype(BF16)
        gate = gate_ref[rows, :]
        sg = sigmoid(gate)
        silu_gate = gate * sg
        y = y_ref[rows, :]
        dsk = dsk_ref[...]
        gain = gain_ref[...]
        mixed = y + dsk * x
        gated = mixed * silu_gate
        r = rq_ref[rows, 0:1]
        q = rq_ref[rows, 1:2]
        d_norm = dgn[rows, :]
        scaled = gated * r
        gnorm_ref[rows, :] = (scaled * gain).astype(BF16)
        d_gated = (r * gain) * d_norm - gated * q
        dmix = d_gated * silu_gate
        dgate = (d_gated * mixed * (sg * (1.0 + gate * (1.0 - sg)))).astype(BF16)
        dg_ref[rows, :] = dgate
        dzx[g, rows, :GW] = dgate
        dyb = dmix.astype(BF16)
        dyf = dyb.astype(F32)
        xf = xb.astype(F32)
        wxe = mm_split(pltpu.roll(wx[rows, :], to_front, 1), spread)
        ece = mm_split(pltpu.roll(ec[rows, :], to_front, 1), spread)
        here = pltpu.roll(cjs[rows, :], to_front, 1)
        ecl = ece[Q - 1 : Q, :]
        state = ht_ref[c]
        dh = dhst[...]
        dhb = dh.astype(BF16)
        gx_state = mm(bsc[rows, :], dhb) * wxe
        dye = (dmix * ece).astype(BF16)
        dcs[rows, :] += mm_nt(dye, state)
        dbs[rows, :] += mm_nt((x * wxe).astype(BF16), dhb)
        ends = colsum(xf * gx_state) + ecl * colsum(state.astype(F32) * dh)
        dhst[...] = dh * ecl + mm(ctsc[c], dye)
        scores = ssc[c]
        dst = jnp.zeros((Q, Q), F32)
        parts = []
        for pair in range(GW // Q):
            x2 = xb[:, pair * Q : (pair + 1) * Q]
            dy2 = dyb[:, pair * Q : (pair + 1) * Q]
            zero = jnp.zeros_like(x2)
            xs = [jnp.where(lane < HS, x2, zero), jnp.where(lane < HS, zero, x2)]
            dys = [jnp.where(lane < HS, dy2, zero), jnp.where(lane < HS, zero, dy2)]
            mixers = []
            for half in range(2):
                i = 2 * pair + half
                ci = cumt[c, pl.ds(4 * g + i, 1), :]
                decay = jnp.exp2(jnp.where(causal, ci - here[:, i : i + 1], NEG))
                mixers.append((scores * decay).astype(BF16))
                dst = dst + mm_nt(xs[half], dy2) * decay
            parts.append(mm(jnp.concatenate(mixers, axis=1), jnp.concatenate(dys, axis=0)))
        dstm[c] += dst
        gx = jnp.concatenate(parts, axis=1) + gx_state
        to_heads = lax.rem(4 * g, Q)
        xg = mm_split(xf * gx, gather)
        yg = mm_split(jnp.where(last_row, dyf * y + ends, dyf * y), gather)
        xgs[rows, :] += pltpu.roll(xg, to_heads, 1)
        dcum[rows, :] += pltpu.roll(yg - xg, to_heads, 1)
        dx = gx + dsk * dmix
        dconv = dx * (sx * (1.0 + pre * (1.0 - sx)))
        dvalue = conv_back(dconv, nxt[...], taps).astype(BF16)
        nxt[...] = dconv[:8, :]
        dv_ref[rows, :] = dvalue
        dzx[g, rows, GW:] = dvalue
        sums = [colsum(dconv * taken[j]) for j in range(4)]
        sums += [colsum(dconv), colsum(dmix * x), colsum(d_norm * scaled), jnp.zeros((1, GW), F32)]
        gcx_ref[...] += jnp.concatenate(sums, axis=0)
        return carry

    lax.fori_loop(0, chunks, chunk, 0)

    @pl.when(g == groups - 1)
    def _():
        upper = (iota2((Q, Q), 0) <= iota2((Q, Q), 1)).astype(F32)
        taps = cbc_ref[...]
        gcbc_ref[...] = jnp.zeros_like(gcbc_ref)
        gdt_ref[...] = jnp.zeros_like(gdt_ref)

        def shared_back(back, carry):
            c = chunks - 1 - back
            s, cc = c // per_seq, c % per_seq
            rows = pl.ds(pl.multiple_of(c * Q, Q), Q)

            @pl.when(cc == per_seq - 1)
            def _():
                nxt[...] = jnp.zeros_like(nxt)

            start = pl.multiple_of(s * wide + cc * Q, 8)
            ext = spad[pl.ds(start, Q + 8), :]
            taken = [shifted(ext, 3 - j) for j in range(4)]
            pre = taps[4:5, :]
            for j in range(4):
                pre = pre + taps[j : j + 1, :] * taken[j]
            sx = sigmoid(pre)
            dst = dstm[c]
            d_b = dbs[rows, :] + mm(dst.astype(BF16), csc[rows, :])
            d_c = dcs[rows, :] + mm(dst.T.astype(BF16), bsc[rows, :])
            dconv = jnp.concatenate([d_b, d_c], axis=1) * (sx * (1.0 + pre * (1.0 - sx)))
            dsh_ref[rows, :] = conv_back(dconv, nxt[...], taps).astype(BF16)
            nxt[...] = dconv[:8, :]
            sums = [colsum(dconv * taken[j]) for j in range(4)] + [colsum(dconv), jnp.zeros((3, GW), F32)]
            gcbc_ref[...] += jnp.concatenate(sums, axis=0)
            da = jnp.dot(upper, dcum[rows, :], precision=lax.Precision.HIGHEST, preferred_element_type=F32)
            pre = stin_ref[rows, :] + dtb_ref[...]
            step = jnp.maximum(pre, 0.0) + jnp.log1p(jnp.exp(-jnp.abs(pre)))
            sig = sigmoid(pre)
            rate = rate_ref[...] * (1.0 / LOG2E)
            dpre = da * rate * sig + xgs[rows, :] * (sig / jnp.maximum(step, 1e-37))
            ddt_ref[rows, :] = dpre.astype(BF16)
            gdt_ref[...] += jnp.concatenate([colsum(dpre), colsum(step * da) * rate, jnp.zeros((6, Q), F32)], axis=0)
            return carry

        lax.fori_loop(0, chunks, shared_back, 0)
        for k in range(groups):
            for c in gate_copies[k]:
                c.wait()
        for s in range(rows_all // 256):
            rows = pl.ds(s * 256, 256)
            total = mm_nt(dsh_ref[rows, :], wbc_ref[...]) + mm_nt(ddt_ref[rows, :], wdt_ref[...])
            for k in range(groups):
                total = total + mm_nt(dzx[k, rows, :], wbuf[k])
            dn_ref[rows, :] = total.astype(BF16)


def layer_backward(dout, rq, gate, value, y, ht, shin, stin, wbc, wdt, cx, cbc, dtb, rate2, dsk, gain, pieces1, pieces2, interpret=False):
    rows, width = dout.shape
    inner = gain.shape[1]
    groups = inner // GW
    chunks = rows // Q
    n1, n2 = len(pieces1), len(pieces2)
    col = lambda r: pl.BlockSpec((r, GW), lambda g: (0, g))
    anywhere = pl.BlockSpec(memory_space=pl.ANY)
    in_specs = [full(dout.shape), full(rq.shape), col(rows), col(rows), col(rows), pl.BlockSpec((chunks, Q, GW), lambda g: (0, 0, g)),
                full(shin.shape), full(stin.shape), full(wbc.shape), full(wdt.shape), col(8), full(cbc.shape), full(dtb.shape),
                full(rate2.shape), col(1), col(1)] + [anywhere] * (n1 + n2)
    args = [dout, rq, gate, value, y, ht, shin, stin, wbc, wdt, cx, cbc, dtb, rate2, dsk, gain, *pieces1, *pieces2]
    sds = jax.ShapeDtypeStruct
    out_shape = [sds((rows, width), BF16), sds((rows, inner), BF16), sds((rows, inner), BF16), sds((rows, inner), BF16),
                 sds((rows, 2 * Q), BF16), sds((rows, Q), BF16), sds((8, inner), F32), sds((8, 2 * Q), F32), sds((8, Q), F32)]
    out_specs = [full((rows, width)), col(rows), col(rows), col(rows), full((rows, 2 * Q)), full((rows, Q)), col(8), full((8, 2 * Q)), full((8, Q))]
    vm = pltpu.VMEM
    padded = rows // LEN * (8 + LEN)
    scratch = [
        vm((groups, width, 2 * GW), BF16), vm((groups, width, GW), BF16), vm((padded, GW), F32), vm((padded, GW), F32),
        vm((rows, Q), BF16), vm((rows, Q), BF16), vm((chunks, Q, Q), BF16), vm((chunks, Q, Q), F32),
        vm((rows, Q), F32), vm((rows, Q), F32), vm((rows, Q), F32), vm((chunks, 16, Q), F32),
        vm((rows, GW), F32), vm((groups, rows, 2 * GW), BF16), vm((Q, GW), F32), vm((8, GW), F32),
        vm((chunks, Q, Q), F32), vm((rows, Q), F32), vm((rows, Q), F32), vm((rows, Q), F32), vm((rows, Q), F32),
        pltpu.SemaphoreType.DMA((groups, n1, 2)), pltpu.SemaphoreType.DMA((groups, n2)),
    ]
    flops = 2 * rows * width * (3 * inner + 384)
    return pl.pallas_call(
        functools.partial(bwd_kernel, n1, n2, groups),
        grid=(groups,), in_specs=in_specs, out_specs=out_specs, out_shape=out_shape, scratch_shapes=scratch,
        compiler_params=pltpu.CompilerParams(dimension_semantics=("arbitrary",), vmem_limit_bytes=60 << 20),
        cost_estimate=pl.CostEstimate(flops=flops, bytes_accessed=30 << 20, transcendentals=rows * inner * 5),
        name="mixer_backward", interpret=interpret,
    )(*args)


def grad_kernel(groups, *refs):
    lhs_ref, *refs = refs
    rhs, refs = refs[: len(groups)], refs[len(groups) :]
    outs, turned = refs[:-1], refs[-1]
    g = pl.program_id(0)

    @pl.when(g == 0)
    def _():
        for k in range(turned.shape[0] // 256):
            cols = pl.ds(k * 256, 256)
            turned[cols, :] = lhs_ref[:, cols].astype(F32).T.astype(BF16)

    first = 0
    for ref, count in zip(rhs, groups):

        @pl.when((g >= first) & (g < first + count))
        def _():
            row = 0
            for out in outs:
                rows = out.shape[0]
                out[...] = mm(turned[pl.ds(row, rows), :], ref[...]).astype(BF16)
                row += rows

        first += count


def weight_grads(lhs, rhs, pieces):
    rows, width = lhs.shape
    groups = [a.shape[1] // GW for a in rhs]
    total = sum(groups)
    specs, first = [full(lhs.shape)], 0
    for count in groups:
        specs.append(pl.BlockSpec((rows, GW), lambda g, first=first, count=count: (0, jnp.clip(g - first, 0, count - 1))))
        first += count
    height = width // pieces
    return pl.pallas_call(
        functools.partial(grad_kernel, groups),
        grid=(total,), in_specs=specs,
        out_specs=[pl.BlockSpec((height, GW), lambda g: (0, g))] * pieces,
        out_shape=[jax.ShapeDtypeStruct((height, total * GW), BF16)] * pieces,
        scratch_shapes=[pltpu.VMEM((width, rows), BF16)],
        compiler_params=pltpu.CompilerParams(dimension_semantics=("arbitrary",), vmem_limit_bytes=60 << 20),
        cost_estimate=pl.CostEstimate(flops=2 * rows * width * total * GW, bytes_accessed=12 << 20, transcendentals=0),
        name="weight_grads",
    )(lhs, *rhs)


RING = (0, 1, 3, 2)
SWAP = [(0, 1), (1, 0)]


class Ring:
    def __init__(self, count):
        self.count = count
        self.blocks = count
        place = lax.axis_index("dp")
        z, self.x = place // 2, place % 2
        order = jnp.array(RING, jnp.int32)
        spot = order[z]
        across = [order[(spot - k) % 4] for k in range(4)]
        self.ids = [a * 2 + self.x for a in across] + [a * 2 + 1 - self.x for a in across]
        self.inverse = []
        for b in range(8):
            k = (spot - RING[b // 2]) % 4
            self.inverse.append(k + jnp.where(self.x == b % 2, 0, 4))
        follow = {RING[i]: RING[(i + 1) % 4] for i in range(4)}
        self.along = [(z * 2 + x, follow[z] * 2 + x) for z in range(4) for x in range(2)]
        self.cross = [(i, i ^ 1) for i in range(8)]

    def gather(self, own):
        mine = [own]
        theirs = []
        for k in range(4):
            if k < 3:
                mine.append(lax.ppermute(mine[k], "dp", self.along))
            theirs.append(lax.ppermute(mine[k], "dp", self.cross))
        return mine + theirs

    def scatter(self, pieces):
        summed = {}
        for k in (1, 2, 3, 0):
            came = lax.ppermute(pieces[4 + k], "dp", self.cross)
            summed[k] = add(pieces[k], came)
        total = summed[1]
        for k in (2, 3, 0):
            total = add(lax.ppermute(total, "dp", self.along), summed[k])
        return total

    def to_slots(self, a):
        return pick_blocks(a, self.ids)

    def from_slots(self, a):
        return pick_blocks(a, self.inverse)


class Whole:
    def __init__(self, count):
        self.count = count
        self.blocks = 1

    def gather(self, own):
        return [lax.all_gather(own, "dp", axis=0, tiled=True)]

    def scatter(self, pieces):
        return lax.psum_scatter(pieces[0], "dp", scatter_dimension=0, tiled=True)

    def to_slots(self, a):
        return a

    from_slots = to_slots


def add(a, b):
    return (a.astype(F32) + b.astype(F32)).astype(BF16)


def pick_blocks(a, ids):
    size = a.shape[-1] // len(ids)
    return jnp.concatenate([lax.dynamic_slice_in_dim(a, i * size, size, a.ndim - 1) for i in ids], axis=-1)


def inverse_rms(h):
    return lax.rsqrt(jnp.mean(h * h, axis=-1, keepdims=True) + EPS)


def lanes(row, count=Q):
    return jnp.pad(row, ((0, 0), (0, count - row.shape[1])))


def local(boundary, norm_gain, in_zx, in_bc, in_dt, conv_x, conv_bc, dt_bias, a_log, d_skip, gate_gain, out_w):
    p, t = lax.axis_index("pipe"), lax.axis_index("tensor")
    count = lax.axis_size("dp")
    dp = (Ring if count == 8 else Whole)(count)
    tokens, part = boundary.shape[1:]
    width = 2 * part
    height = in_zx.shape[1]
    half = gate_gain.shape[1]
    inner = half // 2
    full_inner = 2 * half
    heads = dt_bias.shape[1] // 2

    def mine(first, second):
        return jnp.where(t == 0, first, second)

    def core_swap(a):
        return lax.ppermute(a, "tensor", SWAP)

    def chip_swap(a):
        return lax.ppermute(a, "pipe", SWAP)

    def side(a, which, axis):
        size = a.shape[axis] // 2
        return lax.dynamic_slice_in_dim(a, which * size, size, axis)

    src_in = jnp.concatenate([in_zx[0].reshape(height, 2 * half), in_bc[0], lanes(in_dt[0])], axis=1)
    src_out = out_w[0].T
    turn = [(0, 0), (1, 2), (2, 1), (3, 3)]
    src_in = lax.ppermute(src_in, ("pipe", "tensor"), turn)
    src_out = lax.ppermute(src_out, ("pipe", "tensor"), turn)

    def quarter(which):
        return (
            jnp.concatenate(
                [side(src_in[:, :half], which, 1), side(src_in[:, half : 2 * half], which, 1),
                 side(src_in[:, 2 * half : 2 * half + 2 * Q], which, 1), src_in[:, 2 * half + 2 * Q :]], axis=1),
            side(src_out, which, 1),
        )

    kept, sent = quarter(t), quarter(1 - t)
    came = tuple(core_swap(a) for a in sent)
    in0, out0 = (mine(a, b) for a, b in zip(kept, came))
    in1, out1 = (mine(b, a) for a, b in zip(kept, came))
    body = 2 * inner + Q
    steps_both = in0[:, body:] + jnp.roll(in1[:, body:], Q // 2, axis=1)
    own1 = [jnp.concatenate([in0[:, :body], steps_both], axis=1), in1[:, :body]]
    own2 = [out0, out1]

    flat = [conv_x[0].reshape(-1), gate_gain[0], dt_bias[0], a_log[0], d_skip[0], norm_gain[0], conv_bc[0].reshape(-1)]
    sizes = [a.shape[0] for a in flat]
    one = jnp.concatenate(flat)
    one = jnp.pad(one, (0, -one.shape[0] % 1024)).reshape(-1, Q)
    two = chip_swap(one)
    two = jnp.where(p == 0, jnp.stack([one, two]), jnp.stack([two, one]))
    four = core_swap(two)
    four = mine(jnp.stack([two, four], axis=1), jnp.stack([four, two], axis=1))
    four = four.reshape(2, 2, -1)

    def layer_params(layer):
        row = lax.dynamic_index_in_dim(four[layer], p, 0, keepdims=False)
        parts, at = [], 0
        for size in sizes:
            parts.append(row[at : at + size])
            at += size
        taps, gain, dtb, alog, dsk, ng, cbc = parts
        taps = jnp.pad(side(taps.reshape(5, half), t, 1), ((0, 3), (0, 0)))
        cbc = jnp.pad(cbc.reshape(5, 2 * Q), ((0, 3), (0, 0)))
        gain = side(gain[None], t, 1)
        dtb, rate, dsk = (side(a[None], t, 1) for a in (dtb, -jnp.exp(alog), dsk))
        return dict(ng=dp.to_slots(ng[None]), cx=taps, cbc=cbc, dtb=lanes(dtb), rate2=lanes(rate * LOG2E),
                    dsk=jnp.repeat(dsk, HS, axis=1), gain=gain)

    params = [layer_params(0), layer_params(1)]

    here = boundary[0]
    there = chip_swap(here)

    def all_features(a):
        b = core_swap(a)
        return dp.to_slots(mine(jnp.concatenate([a, b], axis=1), jnp.concatenate([b, a], axis=1)))

    hidden0 = all_features(jnp.where(p == 0, here, there))
    grad1 = all_features(jnp.where(p == 0, there, here))

    pieces1 = [dp.gather(a) for a in own1]
    pieces2 = [dp.gather(a) for a in own2]
    steps_all = jnp.concatenate([a[:, body:] for a in pieces1[0]], axis=0)

    def extra_weights(layer):
        mine_bc = jnp.concatenate([a[:, 2 * inner : body] for a in pieces1[layer]], axis=0)
        other = core_swap(mine_bc)
        wbc = mine(jnp.concatenate([mine_bc, other], axis=1), jnp.concatenate([other, mine_bc], axis=1))
        wdt = lax.dynamic_slice_in_dim(steps_all, layer * (Q // 2) + t * heads, heads, 1)
        return wbc, lanes(wdt)

    extras = [extra_weights(0), extra_weights(1)]

    def weights(layer):
        k = params[layer]
        return (*extras[layer], k["cx"], k["cbc"], k["dtb"], k["rate2"], k["dsk"], k["gain"], pieces1[layer], pieces2[layer])

    def rows_of(a):
        return side(a, t, 0)

    def over_cores(a):
        return add(rows_of(a), core_swap(side(a, 1 - t, 0)))

    def both_rows(a):
        b = core_swap(a)
        return mine(jnp.concatenate([a, b], axis=0), jnp.concatenate([b, a], axis=0))

    def inverse_gate(squares):
        return lax.rsqrt(squares / full_inner + EPS)

    def columns(r, dot):
        return lanes(jnp.stack([r, r**3 * dot / full_inner], axis=1))

    part0, ss0, normed0, gate0, value0, y0, shin0, stin0, ht0 = layer_forward(hidden0, params[0]["ng"], *weights(0))
    r0 = inverse_gate(lax.psum(ss0[0], ("pipe", "tensor")))
    summed = over_cores(part0)
    mixed0 = summed.astype(F32) + chip_swap(summed).astype(F32)
    hidden0_my = rows_of(hidden0).astype(F32)
    hidden1_my = (hidden0_my + rows_of(r0)[:, None] * mixed0).astype(BF16)
    hidden1 = both_rows(hidden1_my)
    part1, ss1, normed1, gate1, value1, y1, shin1, stin1, ht1, dot1 = layer_forward(
        hidden1, params[1]["ng"], *weights(1), dout=grad1)
    ss1, dot1 = lax.psum(jnp.stack([ss1[0], dot1[0]]), ("pipe", "tensor"))
    r1 = inverse_gate(ss1)
    summed = over_cores(part1)
    mixed1 = summed.astype(F32) + lax.ppermute(summed, "pipe", [(0, 1)]).astype(F32)
    out_my = (hidden1_my.astype(F32) + rows_of(r1)[:, None] * mixed1).astype(BF16)

    def rms_back(dn, h, gain):
        scale = inverse_rms(h)
        pulled = dn * gain
        return scale * pulled - h * scale**3 * jnp.mean(pulled * h, axis=-1, keepdims=True), jnp.sum(dn * h * scale, axis=0)

    (dn1, dg1, dv1, gnorm1, dsh1, ddt1, gcx1, gcbc1, gdt1) = layer_backward(
        grad1, columns(r1, dot1), gate1, value1, y1, ht1, shin1, stin1, *weights(1))
    summed = over_cores(dn1)
    dn1 = summed.astype(F32) + chip_swap(summed).astype(F32)
    dh, gng1 = rms_back(dn1, hidden1_my.astype(F32), params[1]["ng"])
    grad0_my = (rows_of(grad1).astype(F32) + dh).astype(BF16)
    dot0 = both_rows(jnp.sum(grad0_my.astype(F32) * mixed0, axis=1))
    grad0 = both_rows(grad0_my)
    gout1 = weight_grads(grad1, [gnorm1], dp.blocks)
    gin1 = weight_grads(normed1, [dg1, dv1], dp.blocks)
    sum_out1 = dp.scatter(gout1)
    sum_in1 = dp.scatter(gin1)

    (dn0, dg0, dv0, gnorm0, dsh0, ddt0, gcx0, gcbc0, gdt0) = layer_backward(
        grad0, columns(r0, dot0), gate0, value0, y0, ht0, shin0, stin0, *weights(0))
    gout0 = weight_grads(grad0, [gnorm0], dp.blocks)
    gin0 = weight_grads(normed0, [dg0, dv0], dp.blocks)
    sum_out0 = dp.scatter(gout0)
    sum_in0 = dp.scatter(gin0)
    summed = over_cores(dn0)
    dn0 = summed.astype(F32) + lax.ppermute(summed, "pipe", [(1, 0)]).astype(F32)
    dh, gng0 = rms_back(dn0, hidden0_my, params[0]["ng"])
    first_my = (grad0_my.astype(F32) + dh).astype(BF16)

    end = dp.from_slots(jnp.where(p == 0, first_my, out_my))
    came = core_swap(side(end, 1 - t, 1))
    kept = side(end, t, 1)
    ends = mine(jnp.concatenate([kept, came], axis=0), jnp.concatenate([came, kept], axis=0))[None]

    bc = [mm_tn(n, d).astype(BF16) for n, d in ((normed0, dsh0), (normed1, dsh1))]
    bc = [add(side(a, t, 1), core_swap(side(a, 1 - t, 1))) for a in bc]
    steps = [mm_tn(n, d)[:, : Q // 2].astype(BF16) for n, d in ((normed0, ddt0), (normed1, ddt1))]
    narrow = jnp.concatenate([*bc, *steps], axis=1)
    narrow = dp.scatter([narrow[k * (width // dp.blocks) : (k + 1) * (width // dp.blocks)] for k in range(dp.blocks)])
    two = chip_swap(narrow)
    two = jnp.where(p == 0, jnp.stack([narrow, two]), jnp.stack([two, narrow]))
    four = core_swap(two)
    four = mine(jnp.stack([two, four], axis=1), jnp.stack([four, two], axis=1)).astype(F32)
    own_bc = lax.dynamic_slice_in_dim(four, p * Q, Q, 3)
    own_bc = own_bc[0] + own_bc[1]
    g_bc = jnp.concatenate([own_bc[0], own_bc[1]], axis=1)
    own_dt = lax.dynamic_index_in_dim(four, t, 0, keepdims=False)
    own_dt = lax.dynamic_slice_in_dim(own_dt, 2 * Q + p * (Q // 2), heads, 2)
    g_dt = jnp.concatenate([own_dt[0], own_dt[1]], axis=1)

    def home(results):
        routes = [([(0, 0), (2, 1)], [(1, 0), (3, 1)]), ([(0, 2), (2, 3)], [(1, 2), (3, 3)])]
        quarters = []
        for q in range(2):
            quarters.append(jnp.where(p == 0, *[lax.ppermute(a, ("pipe", "tensor"), r[q]) for a, r in zip(results, routes)]))
        return quarters

    first, second = home((sum_in0, sum_in1))
    g_zx = jnp.concatenate([first.reshape(height, 2, inner), second.reshape(height, 2, inner)], axis=2).astype(F32)
    first, second = home((sum_out0, sum_out1))
    g_out = jnp.concatenate([first, second], axis=1).astype(F32).T

    def per_quarter(gcx, gdt):
        return jnp.concatenate([gcx[:5].reshape(-1), gcx[6], gcx[5].reshape(heads, HS).sum(axis=1), gdt[0, :heads], gdt[1, :heads]])

    once = (p == 0).astype(F32)
    quarters = jnp.stack([per_quarter(gcx0, gdt0), per_quarter(gcx1, gdt1)])
    length = quarters.shape[1]
    holder = jnp.zeros((2, 4, length), F32)
    holder = lax.dynamic_update_slice(holder, quarters[:, None], (0, p * 2 + t, 0))
    shared = jnp.stack([
        jnp.concatenate([dp.from_slots(gng[None])[0] * once, gcbc[:5].reshape(-1)])
        for gng, gcbc in ((gng0, gcbc0), (gng1, gcbc1))])
    holder, shared = lax.psum((holder, shared), ("pipe", "dp", "tensor"))
    shared = lax.dynamic_index_in_dim(shared, p, 0, keepdims=False)
    holder = lax.dynamic_index_in_dim(holder, p, 0, keepdims=False)
    holder = lax.dynamic_slice_in_dim(holder, 2 * t, 2, 0)
    at = 5 * inner
    g_cx = jnp.concatenate([holder[0, :at].reshape(5, inner), holder[1, :at].reshape(5, inner)], axis=1)
    g_gain = holder[:, at : at + inner].reshape(-1)
    at += inner
    g_dsk, g_dtb, g_alog = (holder[:, at + k * heads : at + (k + 1) * heads].reshape(-1) for k in range(3))
    return (ends, shared[:width][None], g_zx[None], g_bc[None], g_dt[None], g_cx[None], shared[width:].reshape(5, 2 * Q)[None],
            g_dtb[None], g_alog[None], g_dsk[None], g_gain[None], g_out[None])


def solution(mesh):
    pipe, both, wide = ("pipe", "dp", "tensor"), ("pipe", "tensor"), P("pipe", None, "tensor")
    return jax.shard_map(
        local, mesh=mesh,
        in_specs=(P(*pipe), P("pipe", None), P("pipe", "dp", None, "tensor"), P("pipe", "dp", None), P(*pipe), wide,
                  P("pipe", None, None), P(*both), P(*both), P(*both), P(*both), P("pipe", "tensor", "dp")),
        out_specs=(P(*pipe), P("pipe", None), P("pipe", "dp", None, "tensor"), P("pipe", "dp", None), P(*pipe), wide,
                   P("pipe", None, None), P(*both), P(*both), P(*both), P(*both), P("pipe", "tensor", "dp")),
        check_vma=False,
    )
```

```python
import functools
import jax
import jax.numpy as jnp
from jax import lax
from jax.experimental import pallas as pl
from jax.experimental.pallas import tpu as pltpu
from jax.sharding import PartitionSpec as P

LEN = 512
Q = 128
GW = 256
HS = 64
EPS = 1e-05
LOG2E = 1.4426950408889634
F32 = jnp.float32
BF16 = jnp.bfloat16
NEG = -1e30
FORWARD_US = 25
BACKWARD_US = 40
GRADS_US = 20


def mm(a, b):
    return jnp.dot(a, b, preferred_element_type=F32)


def mm_nt(a, b):
    return lax.dot_general(a, b, (((1,), (1,)), ((), ())), preferred_element_type=F32)


def mm_tn(a, b):
    return lax.dot_general(a, b, (((0,), (0,)), ((), ())), preferred_element_type=F32)


def halves(a):
    high = a.astype(BF16)
    return high, (a - high.astype(F32)).astype(BF16)


def mm_split(a, b):
    high, rest = halves(a)
    return mm(high, b) + mm(rest, b)


def sigmoid(a):
    return 1.0 / (1.0 + jnp.exp2(a * (-LOG2E)))


def iota2(shape, axis):
    return lax.broadcasted_iota(jnp.int32, shape, axis)


def spread_matrix(transposed=False):
    if transposed:
        return (iota2((GW, Q), 0) // HS == iota2((GW, Q), 1)).astype(F32).astype(BF16)
    return (iota2((Q, GW), 1) // HS == iota2((Q, GW), 0)).astype(F32).astype(BF16)


def lower_ones():
    return (iota2((Q, Q), 0) >= iota2((Q, Q), 1)).astype(F32)


def shifted(ext, by):
    if by == 0:
        return ext[8:, :]
    return pltpu.roll(ext, by, 0)[8:, :]


def conv_at(pad_ref, start, taps):
    ext = pad_ref[pl.ds(pl.multiple_of(start, 8), Q + 8), :]
    out = taps[4:5, :]
    for j in range(4):
        out = out + taps[j : j + 1, :] * shifted(ext, 3 - j)
    return out


def expand(parts, spread):
    high, rest = halves(jnp.concatenate(parts, axis=0))
    out = mm(high, spread) + mm(rest, spread)
    return [out[k * Q : (k + 1) * Q] for k in range(len(parts))]


def weight_copies(starts, pieces, bufs, sems, groups):
    wbuf, obuf, wbc, wdt = bufs
    inner = groups * GW
    zx, out, narrow = [[] for _ in range(groups)], [[] for _ in range(groups)], []
    for k, piece in enumerate(pieces):
        here = pl.ds(pl.multiple_of(starts[k], 16), piece.shape[0])
        for g in range(groups):
            for part, (into, ref, at) in enumerate(((zx, wbuf, 0), (zx, wbuf, GW), (out, obuf, 0))):
                into[g].append(pltpu.make_async_copy(
                    piece.at[:, pl.ds(part * inner + g * GW, GW)], ref.at[g, here, pl.ds(at, GW)], sems.at[k, 3 * g + part]))
        last = 3 * groups
        narrow.append(pltpu.make_async_copy(piece.at[:, pl.ds(3 * inner, 2 * Q)], wbc.at[here, :], sems.at[k, last]))
        narrow.append(pltpu.make_async_copy(piece.at[:, pl.ds(3 * inner + 2 * Q, Q)], wdt.at[here, :], sems.at[k, last + 1]))
    return zx, out, narrow


def weight_scratch(pieces, groups, width):
    vm = pltpu.VMEM
    return [vm((groups, width, 2 * GW), BF16), vm((groups, width, GW), BF16), vm((width, 2 * Q), BF16), vm((width, Q), BF16),
            pltpu.SemaphoreType.DMA((len(pieces), 3 * groups + 2))]


def each_group(copies, act):
    for k, mine in enumerate(copies):

        @pl.when(pl.program_id(0) == k)
        def _():
            for c in mine:
                act(c)


HALF = LEN // 2
WIDE = 8 + LEN
PER = LEN // Q


def half_rows(s, which):
    return pl.ds(pl.multiple_of(s * LEN + which * HALF, HALF), HALF)


def chunk_rows(s, cc):
    return pl.ds(pl.multiple_of(s * LEN + cc * Q, Q), Q)


def steps_of(stin, dtb, rate, tri):
    pre = stin + dtb
    step = jnp.maximum(pre, 0.0) + jnp.log1p(jnp.exp(-jnp.abs(pre)))
    cumulative = jnp.dot(tri, step * rate, precision=lax.Precision.HIGHEST, preferred_element_type=F32)
    return pre, step, cumulative, cumulative - jnp.log2(step)


def fwd_kernel(n, nseq, top, groups, unroll, starts, *refs):
    h_refs, (ng_ref, col_ref, all_ref), refs = refs[: 2 * nseq], refs[2 * nseq : 2 * nseq + 3], refs[2 * nseq + 3 :]
    cx_ref, gain_ref, dsk_ref, cbc_ref, dtb_ref, rate_ref = small_refs(col_ref, all_ref)
    if top:
        dout_refs, refs = refs[: 2 * nseq], refs[2 * nseq :]
    pieces, refs = refs[:n], refs[n:]
    p_refs, refs = refs[:2], refs[2:]
    (ss_ref, gate_ref, val_ref, y_ref, shin_ref, stin_ref, ht_ref), refs = refs[:7], refs[7:]
    if top:
        dot_ref, refs = refs[0], refs[1:]
    bufs, sems, refs = refs[:4], refs[4], refs[5:]
    wbuf, obuf, wbc_ref, wdt_ref = bufs
    (nrm_ref, vpad, csc, btsc, ssc, cum, wx, ec, cjt, gn, hst, ssum) = refs[:12]
    dsum, dgn = refs[12:] if top else (None, None)
    g = pl.program_id(0)
    core = starts[n]
    sides = [(s, which) for s in range(nseq) for which in (core, 1 - core)]
    gate_copies, out_copies, narrow_copies = weight_copies(starts, pieces, bufs, sems, groups)

    @pl.when(g == 0)
    def _():
        for c in narrow_copies:
            c.start()
        for k in range(groups):
            for c in gate_copies[k] + out_copies[k]:
                c.start()
        for (s, which), h_ref in zip(sides, h_refs):

            def norm_rows(c, carry):
                h = h_ref[pl.ds(pl.multiple_of(c * Q, Q), Q), :].astype(F32)
                scale = lax.rsqrt(jnp.mean(h * h, axis=-1, keepdims=True) + EPS)
                at = pl.multiple_of(s * LEN + which * HALF + c * Q, Q)
                nrm_ref[pl.ds(at, Q), :] = (h * scale * ng_ref[...]).astype(BF16)
                return carry

            lax.fori_loop(0, HALF // Q, norm_rows, 0, unroll=True)
        for c in narrow_copies:
            c.wait()
        ssum[...] = jnp.zeros_like(ssum)
        if top:
            dsum[...] = jnp.zeros_like(dsum)
        for s in range(nseq):
            rows = pl.ds(s * LEN, LEN)
            normed = nrm_ref[rows, :]
            shin = mm(normed, wbc_ref[...])
            shin_ref[rows, :] = shin
            vpad[pl.ds(s * WIDE, 8), :] = jnp.zeros((8, GW), F32)
            vpad[pl.ds(s * WIDE + 8, LEN), :] = shin
            stin_ref[rows, :] = mm(normed, wdt_ref[...])
        tri = lower_ones()
        taps = cbc_ref[...]

        def shared_rows(cc, carry):
            for s in range(nseq):
                c, rows = s * PER + cc, chunk_rows(s, cc)
                pre = conv_at(vpad, s * WIDE + cc * Q, taps)
                act = (pre * sigmoid(pre)).astype(BF16)
                bmat, cmat = act[:, :Q], act[:, Q:]
                bt = bmat.astype(F32).T.astype(BF16)
                btsc[c] = bt
                csc[rows, :] = cmat
                ssc[c] = mm(cmat, bt)
                _, _, cumulative, cj = steps_of(stin_ref[rows, :], dtb_ref[...], rate_ref[...], tri)
                cum[rows, :] = cumulative
                ec[rows, :] = jnp.exp2(cumulative)
                wx[rows, :] = jnp.exp2(cumulative[Q - 1 : Q, :] - cj)
                cjt[c] = cj.T[:16, :]
            return carry

        lax.fori_loop(0, PER, shared_rows, 0)

    each_group(gate_copies, lambda c: c.wait())
    each_group(out_copies, lambda c: c.wait())
    for s in range(nseq):
        rows = pl.ds(s * LEN, LEN)
        normed = nrm_ref[rows, :]
        gate_ref[rows, :] = mm(normed, wbuf[g, :, :GW]).astype(BF16)
        value = mm(normed, wbuf[g, :, GW:]).astype(BF16)
        val_ref[rows, :] = value
        vpad[pl.ds(s * WIDE, 8), :] = jnp.zeros((8, GW), F32)
        vpad[pl.ds(s * WIDE + 8, LEN), :] = value.astype(F32)
    if top:
        for (s, which), ref in zip(sides, dout_refs):
            dgn[half_rows(s, which), :] = mm(ref[...], obuf[g])
    taps = cx_ref[...]
    spread = spread_matrix()
    shift = lax.rem(Q - 4 * g, Q)
    causal = iota2((Q, Q), 0) >= iota2((Q, Q), 1)
    lane = iota2((Q, Q), 1)
    hst[...] = jnp.zeros_like(hst)

    def one(s, cc):
        c, rows = s * PER + cc, chunk_rows(s, cc)
        pre = conv_at(vpad, s * WIDE + cc * Q, taps)
        x = pre * sigmoid(pre)
        xb = x.astype(BF16)
        here = pltpu.roll(cum[rows, :], shift, 1)
        wxe, ece = expand([pltpu.roll(wx[rows, :], shift, 1), pltpu.roll(ec[rows, :], shift, 1)], spread)
        old = hst[s]
        state = old.astype(BF16)
        ht_ref[c] = state
        scores = ssc[c]
        outside = mm(csc[rows, :], state) * ece
        hst[s] = old * ece[Q - 1 : Q, :] + mm(btsc[c], (x * wxe).astype(BF16))
        parts = []
        for pair in range(GW // Q):
            mixers = []
            for half in range(2):
                i = 2 * pair + half
                cj = cjt[c, pl.ds(4 * g + i, 1), :]
                gap = jnp.where(causal, here[:, i : i + 1] - cj, NEG)
                mixers.append((scores * jnp.exp2(gap)).astype(BF16))
            x2 = xb[:, pair * Q : (pair + 1) * Q]
            zero = jnp.zeros_like(x2)
            stacked = jnp.concatenate([jnp.where(lane < HS, x2, zero), jnp.where(lane < HS, zero, x2)], axis=0)
            parts.append(mm(jnp.concatenate(mixers, axis=1), stacked))
        y = jnp.concatenate(parts, axis=1) + outside
        y_ref[rows, :] = y
        gate = gate_ref[rows, :].astype(F32)
        gated = (y + dsk_ref[...] * x) * (gate * sigmoid(gate))
        scaled = gated * gain_ref[...]
        gn[g, rows, :] = scaled.astype(BF16)
        sq = gated * gated
        ssum[rows, :] += sq[:, :Q] + sq[:, Q:]
        if top:
            prod = scaled * dgn[rows, :]
            dsum[rows, :] += prod[:, :Q] + prod[:, Q:]

    def chunk(cc, carry):
        for s in range(nseq):
            one(s, cc)
        return carry

    lax.fori_loop(0, PER, chunk, 0, unroll=unroll)

    @pl.when(g == groups - 1)
    def _():
        ones = jnp.ones((8, Q), BF16)
        high, rest = halves(ssum[...])
        ss_ref[...] = mm_nt(ones, high) + mm_nt(ones, rest)
        if top:
            high, rest = halves(dsum[...])
            dot_ref[...] = mm_nt(ones, high) + mm_nt(ones, rest)
        for i, (s, which) in enumerate(sides):
            rows = half_rows(s, which)
            total = mm_nt(gn[0, rows, :], obuf[0])
            for k in range(1, groups):
                total = total + mm_nt(gn[k, rows, :], obuf[k])
            p_refs[i % 2][pl.ds(s * HALF, HALF), :] = total.astype(BF16)


def grid_call(kernel, name, prefetch, groups, in_specs, out_specs, out_shape, scratch, args, micros):
    return pl.pallas_call(
        kernel,
        grid_spec=pltpu.PrefetchScalarGridSpec(
            num_scalar_prefetch=1, grid=(groups,), in_specs=in_specs, out_specs=out_specs, scratch_shapes=scratch),
        out_shape=out_shape,
        compiler_params=pltpu.CompilerParams(dimension_semantics=("arbitrary",), vmem_limit_bytes=60 << 20),
        cost_estimate=pl.CostEstimate(flops=int(micros * 1.15e9), bytes_accessed=20 << 20, transcendentals=0),
        name=name,
    )(prefetch, *args)


def full(shape):
    zeros = (0,) * len(shape)
    return pl.BlockSpec(shape, lambda g, *_: zeros)


def col(rows, at=0):
    return pl.BlockSpec((rows, GW), lambda g, *_: (at, g))


def row_block(rows, cols, at):
    return pl.BlockSpec((rows, cols), lambda g, *_: (at, 0))


ANYWHERE = pl.BlockSpec(memory_space=pl.ANY)


def half_specs(operands):
    return [row_block(HALF, a.shape[1], at) for a, at in operands]


def small_refs(by_group, every):
    return (by_group.at[0:5, :], by_group.at[5:6, :], by_group.at[6:7, :], every.at[8:13, 0 : 2 * Q],
            every.at[8:9, 2 * Q : 3 * Q], every.at[9:10, 2 * Q : 3 * Q])


def small_specs(small):
    return [col(8), full(small.shape)]


def layer_forward(hs, ng, small, starts, pieces, douts=(), unroll=4):
    width = hs[0][0].shape[1]
    inner = small.shape[1]
    nseq, n, top, groups = len(hs) // 2, len(pieces), len(douts) > 0, inner // GW
    rows, chunks = nseq * LEN, nseq * PER
    in_specs = half_specs(hs) + [full(ng.shape)] + small_specs(small) + half_specs(douts) + [ANYWHERE] * n
    args = [a for a, _ in hs] + [ng, small, small] + [a for a, _ in douts] + [*pieces]
    sds = jax.ShapeDtypeStruct
    out_shape = [sds((nseq * HALF, width), BF16)] * 2 + [
        sds((8, rows), F32), sds((rows, inner), BF16), sds((rows, inner), BF16), sds((rows, inner), F32),
        sds((rows, 2 * Q), F32), sds((rows, Q), F32), sds((chunks, Q, inner), BF16)]
    out_specs = [full((nseq * HALF, width))] * 2 + [
        full((8, rows)), col(rows), col(rows), col(rows), full((rows, 2 * Q)), full((rows, Q)),
        pl.BlockSpec((chunks, Q, GW), lambda g, *_: (0, 0, g))]
    if top:
        out_shape.append(sds((8, rows), F32))
        out_specs.append(full((8, rows)))
    vm = pltpu.VMEM
    scratch = weight_scratch(pieces, groups, width) + [
        vm((rows, width), BF16), vm((nseq * WIDE, GW), F32), vm((rows, Q), BF16), vm((chunks, Q, Q), BF16), vm((chunks, Q, Q), F32),
        vm((rows, Q), F32), vm((rows, Q), F32), vm((rows, Q), F32), vm((chunks, 16, Q), F32),
        vm((groups, rows, GW), BF16), vm((nseq, Q, GW), F32), vm((rows, Q), F32)]
    if top:
        scratch += [vm((rows, Q), F32), vm((rows, GW), F32)]
    out = grid_call(functools.partial(fwd_kernel, n, nseq, top, groups, unroll), "mixer_forward", starts, groups, in_specs, out_specs,
                    out_shape, scratch, args, FORWARD_US)
    return out[:2], out[2:]


def colsum(a):
    return jnp.sum(a, axis=0, keepdims=True)


def ahead(ext, by):
    if by == 0:
        return ext[:Q, :]
    return pltpu.roll(ext, Q + 8 - by, 0)[:Q, :]


def conv_back(dconv, after, taps):
    ext = jnp.concatenate([dconv, after], axis=0)
    out = taps[3:4, :] * dconv
    for j in range(3):
        out = out + taps[j : j + 1, :] * ahead(ext, 3 - j)
    return out


def bwd_kernel(n, nseq, groups, unroll, starts, *refs):
    do_refs, refs = refs[: 2 * nseq], refs[2 * nseq :]
    (rq_ref, gate_ref, val_ref, y_ref, ht_ref, shin_ref, stin_ref), refs = refs[:7], refs[7:]
    cx_ref, gain_ref, dsk_ref, cbc_ref, dtb_ref, rate_ref = small_refs(*refs[:2])
    refs = refs[2:]
    pieces, refs = refs[:n], refs[n:]
    dn_refs, refs = refs[: 2 * nseq], refs[2 * nseq :]
    (dg_ref, dv_ref, gnorm_ref, dsh_ref, ddt_ref, gcx_ref, gcbc_ref, gdt_ref), refs = refs[:8], refs[8:]
    bufs, sems, refs = refs[:4], refs[4], refs[5:]
    wbuf, obuf, wbc_ref, wdt_ref = bufs
    (vpad, spad, bsc, csc, ctsc, ssc, cjs, wx, ec, cumt, dgn, dzx, dhst, nxt, dstm, dbs, dcs, dcum, xgs) = refs
    g = pl.program_id(0)
    core = starts[n]
    sides = [(s, which) for s in range(nseq) for which in (core, 1 - core)]
    gate_copies, out_copies, narrow_copies = weight_copies(starts, pieces, bufs, sems, groups)

    @pl.when(g == 0)
    def _():
        for k in range(groups):
            for c in out_copies[k]:
                c.start()
        for c in narrow_copies:
            c.start()
        for k in range(groups):
            for c in gate_copies[k]:
                c.start()
        for s in range(nseq):
            spad[pl.ds(s * WIDE, 8), :] = jnp.zeros((8, GW), F32)
            spad[pl.ds(s * WIDE + 8, LEN), :] = shin_ref[pl.ds(s * LEN, LEN), :]
        tri = lower_ones()
        taps = cbc_ref[...]

        def shared_rows(cc, carry):
            for s in range(nseq):
                c, rows = s * PER + cc, chunk_rows(s, cc)
                pre = conv_at(spad, s * WIDE + cc * Q, taps)
                act = (pre * sigmoid(pre)).astype(BF16)
                bmat, cmat = act[:, :Q], act[:, Q:]
                ct = cmat.astype(F32).T.astype(BF16)
                bsc[rows, :] = bmat
                csc[rows, :] = cmat
                ctsc[c] = ct
                ssc[c] = mm(bmat, ct)
                _, _, cumulative, cj = steps_of(stin_ref[rows, :], dtb_ref[...], rate_ref[...], tri)
                cjs[rows, :] = cj
                ec[rows, :] = jnp.exp2(cumulative)
                wx[rows, :] = jnp.exp2(cumulative[Q - 1 : Q, :] - cj)
                cumt[c] = cumulative.T[:16, :]
            return carry

        lax.fori_loop(0, PER, shared_rows, 0, unroll=unroll)
        for ref in (dstm, dbs, dcs, dcum, xgs):
            ref[...] = jnp.zeros_like(ref)

    each_group(out_copies, lambda c: c.wait())
    for (s, which), ref in zip(sides, do_refs):
        dgn[half_rows(s, which), :] = mm(ref[...], obuf[g])
    for s in range(nseq):
        vpad[pl.ds(s * WIDE, 8), :] = jnp.zeros((8, GW), F32)
        vpad[pl.ds(s * WIDE + 8, LEN), :] = val_ref[pl.ds(s * LEN, LEN), :].astype(F32)
    gcx_ref[...] = jnp.zeros_like(gcx_ref)
    dhst[...] = jnp.zeros_like(dhst)
    nxt[...] = jnp.zeros_like(nxt)
    taps = cx_ref[...]
    spread = spread_matrix()
    gather = spread_matrix(True)
    to_front = lax.rem(Q - 4 * g, Q)
    causal = iota2((Q, Q), 0) <= iota2((Q, Q), 1)
    lane = iota2((Q, Q), 1)
    last_row = iota2((Q, GW), 0) == Q - 1

    def one(s, cc):
        c, rows = s * PER + cc, chunk_rows(s, cc)
        start = pl.multiple_of(s * WIDE + cc * Q, 8)
        ext = vpad[pl.ds(start, Q + 8), :]
        taken = [shifted(ext, 3 - j) for j in range(4)]
        pre = taps[4:5, :]
        for j in range(4):
            pre = pre + taps[j : j + 1, :] * taken[j]
        sx = sigmoid(pre)
        x = pre * sx
        xb = x.astype(BF16)
        gate = gate_ref[rows, :].astype(F32)
        sg = sigmoid(gate)
        silu_gate = gate * sg
        y = y_ref[rows, :]
        dsk = dsk_ref[...]
        gain = gain_ref[...]
        mixed = y + dsk * x
        gated = mixed * silu_gate
        r = rq_ref[rows, 0:1]
        q = rq_ref[rows, 1:2]
        d_norm = dgn[rows, :]
        scaled = gated * r
        gnorm_ref[rows, :] = (scaled * gain).astype(BF16)
        d_gated = (r * gain) * d_norm - gated * q
        dmix = d_gated * silu_gate
        dgate = (d_gated * mixed * (sg * (1.0 + gate * (1.0 - sg)))).astype(BF16)
        dg_ref[rows, :] = dgate
        dzx[g, rows, :GW] = dgate
        dyb = dmix.astype(BF16)
        dyf = dyb.astype(F32)
        xf = xb.astype(F32)
        wxe, ece = expand([pltpu.roll(wx[rows, :], to_front, 1), pltpu.roll(ec[rows, :], to_front, 1)], spread)
        here = pltpu.roll(cjs[rows, :], to_front, 1)
        ecl = ece[Q - 1 : Q, :]
        state = ht_ref[c]
        dh = dhst[s]
        dhb = dh.astype(BF16)
        gx_state = mm(bsc[rows, :], dhb) * wxe
        dye = (dmix * ece).astype(BF16)
        dcs[rows, :] += mm_nt(dye, state)
        dbs[rows, :] += mm_nt((x * wxe).astype(BF16), dhb)
        ends = colsum(xf * gx_state) + ecl * colsum(state.astype(F32) * dh)
        dhst[s] = dh * ecl + mm(ctsc[c], dye)
        scores = ssc[c]
        dst = jnp.zeros((Q, Q), F32)
        parts = []
        for pair in range(GW // Q):
            x2 = xb[:, pair * Q : (pair + 1) * Q]
            dy2 = dyb[:, pair * Q : (pair + 1) * Q]
            zero = jnp.zeros_like(x2)
            xs = [jnp.where(lane < HS, x2, zero), jnp.where(lane < HS, zero, x2)]
            dys = [jnp.where(lane < HS, dy2, zero), jnp.where(lane < HS, zero, dy2)]
            mixers = []
            for half in range(2):
                i = 2 * pair + half
                ci = cumt[c, pl.ds(4 * g + i, 1), :]
                decay = jnp.exp2(jnp.where(causal, ci - here[:, i : i + 1], NEG))
                mixers.append((scores * decay).astype(BF16))
                dst = dst + mm_nt(xs[half], dy2) * decay
            parts.append(mm(jnp.concatenate(mixers, axis=1), jnp.concatenate(dys, axis=0)))
        dstm[c] += dst
        gx = jnp.concatenate(parts, axis=1) + gx_state
        to_heads = lax.rem(4 * g, Q)
        xg, yg = expand([xf * gx, jnp.where(last_row, dyf * y + ends, dyf * y)], gather)
        xgs[rows, :] += pltpu.roll(xg, to_heads, 1)
        dcum[rows, :] += pltpu.roll(yg - xg, to_heads, 1)
        dx = gx + dsk * dmix
        dconv = dx * (sx * (1.0 + pre * (1.0 - sx)))
        dvalue = conv_back(dconv, nxt[s], taps).astype(BF16)
        nxt[s] = dconv[:8, :]
        dv_ref[rows, :] = dvalue
        dzx[g, rows, GW:] = dvalue
        sums = [colsum(dconv * taken[j]) for j in range(4)]
        sums += [colsum(dconv), colsum(dmix * x), colsum(d_norm * scaled), jnp.zeros((1, GW), F32)]
        gcx_ref[...] += jnp.concatenate(sums, axis=0)

    def chunk(back, carry):
        for s in range(nseq):
            one(s, PER - 1 - back)
        return carry

    lax.fori_loop(0, PER, chunk, 0, unroll=unroll)

    @pl.when(g == groups - 1)
    def _():
        upper = (iota2((Q, Q), 0) <= iota2((Q, Q), 1)).astype(F32)
        taps = cbc_ref[...]
        gcbc_ref[...] = jnp.zeros_like(gcbc_ref)
        gdt_ref[...] = jnp.zeros_like(gdt_ref)
        nxt[...] = jnp.zeros_like(nxt)

        def shared_back(s, cc):
            c, rows = s * PER + cc, chunk_rows(s, cc)
            start = pl.multiple_of(s * WIDE + cc * Q, 8)
            ext = spad[pl.ds(start, Q + 8), :]
            taken = [shifted(ext, 3 - j) for j in range(4)]
            pre = taps[4:5, :]
            for j in range(4):
                pre = pre + taps[j : j + 1, :] * taken[j]
            sx = sigmoid(pre)
            dst = dstm[c]
            d_b = dbs[rows, :] + mm(dst.astype(BF16), csc[rows, :])
            d_c = dcs[rows, :] + mm(dst.T.astype(BF16), bsc[rows, :])
            dconv = jnp.concatenate([d_b, d_c], axis=1) * (sx * (1.0 + pre * (1.0 - sx)))
            dsh_ref[rows, :] = conv_back(dconv, nxt[s], taps).astype(BF16)
            nxt[s] = dconv[:8, :]
            sums = [colsum(dconv * taken[j]) for j in range(4)] + [colsum(dconv), jnp.zeros((3, GW), F32)]
            gcbc_ref[...] += jnp.concatenate(sums, axis=0)
            da = jnp.dot(upper, dcum[rows, :], precision=lax.Precision.HIGHEST, preferred_element_type=F32)
            pre = stin_ref[rows, :] + dtb_ref[...]
            step = jnp.maximum(pre, 0.0) + jnp.log1p(jnp.exp(-jnp.abs(pre)))
            sig = sigmoid(pre)
            rate = rate_ref[...] * (1.0 / LOG2E)
            dpre = da * rate * sig + xgs[rows, :] * (sig / jnp.maximum(step, 1e-37))
            ddt_ref[rows, :] = dpre.astype(BF16)
            gdt_ref[...] += jnp.concatenate([colsum(dpre), colsum(step * da) * rate, jnp.zeros((6, Q), F32)], axis=0)

        def back_rows(back, carry):
            for s in range(nseq):
                shared_back(s, PER - 1 - back)
            return carry

        lax.fori_loop(0, PER, back_rows, 0, unroll=unroll)
        for c in narrow_copies:
            c.wait()
        for k in range(groups):
            for c in gate_copies[k]:
                c.wait()
        for (s, which), ref in zip(sides, dn_refs):
            rows = half_rows(s, which)
            total = mm_nt(dsh_ref[rows, :], wbc_ref[...]) + mm_nt(ddt_ref[rows, :], wdt_ref[...])
            for k in range(groups):
                total = total + mm_nt(dzx[k, rows, :], wbuf[k])
            ref[...] = total.astype(BF16)


def layer_backward(douts, rq, saved, at, small, starts, pieces, unroll=4):
    gate, value, y, shin, stin, ht = saved
    width = douts[0][0].shape[1]
    inner = small.shape[1]
    nseq, n, groups = len(douts) // 2, len(pieces), inner // GW
    rows, chunks, at = nseq * LEN, nseq * PER, at // nseq
    in_specs = half_specs(douts) + [
        full(rq.shape), col(rows, at), col(rows, at), col(rows, at),
        pl.BlockSpec((chunks, Q, GW), lambda g, *_: (at, 0, g)), row_block(rows, 2 * Q, at), row_block(rows, Q, at)]
    in_specs += small_specs(small) + [ANYWHERE] * n
    args = [a for a, _ in douts] + [rq, gate, value, y, ht, shin, stin, small, small, *pieces]
    sds = jax.ShapeDtypeStruct
    out_shape = [sds((HALF, width), BF16)] * (2 * nseq) + [sds((rows, inner), BF16)] * 3 + [
        sds((rows, 2 * Q), BF16), sds((rows, Q), BF16), sds((8, inner), F32), sds((8, 2 * Q), F32), sds((8, Q), F32)]
    out_specs = [full((HALF, width))] * (2 * nseq) + [col(rows)] * 3 + [
        full((rows, 2 * Q)), full((rows, Q)), col(8), full((8, 2 * Q)), full((8, Q))]
    vm = pltpu.VMEM
    scratch = weight_scratch(pieces, groups, width) + [
        vm((nseq * WIDE, GW), F32), vm((nseq * WIDE, GW), F32),
        vm((rows, Q), BF16), vm((rows, Q), BF16), vm((chunks, Q, Q), BF16), vm((chunks, Q, Q), F32),
        vm((rows, Q), F32), vm((rows, Q), F32), vm((rows, Q), F32), vm((chunks, 16, Q), F32),
        vm((rows, GW), F32), vm((groups, rows, 2 * GW), BF16), vm((nseq, Q, GW), F32), vm((nseq, 8, GW), F32),
        vm((chunks, Q, Q), F32), vm((rows, Q), F32), vm((rows, Q), F32), vm((rows, Q), F32), vm((rows, Q), F32)]
    out = grid_call(functools.partial(bwd_kernel, n, nseq, groups, unroll), "mixer_backward", starts, groups, in_specs, out_specs,
                    out_shape, scratch, args, BACKWARD_US * nseq / 2)
    return out[: 2 * nseq], out[2 * nseq :]


def grad_kernel(counts, starts, *refs):
    gain_ref, dout, hidden, refs = refs[0], refs[1:5], refs[5:9], refs[9:]
    rhs, refs = refs[: 2 * len(counts)], refs[2 * len(counts) :]
    outs, (turned, whole) = refs[:-2], refs[-2:]
    g = pl.program_id(0)
    core = starts[len(outs)]

    def turn(halves_of, norm):
        for k, ref in enumerate(halves_of):
            base = k // 2 * LEN + (core if k % 2 == 0 else 1 - core) * HALF
            here = pl.ds(pl.multiple_of(base, HALF), HALF)
            if norm:
                h = ref[...].astype(F32)
                scale = lax.rsqrt(jnp.mean(h * h, axis=-1, keepdims=True) + EPS)
            for j in range(turned.shape[0] // GW):
                cols = pl.ds(j * GW, GW)
                part = ref[:, cols]
                if norm:
                    part = (part.astype(F32) * scale * gain_ref[:, cols]).astype(BF16)
                turned[cols, here] = part.T

    pl.when(g == 0)(lambda: turn(dout, False))
    pl.when(g == counts[0])(lambda: turn(hidden, True))
    first = 0
    for i, count in enumerate(counts):

        @pl.when((g >= first) & (g < first + count))
        def _():
            both = jnp.concatenate([rhs[2 * i][...], rhs[2 * i + 1][...]], axis=0)
            whole[...] = mm(turned[...], both).astype(BF16)

        first += count
    for k, out in enumerate(outs):
        out[...] = whole[pl.ds(pl.multiple_of(starts[k], 16), out.shape[0]), :]


def weight_grads(dout, hidden, gain, rhs, starts, heights):
    width = gain.shape[1]
    counts = [a.shape[1] // GW for a, _ in rhs]
    total = sum(counts)
    specs, first = [full(gain.shape)] + half_specs(dout + hidden), 0
    args = [gain] + [a for a, _ in dout + hidden] + [a for pair in rhs for a in pair]
    for count in counts:
        specs += [pl.BlockSpec((LEN, GW), lambda g, *_, first=first, count=count: (0, jnp.clip(g - first, 0, count - 1)))] * 2
        first += count
    return grid_call(functools.partial(grad_kernel, counts), "weight_grads", starts, total, specs,
                     [col(h) for h in heights], [jax.ShapeDtypeStruct((h, total * GW), BF16) for h in heights],
                     [pltpu.VMEM((width, 2 * LEN), BF16), pltpu.VMEM((width, GW), BF16)], args, GRADS_US)


RING = (0, 1, 3, 2)
SWAP = [(0, 1), (1, 0)]


def add(a, b):
    return (a.astype(F32) + b.astype(F32)).astype(BF16)


def after(a, *others):
    return lax.optimization_barrier((a, *others))[0]


class Rounds:
    def __init__(self, **lanes):
        self.lanes, self.results, self.wanted, self.mark = {}, {}, {}, ()
        self.add(**lanes)

    def add(self, **lanes):
        for name, lane in lanes.items():
            self.lanes[name] = lane
            self._go(name, None)

    def _go(self, name, values):
        try:
            self.wanted[name] = list(self.lanes[name].send(values))
        except StopIteration as stop:
            self.results[name] = stop.value
            del self.lanes[name]
            self.wanted.pop(name, None)

    def step(self, count=1):
        for _ in range(count):
            flat, tree = jax.tree.flatten(self.wanted)
            if flat:
                flat = lax.optimization_barrier(tuple(flat))
                self.mark = flat
            for name, values in jax.tree.unflatten(tree, flat).items():
                self._go(name, values)

    def finish(self, name):
        while name not in self.results:
            self.step()
        return self.results[name]


def place_table(rows):
    table = [[row + [core] for core in range(2)] for row in rows]
    table = jnp.array(table, jnp.int32)
    where = (lax.axis_index("dp"), lax.axis_index("tensor"), 0)
    return lax.dynamic_slice(table, where, (1, 1, table.shape[2])).reshape(-1)


class Ring:
    def __init__(self, height):
        follow = {RING[i]: RING[(i + 1) % 4] for i in range(4)}
        self.along = [(z * 2 + x, follow[z] * 2 + x) for z in range(4) for x in range(2)]
        self.cross = [(i, i ^ 1) for i in range(8)]
        self.heights = [height] * 8
        slots, pieces = [], []
        for z in range(4):
            for x in range(2):
                across = [RING[(RING.index(z) - k) % 4] * 2 for k in range(4)]
                slots.append([(a + x) * height for a in across] + [(a + 1 - x) * height for a in across])
                pieces.append(slots[-1] + [slots[-1][7] + height // 2])
        self.slots, self.pieces = place_table(slots), place_table(pieces)

    def z(self, a):
        return lax.ppermute(a, "dp", self.along)

    def x(self, a):
        return lax.ppermute(a, "dp", self.cross)

    def gather(self, own):
        half = own.shape[0] // 2
        mine, theirs = [own], []
        for k in range(3):
            along, across = yield self.z(mine[k]), self.x(mine[k])
            mine.append(along)
            theirs.append(across)
        last = yield self.x(mine[3][:half]), self.z(theirs[2][half:])
        return mine + theirs + list(last)

    def scatter(self, pieces):
        mine, theirs = pieces[:4], list(pieces[4:])
        half = mine[0].shape[0] // 2
        came, passed = yield self.x(theirs[1][:half]), self.z(theirs[1][half:])
        theirs[2] = jnp.concatenate([theirs[2][:half], add(theirs[2][half:], passed)], axis=0)
        total = jnp.concatenate([add(mine[1][:half], came), mine[1][half:]], axis=0)
        for k in (2, 3, 0):
            came, passed = yield self.x(after(theirs[k], came)), self.z(total)
            total = (mine[k].astype(F32) + came.astype(F32) + passed.astype(F32)).astype(BF16)
        return total

    def sum_all(self, a):
        for bit in (1, 2, 4):
            (came,) = yield (lax.ppermute(a, "dp", [(i, i ^ bit) for i in range(8)]),)
            a = a + came
        return a


class Whole:
    def __init__(self, height):
        count = lax.axis_size("dp")
        self.heights = [height * count]
        self.slots = self.pieces = place_table([[0]] * count)

    def gather(self, own):
        return (yield [lax.all_gather(own, "dp", axis=0, tiled=True)])

    def scatter(self, pieces):
        return (yield [lax.psum_scatter(pieces[0], "dp", scatter_dimension=0, tiled=True)])[0]

    def sum_all(self, a):
        return (yield [lax.psum(a, "dp")])[0]


def inverse_rms(h):
    return lax.rsqrt(jnp.mean(h * h, axis=-1, keepdims=True) + EPS)


def lanes(row, count=Q):
    return jnp.pad(row, ((0, 0), (0, count - row.shape[1])))


def local(boundary, norm_gain, in_zx, in_bc, in_dt, conv_x, conv_bc, dt_bias, a_log, d_skip, gate_gain, out_w):
    p, t = lax.axis_index("pipe"), lax.axis_index("tensor")
    height = in_zx.shape[1]
    dp = (Ring if lax.axis_size("dp") == 8 else Whole)(height)
    tokens, part = boundary.shape[1:]
    width = 2 * part
    half = gate_gain.shape[1]
    inner = half // 2
    full_inner = 2 * half
    heads = dt_bias.shape[1] // 2
    both = ("pipe", "tensor")

    def mine(first, second):
        return jnp.where(t == 0, first, second)

    def core_swap(a):
        return lax.ppermute(a, "tensor", SWAP)

    def chip_swap(a):
        return lax.ppermute(a, "pipe", SWAP)

    def side(a, which, axis):
        size = a.shape[axis] // 2
        return lax.dynamic_slice_in_dim(a, which * size, size, axis)

    def all_four(a):
        (b,) = yield (chip_swap(a),)
        two = jnp.where(p == 0, jnp.stack([a, b]), jnp.stack([b, a]))
        (four,) = yield (core_swap(two),)
        return mine(jnp.stack([two, four], axis=1), jnp.stack([four, two], axis=1))

    turned = out_w[0].T
    sources = []
    for q in range(2):
        cols = slice(q * inner, (q + 1) * inner)
        sources.append(jnp.concatenate(
            [in_zx[0, :, 0, cols], in_zx[0, :, 1, cols], turned[:, cols], in_bc[0],
             lanes(in_dt[0][:, q * heads : (q + 1) * heads])], axis=1))
    routes = [[[(0, 0), (1, 2)], [(0, 1), (1, 3)]], [[(2, 0), (3, 2)], [(2, 1), (3, 3)]]]
    own = [mine(*[lax.ppermute(a, both, r) for a, r in zip(sources, route)]) for route in routes]

    def packed(q):
        cols, own = slice(q * inner, (q + 1) * inner), slice(q * heads, (q + 1) * heads)
        steps = [dt_bias[:, own], -jnp.exp(a_log[:, own]) * LOG2E]
        steps = jnp.concatenate([jnp.pad(a, ((0, 0), (0, Q - heads))) for a in steps] + [jnp.zeros((3, Q), F32)], axis=0)
        shared = jnp.concatenate([conv_bc[0], steps], axis=1)
        shared = jnp.concatenate([shared, jnp.zeros((5, inner - 3 * Q), F32)], axis=1)
        top = [conv_x[0][:, cols], gate_gain[:, cols], jnp.repeat(d_skip[:, own], HS, axis=1), jnp.zeros((1, inner), F32)]
        return jnp.concatenate([*top, shared, jnp.zeros((1, inner), F32), norm_gain.reshape(2, inner)], axis=0)

    one = jnp.stack([packed(0), packed(1)])

    def ends_lane(here):
        there = chip_swap(here)
        yield ()
        yield ()
        (there,) = yield (there,)
        ours = [jnp.where(p == 0, here, there), jnp.where(p == 0, there, here)]
        others = yield [core_swap(a) for a in ours]

        def rows(a, b, which):
            left, right = (c.reshape(2, 2, HALF, part) for c in (a, b))
            left, right = (lax.dynamic_index_in_dim(c, which, 1, keepdims=False).reshape(2 * HALF, part) for c in (left, right))
            return mine(jnp.concatenate([left, right], axis=1), jnp.concatenate([right, left], axis=1))

        return [(rows(a, b, t), rows(a, b, 1 - t)) for a, b in zip(ours, others)]

    one, here, *own = lax.optimization_barrier((one, boundary[0], *own))
    rounds = Rounds(weights=dp.gather(own[0]), params=all_four(one), ends=ends_lane(here))
    rounds.step(3)
    mark = rounds.mark
    weights0 = rounds.finish("weights")
    params = rounds.finish("params")
    hidden0, grad1 = rounds.finish("ends")

    def layer_params(layer):
        mine = lax.dynamic_slice(params, (layer, p, t, 0, 0), (1, 1, 1, 16, inner))[0, 0, 0]
        return mine[14:].reshape(1, width), mine

    params = [layer_params(0), layer_params(1)]

    starts, slots = dp.pieces, dp.slots

    def over_cores(my, other):
        return add(my, core_swap(other))

    def in_blocks(pair):
        return [(a, s) for s in range(2) for a in pair]

    def inverse_gate(squares):
        return lax.rsqrt(squares / full_inner + EPS)

    def columns(r, dot):
        return lanes(jnp.stack([r, r**3 * dot / full_inner], axis=1))

    def kept(r):
        return lax.dynamic_index_in_dim(r.reshape(2, 2, HALF), t, 1, keepdims=False).reshape(-1)

    def first_lane(sends, ss):
        *sends, ss = yield (*sends, ss)
        came, more = yield core_swap(sends[1]), chip_swap(ss)
        summed, ss = add(sends[0], came), ss + more
        came = chip_swap(summed)
        (more,) = yield (core_swap(ss),)
        (came,) = yield (came,)
        return summed.astype(F32) + came.astype(F32), ss + more

    rounds = Rounds(weights=dp.gather(after(own[1], *mark)))
    sends, (ss0, *saved0) = layer_forward(in_blocks(hidden0), params[0][0], params[0][1], starts, weights0)
    rounds.add(first=first_lane(sends, ss0[0].reshape(8, -1)))
    weights1 = rounds.finish("weights")
    mixed0, ss0 = rounds.finish("first")
    r0 = inverse_gate(ss0.reshape(-1))
    hidden0_my = hidden0[0].astype(F32)
    hidden1_my = (hidden0_my + kept(r0)[:, None] * mixed0).astype(BF16)
    hidden1 = (hidden1_my, core_swap(hidden1_my))
    top_sends, (ss1, *saved1, dot1) = layer_forward(
        in_blocks(hidden1), params[1][0], params[1][1], starts, weights1, in_blocks(grad1))
    ss1, dot1 = lax.psum(jnp.stack([ss1[0], dot1[0]]), both)
    r1 = inverse_gate(ss1)

    def rms_back(dn, h, gain):
        scale = inverse_rms(h)
        pulled = dn * gain
        return scale * pulled - h * scale**3 * jnp.mean(pulled * h, axis=-1, keepdims=True), jnp.sum(dn * h * scale, axis=0)

    rows = [slice(s * LEN, (s + 1) * LEN) for s in range(2)]
    mid = [slice(s * HALF, (s + 1) * HALF) for s in range(2)]

    def backward1(s, begin):
        return layer_backward([(a, s) for a in grad1], columns(r1[rows[s]], dot1[rows[s]]), saved1, s, params[1][1], begin, weights1)

    def down(s, summed, came):
        dn = summed.astype(F32) + came.astype(F32)
        dh, gng = rms_back(dn, hidden1_my[mid[s]].astype(F32), params[1][0])
        my = (grad1[0][mid[s]].astype(F32) + dh).astype(BF16)
        return my, jnp.sum(my.astype(F32) * mixed0[mid[s]], axis=1), gng

    def both_dots(dot, other):
        return mine(jnp.concatenate([dot, other]), jnp.concatenate([other, dot]))

    def shared_halves(outs):
        dsh = jnp.concatenate([o[3] for o in outs], axis=0)
        return side(dsh, t, 1), core_swap(side(dsh, 1 - t, 1))

    def all_grads(dout, hidden, gain, outs, shared, begin, heights):
        extra = [jnp.concatenate([shared[rows[s]], outs[s][4]], axis=1) for s in range(2)]
        rhs = [[o[k] for o in outs] for k in (2, 0, 1)] + [extra]
        return weight_grads(dout, hidden, gain, rhs, begin, heights)

    sends, outs = backward1(0, starts)
    back1 = [outs]
    summed_a = add(sends[0], core_swap(sends[1]))
    came_a = chip_swap(summed_a)
    sends, outs = backward1(1, after(starts, summed_a))
    back1.append(outs)
    came, came_a, shared_came = lax.optimization_barrier((core_swap(sends[1]), came_a, shared_halves(back1)[1]))
    summed_b = add(sends[0], came)
    came_b = chip_swap(summed_b)
    my_a, dot_a, gng_a = down(0, summed_a, came_a)
    other_a, other_dot = lax.optimization_barrier((core_swap(my_a), core_swap(dot_a)))
    dot_a = both_dots(dot_a, other_dot)
    wide1 = all_grads(in_blocks(grad1), in_blocks(hidden1), params[1][0], back1, add(shared_halves(back1)[0], shared_came),
                      after(slots, other_a, summed_b), dp.heights)
    came_b, *wide1 = lax.optimization_barrier((came_b, *wide1))
    my_b, dot_b, gng_b = down(1, summed_b, came_b)
    gng1 = gng_a + gng_b

    def backward0(s, my, other, dot, begin):
        return layer_backward([(my, 0), (other, 0)], columns(r0[rows[s]], dot), saved0, s, params[0][1], begin, weights0)

    def once(*arrays):
        return (yield arrays)

    def top_lane():
        (came,) = yield (core_swap(after(top_sends[1], my_b)),)
        top = add(top_sends[0], came)
        passed = lax.ppermute(top, "pipe", [(0, 1)])
        yield ()
        (passed,) = yield (passed,)
        mixed = top.astype(F32) + passed.astype(F32)
        return (hidden1_my.astype(F32) + kept(r1)[:, None] * mixed).astype(BF16)

    def first_down(summed):
        passed = lax.ppermute(summed, "pipe", [(1, 0)])
        yield ()
        (passed,) = yield (passed,)
        dn = summed.astype(F32) + passed.astype(F32)
        dh, _ = rms_back(dn, hidden0_my, params[0][0])
        end = jnp.where(p == 0, (jnp.concatenate([my_a, my_b], axis=0).astype(F32) + dh).astype(BF16), rounds.results["top"])
        (came,) = yield (core_swap(side(end, 1 - t, 1)),)
        came, keep = came.reshape(2, HALF, part), side(end, t, 1).reshape(2, HALF, part)
        return mine(jnp.stack([keep, came], axis=1), jnp.stack([came, keep], axis=1)).reshape(1, tokens, part)

    def home(result, layer):
        pairs = [[(0, 0), (2, 1)], [(1, 0), (3, 1)]] if layer == 0 else [[(0, 2), (2, 3)], [(1, 2), (3, 3)]]
        return [lax.ppermute(result, both, pair) for pair in pairs]

    def wide_lane(pieces, layer):
        total = yield from dp.scatter(pieces)
        return (yield home(total, layer))

    def small(outs, gng):
        gcx, gcbc, gdt = (a + b for a, b in zip(outs[0][5:], outs[1][5:]))
        own = [gcx[:5].reshape(-1), gcx[6], gcx[5].reshape(heads, HS).sum(axis=1), gdt[0, :heads], gdt[1, :heads]]
        own = jnp.concatenate(own)
        own = jnp.pad(own, (0, -own.shape[0] % Q))
        return jnp.concatenate([own, gng, gcbc[:5].reshape(-1)]).reshape(-1, Q)

    def small_lane(parts):
        total = yield from dp.sum_all(parts)
        return (yield from all_four(total))

    rounds = Rounds(top=top_lane(), wide1=wide_lane(wide1, 1))
    sends_a, outs_a = backward0(0, my_a, other_a, dot_a, after(starts, wide1[0]))
    rounds.add(now=once(core_swap(my_b), core_swap(dot_b), *sends_a))
    rounds.step()
    other_b, other_dot, *sends_a = rounds.results["now"]
    sends_b, outs_b = backward0(1, my_b, other_b, both_dots(dot_b, other_dot), after(starts, other_b))
    rounds.add(now=once(core_swap(sends_a[1]), *sends_b))
    rounds.step()
    came, *sends_b = rounds.results["now"]
    back0 = [outs_a, outs_b]
    summed_a = add(sends_a[0], came)
    own_shared, shared = shared_halves(back0)
    came, shared = lax.optimization_barrier((core_swap(sends_b[1]), shared))
    summed = jnp.concatenate([summed_a, add(sends_b[0], came)], axis=0)
    wide0 = all_grads([(my_a, 0), (other_a, 0), (my_b, 0), (other_b, 0)], in_blocks(hidden0), params[0][0], back0,
                      add(own_shared, shared), after(slots, summed), dp.heights)
    gng0 = jnp.sum(summed.astype(F32) * hidden0_my * inverse_rms(hidden0_my), axis=0)
    rounds.add(now=once(summed, *wide0))
    rounds.step()
    summed, *wide0 = rounds.results["now"]
    gng1 = jnp.where(p == 0, gng1, jnp.zeros_like(gng1))
    rounds.add(ends=first_down(summed), wide0=wide_lane(wide0, 0), small=small_lane(jnp.stack([small(back0, gng0), small(back1, gng1)])))
    rounds.step(4)
    ends, sums = rounds.finish("ends"), rounds.finish("small")
    quarters = [jnp.where(p == 0, a, b) for a, b in zip(rounds.finish("wide0"), rounds.finish("wide1"))]

    def columns_of(first, size):
        return [a[:, first : first + size].astype(F32) for a in quarters]

    g_out = jnp.concatenate(columns_of(0, inner), axis=1).T
    g_zx = jnp.stack([jnp.concatenate(columns_of(k * inner, inner), axis=1) for k in (1, 2)], axis=1)
    g_bc = jnp.concatenate(columns_of(3 * inner, Q), axis=1)
    g_dt = jnp.concatenate(columns_of(3 * inner + Q, heads), axis=1)
    g_bc = g_bc + core_swap(g_bc)
    sums = lax.dynamic_index_in_dim(sums, p, 2, keepdims=False).reshape(2, 2, -1)
    own_size = sums.shape[2] - width - 10 * Q
    shared = sums[:, :, own_size:].sum(axis=(0, 1))
    holder = lax.dynamic_index_in_dim(sums, t, 0, keepdims=False)
    at = 5 * inner
    g_cx = jnp.concatenate([holder[k, :at].reshape(5, inner) for k in range(2)], axis=1)
    g_gain = holder[:, at : at + inner].reshape(-1)
    at += inner
    g_dsk, g_dtb, g_alog = (holder[:, at + k * heads : at + (k + 1) * heads].reshape(-1) for k in range(3))
    return (ends, shared[:width][None], g_zx[None], g_bc[None], g_dt[None], g_cx[None], shared[width:].reshape(5, 2 * Q)[None],
            g_dtb[None], g_alog[None], g_dsk[None], g_gain[None], g_out[None])


def solution(mesh):
    pipe, both, wide = ("pipe", "dp", "tensor"), ("pipe", "tensor"), P("pipe", None, "tensor")
    return jax.shard_map(
        local, mesh=mesh,
        in_specs=(P(*pipe), P("pipe", None), P("pipe", "dp", None, "tensor"), P("pipe", "dp", None), P(*pipe), wide,
                  P("pipe", None, None), P(*both), P(*both), P(*both), P(*both), P("pipe", "tensor", "dp")),
        out_specs=(P(*pipe), P("pipe", None), P("pipe", "dp", None, "tensor"), P("pipe", "dp", None), P(*pipe), wide,
                   P("pipe", None, None), P(*both), P(*both), P(*both), P(*both), P("pipe", "tensor", "dp")),
        check_vma=False,
    )
```

```python
import functools
import jax
import jax.numpy as jnp
from jax import lax
from jax.experimental import pallas as pl
from jax.experimental.pallas import tpu as pltpu
from jax.sharding import PartitionSpec as P

LEN = 512
Q = 128
GW = 256
HS = 64
EPS = 1e-05
LOG2E = 1.4426950408889634
F32 = jnp.float32
BF16 = jnp.bfloat16
NEG = -1e30
FORWARD_US = 25
BACKWARD_US = 40
GRADS_US = 20


def mm(a, b):
    return jnp.dot(a, b, preferred_element_type=F32)


def mm_nt(a, b):
    return lax.dot_general(a, b, (((1,), (1,)), ((), ())), preferred_element_type=F32)


def mm_tn(a, b):
    return lax.dot_general(a, b, (((0,), (0,)), ((), ())), preferred_element_type=F32)


def halves(a):
    high = a.astype(BF16)
    return high, (a - high.astype(F32)).astype(BF16)


def mm_split(a, b):
    high, rest = halves(a)
    return mm(high, b) + mm(rest, b)


def sigmoid(a):
    return 1.0 / (1.0 + jnp.exp2(a * (-LOG2E)))


def iota2(shape, axis):
    return lax.broadcasted_iota(jnp.int32, shape, axis)


def spread_matrix(transposed=False):
    if transposed:
        return (iota2((GW, Q), 0) // HS == iota2((GW, Q), 1)).astype(F32).astype(BF16)
    return (iota2((Q, GW), 1) // HS == iota2((Q, GW), 0)).astype(F32).astype(BF16)


def lower_ones():
    return (iota2((Q, Q), 0) >= iota2((Q, Q), 1)).astype(F32)


def shifted(ext, by):
    if by == 0:
        return ext[8:, :]
    return pltpu.roll(ext, by, 0)[8:, :]


def conv_at(pad_ref, start, taps):
    ext = pad_ref[pl.ds(pl.multiple_of(start, 8), Q + 8), :]
    out = taps[4:5, :]
    for j in range(4):
        out = out + taps[j : j + 1, :] * shifted(ext, 3 - j)
    return out


def expand(parts, spread):
    high, rest = halves(jnp.concatenate(parts, axis=0))
    out = mm(high, spread) + mm(rest, spread)
    return [out[k * Q : (k + 1) * Q] for k in range(len(parts))]


def weight_copies(starts, pieces, rest_at, bufs, sems, groups):
    wbuf, obuf, wbc, wdt = bufs
    inner = groups * GW
    zx, out, narrow = [[] for _ in range(groups)], [[] for _ in range(groups)], []
    for k in range(len(pieces) // 2):
        front, back = pieces[k], pieces[len(pieces) // 2 + k]
        here = pl.ds(pl.multiple_of(starts[k], 16), front.shape[0])
        for g in range(groups):
            for part in range(2):
                zx[g].append(pltpu.make_async_copy(
                    front.at[:, pl.ds(part * inner + g * GW, GW)], wbuf.at[g, here, pl.ds(part * GW, GW)], sems.at[k, 3 * g + part]))
            out[g].append(pltpu.make_async_copy(
                back.at[:, pl.ds(rest_at + g * GW, GW)], obuf.at[g, here, :], sems.at[k, 3 * g + 2]))
        last, at = 3 * groups, rest_at + inner
        narrow.append(pltpu.make_async_copy(back.at[:, pl.ds(at, 2 * Q)], wbc.at[here, :], sems.at[k, last]))
        narrow.append(pltpu.make_async_copy(back.at[:, pl.ds(at + 2 * Q, Q)], wdt.at[here, :], sems.at[k, last + 1]))
    return zx, out, narrow


def weight_scratch(pieces, groups, width):
    vm = pltpu.VMEM
    return [vm((groups, width, 2 * GW), BF16), vm((groups, width, GW), BF16), vm((width, 2 * Q), BF16), vm((width, Q), BF16),
            pltpu.SemaphoreType.DMA((len(pieces) // 2, 3 * groups + 2))]


def rest_column(pieces, inner):
    return 2 * inner if pieces[0].shape == pieces[len(pieces) // 2].shape else 0


def each_group(copies, act):
    for k, mine in enumerate(copies):

        @pl.when(pl.program_id(0) == k)
        def _():
            for c in mine:
                act(c)


HALF = LEN // 2
WIDE = 8 + LEN
PER = LEN // Q


def half_rows(s, which):
    return pl.ds(pl.multiple_of(s * LEN + which * HALF, HALF), HALF)


def chunk_rows(s, cc):
    return pl.ds(pl.multiple_of(s * LEN + cc * Q, Q), Q)


def steps_of(stin, dtb, rate, tri):
    pre = stin + dtb
    step = jnp.maximum(pre, 0.0) + jnp.log1p(jnp.exp(-jnp.abs(pre)))
    cumulative = jnp.dot(tri, step * rate, precision=lax.Precision.HIGHEST, preferred_element_type=F32)
    return pre, step, cumulative, cumulative - jnp.log2(step)


def fwd_kernel(n, rest_at, nseq, top, groups, unroll, starts, *refs):
    h_refs, (ng_ref, col_ref, all_ref), refs = refs[: 2 * nseq], refs[2 * nseq : 2 * nseq + 3], refs[2 * nseq + 3 :]
    cx_ref, gain_ref, dsk_ref, cbc_ref, dtb_ref, rate_ref = small_refs(col_ref, all_ref)
    if top:
        dout_refs, refs = refs[: 2 * nseq], refs[2 * nseq :]
    pieces, refs = refs[:n], refs[n:]
    p_refs, refs = refs[:2], refs[2:]
    (ss_ref, gate_ref, val_ref, y_ref, shin_ref, stin_ref, ht_ref), refs = refs[:7], refs[7:]
    if top:
        dot_ref, refs = refs[0], refs[1:]
    bufs, sems, refs = refs[:4], refs[4], refs[5:]
    wbuf, obuf, wbc_ref, wdt_ref = bufs
    (nrm_ref, vpad, csc, btsc, ssc, cum, wx, ec, cjt, gn, hst, ssum) = refs[:12]
    dsum, dgn = refs[12:] if top else (None, None)
    g = pl.program_id(0)
    core = starts[n // 2]
    sides = [(s, which) for s in range(nseq) for which in (core, 1 - core)]
    gate_copies, out_copies, narrow_copies = weight_copies(starts, pieces, rest_at, bufs, sems, groups)

    @pl.when(g == 0)
    def _():
        for c in narrow_copies:
            c.start()
        for k in range(groups):
            for c in gate_copies[k] + out_copies[k]:
                c.start()
        for (s, which), h_ref in zip(sides, h_refs):

            def norm_rows(c, carry):
                h = h_ref[pl.ds(pl.multiple_of(c * Q, Q), Q), :].astype(F32)
                scale = lax.rsqrt(jnp.mean(h * h, axis=-1, keepdims=True) + EPS)
                at = pl.multiple_of(s * LEN + which * HALF + c * Q, Q)
                nrm_ref[pl.ds(at, Q), :] = (h * scale * ng_ref[...]).astype(BF16)
                return carry

            lax.fori_loop(0, HALF // Q, norm_rows, 0, unroll=True)
        for c in narrow_copies:
            c.wait()
        ssum[...] = jnp.zeros_like(ssum)
        if top:
            dsum[...] = jnp.zeros_like(dsum)
        for s in range(nseq):
            rows = pl.ds(s * LEN, LEN)
            normed = nrm_ref[rows, :]
            shin = mm(normed, wbc_ref[...])
            shin_ref[rows, :] = shin
            vpad[pl.ds(s * WIDE, 8), :] = jnp.zeros((8, GW), F32)
            vpad[pl.ds(s * WIDE + 8, LEN), :] = shin
            stin_ref[rows, :] = mm(normed, wdt_ref[...])
        tri = lower_ones()
        taps = cbc_ref[...]

        def shared_rows(cc, carry):
            for s in range(nseq):
                c, rows = s * PER + cc, chunk_rows(s, cc)
                pre = conv_at(vpad, s * WIDE + cc * Q, taps)
                act = (pre * sigmoid(pre)).astype(BF16)
                bmat, cmat = act[:, :Q], act[:, Q:]
                bt = bmat.astype(F32).T.astype(BF16)
                btsc[c] = bt
                csc[rows, :] = cmat
                ssc[c] = mm(cmat, bt)
                _, _, cumulative, cj = steps_of(stin_ref[rows, :], dtb_ref[...], rate_ref[...], tri)
                cum[rows, :] = cumulative
                ec[rows, :] = jnp.exp2(cumulative)
                wx[rows, :] = jnp.exp2(cumulative[Q - 1 : Q, :] - cj)
                cjt[c] = cj.T[:16, :]
            return carry

        lax.fori_loop(0, PER, shared_rows, 0, unroll=unroll)

    each_group(gate_copies, lambda c: c.wait())
    each_group(out_copies, lambda c: c.wait())
    for s in range(nseq):
        rows = pl.ds(s * LEN, LEN)
        normed = nrm_ref[rows, :]
        gate_ref[rows, :] = mm(normed, wbuf[g, :, :GW]).astype(BF16)
        value = mm(normed, wbuf[g, :, GW:]).astype(BF16)
        val_ref[rows, :] = value
        vpad[pl.ds(s * WIDE, 8), :] = jnp.zeros((8, GW), F32)
        vpad[pl.ds(s * WIDE + 8, LEN), :] = value.astype(F32)
    if top:
        for (s, which), ref in zip(sides, dout_refs):
            dgn[half_rows(s, which), :] = mm(ref[...], obuf[g])
    taps = cx_ref[...]
    spread = spread_matrix()
    shift = lax.rem(Q - 4 * g, Q)
    causal = iota2((Q, Q), 0) >= iota2((Q, Q), 1)
    lane = iota2((Q, Q), 1)
    hst[...] = jnp.zeros_like(hst)

    def one(s, cc):
        c, rows = s * PER + cc, chunk_rows(s, cc)
        pre = conv_at(vpad, s * WIDE + cc * Q, taps)
        x = pre * sigmoid(pre)
        xb = x.astype(BF16)
        here = pltpu.roll(cum[rows, :], shift, 1)
        wxe, ece = expand([pltpu.roll(wx[rows, :], shift, 1), pltpu.roll(ec[rows, :], shift, 1)], spread)
        old = hst[s]
        state = old.astype(BF16)
        ht_ref[c] = state
        scores = ssc[c]
        outside = mm(csc[rows, :], state) * ece
        hst[s] = old * ece[Q - 1 : Q, :] + mm(btsc[c], (x * wxe).astype(BF16))
        parts = []
        for pair in range(GW // Q):
            mixers = []
            for half in range(2):
                i = 2 * pair + half
                cj = cjt[c, pl.ds(4 * g + i, 1), :]
                gap = jnp.where(causal, here[:, i : i + 1] - cj, NEG)
                mixers.append((scores * jnp.exp2(gap)).astype(BF16))
            x2 = xb[:, pair * Q : (pair + 1) * Q]
            zero = jnp.zeros_like(x2)
            stacked = jnp.concatenate([jnp.where(lane < HS, x2, zero), jnp.where(lane < HS, zero, x2)], axis=0)
            parts.append(mm(jnp.concatenate(mixers, axis=1), stacked))
        y = jnp.concatenate(parts, axis=1) + outside
        y_ref[rows, :] = y
        gate = gate_ref[rows, :].astype(F32)
        gated = (y + dsk_ref[...] * x) * (gate * sigmoid(gate))
        scaled = gated * gain_ref[...]
        gn[g, rows, :] = scaled.astype(BF16)
        sq = gated * gated
        ssum[rows, :] += sq[:, :Q] + sq[:, Q:]
        if top:
            prod = scaled * dgn[rows, :]
            dsum[rows, :] += prod[:, :Q] + prod[:, Q:]

    def chunk(cc, carry):
        for s in range(nseq):
            one(s, cc)
        return carry

    lax.fori_loop(0, PER, chunk, 0, unroll=unroll)

    @pl.when(g == groups - 1)
    def _():
        ones = jnp.ones((8, Q), BF16)
        high, rest = halves(ssum[...])
        ss_ref[...] = mm_nt(ones, high) + mm_nt(ones, rest)
        if top:
            high, rest = halves(dsum[...])
            dot_ref[...] = mm_nt(ones, high) + mm_nt(ones, rest)
        for i, (s, which) in enumerate(sides):
            rows = half_rows(s, which)
            total = mm_nt(gn[0, rows, :], obuf[0])
            for k in range(1, groups):
                total = total + mm_nt(gn[k, rows, :], obuf[k])
            p_refs[i % 2][pl.ds(s * HALF, HALF), :] = total.astype(BF16)


def grid_call(kernel, name, prefetch, groups, in_specs, out_specs, out_shape, scratch, args, micros):
    return pl.pallas_call(
        kernel,
        grid_spec=pltpu.PrefetchScalarGridSpec(
            num_scalar_prefetch=1, grid=(groups,), in_specs=in_specs, out_specs=out_specs, scratch_shapes=scratch),
        out_shape=out_shape,
        compiler_params=pltpu.CompilerParams(dimension_semantics=("arbitrary",), vmem_limit_bytes=60 << 20),
        cost_estimate=pl.CostEstimate(flops=int(micros * 1.15e9), bytes_accessed=20 << 20, transcendentals=0),
        name=name,
    )(prefetch, *args)


def full(shape):
    zeros = (0,) * len(shape)
    return pl.BlockSpec(shape, lambda g, *_: zeros)


def col(rows, at=0):
    return pl.BlockSpec((rows, GW), lambda g, *_: (at, g))


def row_block(rows, cols, at):
    return pl.BlockSpec((rows, cols), lambda g, *_: (at, 0))


ANYWHERE = pl.BlockSpec(memory_space=pl.ANY)


def half_specs(operands):
    return [row_block(HALF, a.shape[1], at) for a, at in operands]


def small_refs(by_group, every):
    return (by_group.at[0:5, :], by_group.at[5:6, :], by_group.at[6:7, :], every.at[8:13, 0 : 2 * Q],
            every.at[8:9, 2 * Q : 3 * Q], every.at[9:10, 2 * Q : 3 * Q])


def small_specs(small):
    return [col(8), full(small.shape)]


def layer_forward(hs, ng, small, starts, pieces, douts=(), unroll=4):
    width = hs[0][0].shape[1]
    inner = small.shape[1]
    nseq, n, top, groups = len(hs) // 2, len(pieces), len(douts) > 0, inner // GW
    rows, chunks = nseq * LEN, nseq * PER
    in_specs = half_specs(hs) + [full(ng.shape)] + small_specs(small) + half_specs(douts) + [ANYWHERE] * n
    args = [a for a, _ in hs] + [ng, small, small] + [a for a, _ in douts] + [*pieces]
    sds = jax.ShapeDtypeStruct
    out_shape = [sds((nseq * HALF, width), BF16)] * 2 + [
        sds((8, rows), F32), sds((rows, inner), BF16), sds((rows, inner), BF16), sds((rows, inner), F32),
        sds((rows, 2 * Q), F32), sds((rows, Q), F32), sds((chunks, Q, inner), BF16)]
    out_specs = [full((nseq * HALF, width))] * 2 + [
        full((8, rows)), col(rows), col(rows), col(rows), full((rows, 2 * Q)), full((rows, Q)),
        pl.BlockSpec((chunks, Q, GW), lambda g, *_: (0, 0, g))]
    if top:
        out_shape.append(sds((8, rows), F32))
        out_specs.append(full((8, rows)))
    vm = pltpu.VMEM
    scratch = weight_scratch(pieces, groups, width) + [
        vm((rows, width), BF16), vm((nseq * WIDE, GW), F32), vm((rows, Q), BF16), vm((chunks, Q, Q), BF16), vm((chunks, Q, Q), F32),
        vm((rows, Q), F32), vm((rows, Q), F32), vm((rows, Q), F32), vm((chunks, 16, Q), F32),
        vm((groups, rows, GW), BF16), vm((nseq, Q, GW), F32), vm((rows, Q), F32)]
    if top:
        scratch += [vm((rows, Q), F32), vm((rows, GW), F32)]
    out = grid_call(functools.partial(fwd_kernel, n, rest_column(pieces, inner), nseq, top, groups, unroll), "mixer_forward", starts, groups, in_specs, out_specs,
                    out_shape, scratch, args, FORWARD_US)
    return out[:2], out[2:]


def colsum(a):
    return jnp.sum(a, axis=0, keepdims=True)


def ahead(ext, by):
    if by == 0:
        return ext[:Q, :]
    return pltpu.roll(ext, Q + 8 - by, 0)[:Q, :]


def conv_back(dconv, after, taps):
    ext = jnp.concatenate([dconv, after], axis=0)
    out = taps[3:4, :] * dconv
    for j in range(3):
        out = out + taps[j : j + 1, :] * ahead(ext, 3 - j)
    return out


def bwd_kernel(n, rest_at, nseq, groups, unroll, starts, *refs):
    do_refs, refs = refs[: 2 * nseq], refs[2 * nseq :]
    (rq_rows, gate_ref, val_ref, y_ref, ht_ref, shin_ref, stin_ref), refs = refs[:7], refs[7:]
    cx_ref, gain_ref, dsk_ref, cbc_ref, dtb_ref, rate_ref = small_refs(*refs[:2])
    refs = refs[2:]
    pieces, refs = refs[:n], refs[n:]
    dn_refs, refs = refs[: 2 * nseq], refs[2 * nseq :]
    (dg_ref, dv_ref, gnorm_ref, own_ref, send_ref, ddt_ref, small_ref), refs = refs[:7], refs[7:]
    gcx_ref, tail_ref = small_ref.at[0:8, :], small_ref.at[8:16, :]
    bufs, sems, refs = refs[:4], refs[4], refs[5:]
    wbuf, obuf, wbc_ref, wdt_ref = bufs
    (vpad, spad, bsc, csc, ctsc, ssc, cjs, wx, ec, cumt, dgn, dzx, dhst, nxt, dstm, dbs, dcs, dcum, xgs, rq_ref, dsh_ref) = refs
    g = pl.program_id(0)
    core = starts[n // 2]
    sides = [(s, which) for s in range(nseq) for which in (core, 1 - core)]
    gate_copies, out_copies, narrow_copies = weight_copies(starts, pieces, rest_at, bufs, sems, groups)

    @pl.when(g == 0)
    def _():
        for k in range(groups):
            for c in out_copies[k]:
                c.start()
        for c in narrow_copies:
            c.start()
        for k in range(groups):
            for c in gate_copies[k]:
                c.start()
        for s in range(nseq):
            spad[pl.ds(s * WIDE, 8), :] = jnp.zeros((8, GW), F32)
            spad[pl.ds(s * WIDE + 8, LEN), :] = shin_ref[pl.ds(s * LEN, LEN), :]
        tri = lower_ones()
        taps = cbc_ref[...]

        def shared_rows(cc, carry):
            for s in range(nseq):
                c, rows = s * PER + cc, chunk_rows(s, cc)
                pre = conv_at(spad, s * WIDE + cc * Q, taps)
                act = (pre * sigmoid(pre)).astype(BF16)
                bmat, cmat = act[:, :Q], act[:, Q:]
                ct = cmat.astype(F32).T.astype(BF16)
                bsc[rows, :] = bmat
                csc[rows, :] = cmat
                ctsc[c] = ct
                ssc[c] = mm(bmat, ct)
                _, _, cumulative, cj = steps_of(stin_ref[rows, :], dtb_ref[...], rate_ref[...], tri)
                cjs[rows, :] = cj
                ec[rows, :] = jnp.exp2(cumulative)
                wx[rows, :] = jnp.exp2(cumulative[Q - 1 : Q, :] - cj)
                cumt[c] = cumulative.T[:16, :]
                rq_ref[rows, :] = rq_rows[:, pl.ds(pl.multiple_of(s * LEN + cc * Q, Q), Q)].T
            return carry

        lax.fori_loop(0, PER, shared_rows, 0, unroll=unroll)
        for ref in (dstm, dbs, dcs, dcum, xgs):
            ref[...] = jnp.zeros_like(ref)

    each_group(out_copies, lambda c: c.wait())
    for (s, which), ref in zip(sides, do_refs):
        dgn[half_rows(s, which), :] = mm(ref[...], obuf[g])
    for s in range(nseq):
        vpad[pl.ds(s * WIDE, 8), :] = jnp.zeros((8, GW), F32)
        vpad[pl.ds(s * WIDE + 8, LEN), :] = val_ref[pl.ds(s * LEN, LEN), :].astype(F32)
    small_ref[...] = jnp.zeros_like(small_ref)
    dhst[...] = jnp.zeros_like(dhst)
    nxt[...] = jnp.zeros_like(nxt)
    taps = cx_ref[...]
    spread = spread_matrix()
    gather = spread_matrix(True)
    to_front = lax.rem(Q - 4 * g, Q)
    causal = iota2((Q, Q), 0) <= iota2((Q, Q), 1)
    lane = iota2((Q, Q), 1)
    last_row = iota2((Q, GW), 0) == Q - 1

    def one(s, cc):
        c, rows = s * PER + cc, chunk_rows(s, cc)
        start = pl.multiple_of(s * WIDE + cc * Q, 8)
        ext = vpad[pl.ds(start, Q + 8), :]
        taken = [shifted(ext, 3 - j) for j in range(4)]
        pre = taps[4:5, :]
        for j in range(4):
            pre = pre + taps[j : j + 1, :] * taken[j]
        sx = sigmoid(pre)
        x = pre * sx
        xb = x.astype(BF16)
        gate = gate_ref[rows, :].astype(F32)
        sg = sigmoid(gate)
        silu_gate = gate * sg
        y = y_ref[rows, :]
        dsk = dsk_ref[...]
        gain = gain_ref[...]
        mixed = y + dsk * x
        gated = mixed * silu_gate
        r = rq_ref[rows, 0:1]
        q = rq_ref[rows, 1:2]
        d_norm = dgn[rows, :]
        scaled = gated * r
        gnorm_ref[rows, :] = (scaled * gain).astype(BF16)
        d_gated = (r * gain) * d_norm - gated * q
        dmix = d_gated * silu_gate
        dgate = (d_gated * mixed * (sg * (1.0 + gate * (1.0 - sg)))).astype(BF16)
        dg_ref[rows, :] = dgate
        dzx[g, rows, :GW] = dgate
        dyb = dmix.astype(BF16)
        dyf = dyb.astype(F32)
        xf = xb.astype(F32)
        wxe, ece = expand([pltpu.roll(wx[rows, :], to_front, 1), pltpu.roll(ec[rows, :], to_front, 1)], spread)
        here = pltpu.roll(cjs[rows, :], to_front, 1)
        ecl = ece[Q - 1 : Q, :]
        state = ht_ref[c]
        dh = dhst[s]
        dhb = dh.astype(BF16)
        gx_state = mm(bsc[rows, :], dhb) * wxe
        dye = (dmix * ece).astype(BF16)
        dcs[rows, :] += mm_nt(dye, state)
        dbs[rows, :] += mm_nt((x * wxe).astype(BF16), dhb)
        ends = colsum(xf * gx_state) + ecl * colsum(state.astype(F32) * dh)
        dhst[s] = dh * ecl + mm(ctsc[c], dye)
        scores = ssc[c]
        dst = jnp.zeros((Q, Q), F32)
        parts = []
        for pair in range(GW // Q):
            x2 = xb[:, pair * Q : (pair + 1) * Q]
            dy2 = dyb[:, pair * Q : (pair + 1) * Q]
            zero = jnp.zeros_like(x2)
            xs = [jnp.where(lane < HS, x2, zero), jnp.where(lane < HS, zero, x2)]
            dys = [jnp.where(lane < HS, dy2, zero), jnp.where(lane < HS, zero, dy2)]
            mixers = []
            for half in range(2):
                i = 2 * pair + half
                ci = cumt[c, pl.ds(4 * g + i, 1), :]
                decay = jnp.exp2(jnp.where(causal, ci - here[:, i : i + 1], NEG))
                mixers.append((scores * decay).astype(BF16))
                dst = dst + mm_nt(xs[half], dy2) * decay
            parts.append(mm(jnp.concatenate(mixers, axis=1), jnp.concatenate(dys, axis=0)))
        dstm[c] += dst
        gx = jnp.concatenate(parts, axis=1) + gx_state
        to_heads = lax.rem(4 * g, Q)
        xg, yg = expand([xf * gx, jnp.where(last_row, dyf * y + ends, dyf * y)], gather)
        xgs[rows, :] += pltpu.roll(xg, to_heads, 1)
        dcum[rows, :] += pltpu.roll(yg - xg, to_heads, 1)
        dx = gx + dsk * dmix
        dconv = dx * (sx * (1.0 + pre * (1.0 - sx)))
        dvalue = conv_back(dconv, nxt[s], taps).astype(BF16)
        nxt[s] = dconv[:8, :]
        dv_ref[rows, :] = dvalue
        dzx[g, rows, GW:] = dvalue
        sums = [colsum(dconv * taken[j]) for j in range(4)]
        sums += [colsum(dconv), colsum(dmix * x), colsum(d_norm * scaled), jnp.zeros((1, GW), F32)]
        gcx_ref[...] += jnp.concatenate(sums, axis=0)

    def chunk(back, carry):
        for s in range(nseq):
            one(s, PER - 1 - back)
        return carry

    lax.fori_loop(0, PER, chunk, 0, unroll=unroll)

    @pl.when(g == groups - 1)
    def _():
        upper = (iota2((Q, Q), 0) <= iota2((Q, Q), 1)).astype(F32)
        taps = cbc_ref[...]
        nxt[...] = jnp.zeros_like(nxt)

        def shared_back(s, cc):
            c, rows = s * PER + cc, chunk_rows(s, cc)
            start = pl.multiple_of(s * WIDE + cc * Q, 8)
            ext = spad[pl.ds(start, Q + 8), :]
            taken = [shifted(ext, 3 - j) for j in range(4)]
            pre = taps[4:5, :]
            for j in range(4):
                pre = pre + taps[j : j + 1, :] * taken[j]
            sx = sigmoid(pre)
            dst = dstm[c]
            d_b = dbs[rows, :] + mm(dst.astype(BF16), csc[rows, :])
            d_c = dcs[rows, :] + mm(dst.T.astype(BF16), bsc[rows, :])
            dconv = jnp.concatenate([d_b, d_c], axis=1) * (sx * (1.0 + pre * (1.0 - sx)))
            back = conv_back(dconv, nxt[s], taps).astype(BF16)
            dsh_ref[rows, :] = back
            first = core == 0
            own_ref[rows, :] = jnp.where(first, back[:, :Q], back[:, Q:])
            send_ref[rows, :] = jnp.where(first, back[:, Q:], back[:, :Q])
            nxt[s] = dconv[:8, :]
            sums = [colsum(dconv * taken[j]) for j in range(4)] + [colsum(dconv)]
            da = jnp.dot(upper, dcum[rows, :], precision=lax.Precision.HIGHEST, preferred_element_type=F32)
            pre = stin_ref[rows, :] + dtb_ref[...]
            step = jnp.maximum(pre, 0.0) + jnp.log1p(jnp.exp(-jnp.abs(pre)))
            sig = sigmoid(pre)
            rate = rate_ref[...] * (1.0 / LOG2E)
            dpre = da * rate * sig + xgs[rows, :] * (sig / jnp.maximum(step, 1e-37))
            ddt_ref[rows, :] = dpre.astype(BF16)
            wide = jnp.zeros((1, GW - Q), F32)
            sums += [jnp.concatenate([a, wide], axis=1) for a in (colsum(dpre), colsum(step * da) * rate)]
            tail_ref[...] += jnp.concatenate(sums + [jnp.zeros((1, GW), F32)], axis=0)

        def back_rows(back, carry):
            for s in range(nseq):
                shared_back(s, PER - 1 - back)
            return carry

        lax.fori_loop(0, PER, back_rows, 0, unroll=unroll)
        for c in narrow_copies:
            c.wait()
        for k in range(groups):
            for c in gate_copies[k]:
                c.wait()
        for (s, which), ref in zip(sides, dn_refs):
            rows = half_rows(s, which)
            total = mm_nt(dsh_ref[rows, :], wbc_ref[...]) + mm_nt(ddt_ref[rows, :], wdt_ref[...])
            for k in range(groups):
                total = total + mm_nt(dzx[k, rows, :], wbuf[k])
            ref[...] = total.astype(BF16)


def layer_backward(douts, rq, saved, at, small, starts, pieces, unroll=4):
    gate, value, y, shin, stin, ht = saved
    width = douts[0][0].shape[1]
    inner = small.shape[1]
    nseq, n, groups = len(douts) // 2, len(pieces), inner // GW
    rows, chunks, at = nseq * LEN, nseq * PER, at // nseq
    in_specs = half_specs(douts) + [
        full(rq.shape), col(rows, at), col(rows, at), col(rows, at),
        pl.BlockSpec((chunks, Q, GW), lambda g, *_: (at, 0, g)), row_block(rows, 2 * Q, at), row_block(rows, Q, at)]
    in_specs += small_specs(small) + [ANYWHERE] * n
    args = [a for a, _ in douts] + [rq, gate, value, y, ht, shin, stin, small, small, *pieces]
    sds = jax.ShapeDtypeStruct
    out_shape = [sds((HALF, width), BF16)] * (2 * nseq) + [sds((rows, inner), BF16)] * 3 + [
        sds((rows, Q), BF16), sds((rows, Q), BF16), sds((rows, Q), BF16), sds((16, inner), F32)]
    out_specs = [full((HALF, width))] * (2 * nseq) + [col(rows)] * 3 + [full((rows, Q))] * 3 + [col(16)]
    vm = pltpu.VMEM
    scratch = weight_scratch(pieces, groups, width) + [
        vm((nseq * WIDE, GW), F32), vm((nseq * WIDE, GW), F32),
        vm((rows, Q), BF16), vm((rows, Q), BF16), vm((chunks, Q, Q), BF16), vm((chunks, Q, Q), F32),
        vm((rows, Q), F32), vm((rows, Q), F32), vm((rows, Q), F32), vm((chunks, 16, Q), F32),
        vm((rows, GW), F32), vm((groups, rows, 2 * GW), BF16), vm((nseq, Q, GW), F32), vm((nseq, 8, GW), F32),
        vm((chunks, Q, Q), F32), vm((rows, Q), F32), vm((rows, Q), F32), vm((rows, Q), F32), vm((rows, Q), F32),
        vm((rows, 8), F32), vm((rows, 2 * Q), BF16)]
    out = grid_call(functools.partial(bwd_kernel, n, rest_column(pieces, inner), nseq, groups, unroll), "mixer_backward", starts, groups, in_specs, out_specs,
                    out_shape, scratch, args, BACKWARD_US * nseq / 2)
    return out[: 2 * nseq], out[2 * nseq :]


def grad_kernel(steps, norms, starts, *refs):
    gain_ref, refs = refs[0], refs[1:]
    lhs, refs = refs[: 4 * len(norms)], refs[4 * len(norms) :]
    outs, (turned, whole) = refs[:-2], refs[-2:]
    g = pl.program_id(0)

    def turn(halves_of, norm):
        core = starts[starts.shape[0] - 1]
        for k, ref in enumerate(halves_of):
            base = k // 2 * LEN + (core if k % 2 == 0 else 1 - core) * HALF
            here = pl.ds(pl.multiple_of(base, HALF), HALF)
            if norm:
                h = ref[...].astype(F32)
                scale = lax.rsqrt(jnp.mean(h * h, axis=-1, keepdims=True) + EPS)
            for j in range(turned.shape[0] // GW):
                cols = pl.ds(j * GW, GW)
                part = ref[:, cols]
                if norm:
                    part = (part.astype(F32) * scale * gain_ref[:, cols]).astype(BF16)
                turned[cols, here] = part.T

    first, ready = 0, None
    for source, count, width in steps:
        rhs, outs = outs[:width], outs[width:]
        if source != ready:
            pl.when(g == first)(functools.partial(turn, lhs[4 * source : 4 * source + 4], norms[source]))
            ready = source

        @pl.when((g >= first) & (g < first + count))
        def _():
            both = jnp.concatenate([ref[...] for ref in rhs[:2]], axis=0)
            if width == 6:
                came, steps_in = (jnp.concatenate([ref[...] for ref in rhs[k : k + 2]], axis=0) for k in (2, 4))
                both = jnp.concatenate([(both.astype(F32) + came.astype(F32)).astype(BF16), steps_in], axis=1)
            whole[...] = mm(turned[...], both).astype(BF16)

        first += count
    for k, out in enumerate(outs):
        out[...] = whole[pl.ds(pl.multiple_of(starts[k], 16), out.shape[0]), :]


def weight_grads(lhs, norms, gain, rhs, starts, heights, micros):
    width = gain.shape[1]
    steps = [(source, max(arrays[0].shape[1] // GW, 1), len(arrays)) for source, arrays in rhs]
    total = sum(count for _, count, _ in steps)
    flat = [operand for source in lhs for operand in source]
    specs, first = [full(gain.shape)] + half_specs(flat), 0
    args = [gain] + [a for a, _ in flat] + [a for _, arrays in rhs for a in arrays]
    for (_, arrays), (_, count, _) in zip(rhs, steps):
        for a in arrays:
            specs.append(pl.BlockSpec(
                (LEN, min(GW, a.shape[1])), lambda g, *_, first=first, count=count: (0, jnp.clip(g - first, 0, count - 1))))
        first += count
    return grid_call(functools.partial(grad_kernel, steps, norms), "weight_grads", starts, total, specs,
                     [col(h) for h in heights], [jax.ShapeDtypeStruct((h, total * GW), BF16) for h in heights],
                     [pltpu.VMEM((width, 2 * LEN), BF16), pltpu.VMEM((width, GW), BF16)], args, micros)


RING = (0, 1, 3, 2)
SWAP = [(0, 1), (1, 0)]


def add(a, b):
    return (a.astype(F32) + b.astype(F32)).astype(BF16)


def after(a, *others):
    return lax.optimization_barrier((a, *others))[0]


class Rounds:
    def __init__(self, **lanes):
        self.lanes, self.results, self.wanted, self.mark = {}, {}, {}, ()
        self.add(**lanes)

    def add(self, **lanes):
        for name, lane in lanes.items():
            self.results.pop(name, None)
            self.lanes[name] = lane
            self._go(name, None)

    def _go(self, name, values):
        try:
            self.wanted[name] = list(self.lanes[name].send(values))
        except StopIteration as stop:
            self.results[name] = stop.value
            del self.lanes[name]
            self.wanted.pop(name, None)

    def step(self, count=1, others=()):
        for _ in range(count):
            flat, tree = jax.tree.flatten(self.wanted)
            if flat or others:
                flat = lax.optimization_barrier((*flat, *others))
                flat, others = flat[: tree.num_leaves], flat[tree.num_leaves :]
                self.mark = flat or others
            for name, values in jax.tree.unflatten(tree, flat).items():
                self._go(name, values)
        return others

    def finish(self, name):
        while name not in self.results:
            self.step()
        return self.results[name]


def untied(lane):
    values = None
    while True:
        try:
            arrays, _ = lane.send(values)
        except StopIteration as stop:
            return stop.value
        values = yield arrays


def in_turns(first, second, background):
    lanes, results, tie = [first, second], [None, None], ()
    wants = [next(lane) for lane in lanes]

    def send(i, values):
        try:
            wants[i] = lanes[i].send(values)
            return (wants[i][1],) if wants[i][1] is not None else ()
        except StopIteration as stop:
            results[i], lanes[i] = stop.value, None
            return ()

    while lanes != [None, None]:
        for i in range(2):
            if lanes[i] is None or (i == 0 and wants[0][1] is None):
                continue
            arrays = tuple(wants[i][0])
            if i == 0:
                tie = send(0, lax.optimization_barrier(arrays + tie)[: len(arrays)])
                continue
            ending = tuple(wants[0][0]) if lanes[0] is not None and wants[0][1] is None else ()
            got = background.step(1, arrays + ending + tie)
            tie = send(1, got[: len(arrays)])
            if ending:
                send(0, got[len(arrays) : len(arrays) + len(ending)])
    return results


def place_table(rows):
    table = [[row + [core] for core in range(2)] for row in rows]
    table = jnp.array(table, jnp.int32)
    where = (lax.axis_index("dp"), lax.axis_index("tensor"), 0)
    return lax.dynamic_slice(table, where, (1, 1, table.shape[2])).reshape(-1)


class Ring:
    def __init__(self, height):
        follow = {RING[i]: RING[(i + 1) % 4] for i in range(4)}
        self.along = [(z * 2 + x, follow[z] * 2 + x) for z in range(4) for x in range(2)]
        self.cross = [(i, i ^ 1) for i in range(8)]
        self.heights = [height] * 8
        slots, pieces = [], []
        for z in range(4):
            for x in range(2):
                across = [RING[(RING.index(z) - k) % 4] * 2 for k in range(4)]
                slots.append([(a + x) * height for a in across] + [(a + 1 - x) * height for a in across])
                pieces.append(slots[-1] + [slots[-1][7] + height // 2])
        self.slots, self.pieces = place_table(slots), place_table(pieces)

    def z(self, a):
        return lax.ppermute(a, "dp", self.along)

    def x(self, a):
        return lax.ppermute(a, "dp", self.cross)

    def gather(self, own):
        half = own.shape[0] // 2
        mine, theirs = [own], []
        for k in range(3):
            along, across = yield (self.z(mine[k]), self.x(mine[k])), mine[k]
            mine.append(along)
            theirs.append(across)
        last = yield (self.x(mine[3][:half]), self.z(theirs[2][half:])), theirs[2]
        return mine + theirs + list(last)

    def scatter(self, pieces, plain=False):
        mine, theirs = pieces[:4], list(pieces[4:])
        half = mine[0].shape[0] // 2
        if plain:
            (came,) = yield (self.x(theirs[1]),), theirs[1]
            total = add(mine[1], came)
            for k in (2, 3, 0):
                came, passed = yield (self.x(after(theirs[k], came)), self.z(total)), total
                total = (mine[k].astype(F32) + came.astype(F32) + passed.astype(F32)).astype(BF16)
            return total
        came, passed = yield (self.x(theirs[1][:half]), self.z(theirs[1][half:])), theirs[1]
        theirs[2] = jnp.concatenate([theirs[2][:half], add(theirs[2][half:], passed)], axis=0)
        total = jnp.concatenate([add(mine[1][:half], came), mine[1][half:]], axis=0)
        for k in (2, 3, 0):
            came, passed = yield (self.x(after(theirs[k], came)), self.z(total)), total
            total = (mine[k].astype(F32) + came.astype(F32) + passed.astype(F32)).astype(BF16)
        return total

    def sum_all(self, a):
        for bit in (1, 2, 4):
            (came,) = yield (lax.ppermute(a, "dp", [(i, i ^ bit) for i in range(8)]),)
            a = a + came
        return a


class Whole:
    def __init__(self, height):
        count = lax.axis_size("dp")
        self.heights = [height * count]
        self.slots = self.pieces = place_table([[0]] * count)

    def gather(self, own):
        return list((yield [lax.all_gather(own, "dp", axis=0, tiled=True)], own))

    def scatter(self, pieces, plain=False):
        return (yield [lax.psum_scatter(pieces[0], "dp", scatter_dimension=0, tiled=True)], pieces[0])[0]

    def sum_all(self, a):
        return (yield [lax.psum(a, "dp")])[0]


def inverse_rms(h):
    return lax.rsqrt(jnp.mean(h * h, axis=-1, keepdims=True) + EPS)


def lanes(row, count=Q):
    return jnp.pad(row, ((0, 0), (0, count - row.shape[1])))


def local(boundary, norm_gain, in_zx, in_bc, in_dt, conv_x, conv_bc, dt_bias, a_log, d_skip, gate_gain, out_w):
    p, t = lax.axis_index("pipe"), lax.axis_index("tensor")
    height = in_zx.shape[1]
    dp = (Ring if lax.axis_size("dp") == 8 else Whole)(height)
    tokens, part = boundary.shape[1:]
    width = 2 * part
    half = gate_gain.shape[1]
    inner = half // 2
    full_inner = 2 * half
    heads = dt_bias.shape[1] // 2
    both = ("pipe", "tensor")

    def mine(first, second):
        return jnp.where(t == 0, first, second)

    def core_swap(a):
        return lax.ppermute(a, "tensor", SWAP)

    def chip_swap(a):
        return lax.ppermute(a, "pipe", SWAP)

    def side(a, which, axis):
        size = a.shape[axis] // 2
        return lax.dynamic_slice_in_dim(a, which * size, size, axis)

    def all_four(a):
        (b,) = yield (chip_swap(a),)
        two = jnp.where(p == 0, jnp.stack([a, b]), jnp.stack([b, a]))
        (four,) = yield (core_swap(two),)
        return mine(jnp.stack([two, four], axis=1), jnp.stack([four, two], axis=1))

    turned = out_w[0].T
    sources = []
    for q in range(2):
        cols = slice(q * inner, (q + 1) * inner)
        steps = lanes(in_dt[0][:, q * heads : (q + 1) * heads])
        sources.append((jnp.concatenate([in_zx[0, :, 0, cols], in_zx[0, :, 1, cols]], axis=1),
                        jnp.concatenate([turned[:, cols], in_bc[0], steps], axis=1)))
    routes = [[[(0, 0), (1, 2)], [(0, 1), (1, 3)]], [[(2, 0), (3, 2)], [(2, 1), (3, 3)]]]

    def owned(layer, parts):
        came = [[lax.ppermute(a, both, r) for a in quarter] for quarter, r in zip(parts, routes[layer])]
        return [mine(*pair) for pair in zip(*came)]

    own0 = owned(0, sources)
    (own1,) = owned(1, [[jnp.concatenate(quarter, axis=1)] for quarter in sources])

    def packed(q):
        cols, own = slice(q * inner, (q + 1) * inner), slice(q * heads, (q + 1) * heads)
        steps = [dt_bias[:, own], -jnp.exp(a_log[:, own]) * LOG2E]
        steps = jnp.concatenate([jnp.pad(a, ((0, 0), (0, Q - heads))) for a in steps] + [jnp.zeros((3, Q), F32)], axis=0)
        shared = jnp.concatenate([conv_bc[0], steps], axis=1)
        shared = jnp.concatenate([shared, jnp.zeros((5, inner - 3 * Q), F32)], axis=1)
        top = [conv_x[0][:, cols], gate_gain[:, cols], jnp.repeat(d_skip[:, own], HS, axis=1), jnp.zeros((1, inner), F32)]
        return jnp.concatenate([*top, shared, jnp.zeros((1, inner), F32), norm_gain.reshape(2, inner)], axis=0)

    one = jnp.stack([packed(0), packed(1)])

    def ends_lane(here):
        there = chip_swap(here)
        yield ()
        yield ()
        (there,) = yield (there,)
        ours = [jnp.where(p == 0, here, there), jnp.where(p == 0, there, here)]
        others = yield [core_swap(a) for a in ours]

        def rows(a, b, which):
            left, right = (c.reshape(2, 2, HALF, part) for c in (a, b))
            left, right = (lax.dynamic_index_in_dim(c, which, 1, keepdims=False).reshape(2 * HALF, part) for c in (left, right))
            return mine(jnp.concatenate([left, right], axis=1), jnp.concatenate([right, left], axis=1))

        return [(rows(a, b, t), rows(a, b, 1 - t)) for a, b in zip(ours, others)]

    def once(*arrays):
        return (yield arrays)

    one, here, own0[0] = lax.optimization_barrier((one, boundary[0], own0[0]))
    rounds = Rounds(own1=once(own1), params=all_four(one), ends=ends_lane(here))
    front, back = in_turns(dp.gather(own0[0]), dp.gather(own0[1]), rounds)
    weights0, mark = front + back, back[3 % len(back) :][:4]
    (own1,) = rounds.finish("own1")
    params = rounds.finish("params")
    hidden0, grad1 = rounds.finish("ends")

    def layer_params(layer):
        mine = lax.dynamic_slice(params, (layer, p, t, 0, 0), (1, 1, 1, 16, inner))[0, 0, 0]
        return mine[14:].reshape(1, width), mine

    params = [layer_params(0), layer_params(1)]

    starts, slots = dp.pieces, dp.slots

    def over_cores(my, other):
        return add(my, core_swap(other))

    def in_blocks(pair):
        return [(a, s) for s in range(2) for a in pair]

    def inverse_gate(squares):
        return lax.rsqrt(squares / full_inner + EPS)

    def columns(r, dot):
        return jnp.pad(jnp.stack([r, r**3 * dot / full_inner]), ((0, 6), (0, 0)))

    def kept(r):
        return lax.dynamic_index_in_dim(r.reshape(2, 2, HALF), t, 1, keepdims=False).reshape(-1)

    def first_lane(sends, ss):
        *sends, ss = yield (*sends, ss)
        came, more = yield core_swap(sends[1]), chip_swap(ss)
        summed, ss = add(sends[0], came), ss + more
        came = chip_swap(summed)
        (more,) = yield (core_swap(ss),)
        (came,) = yield (came,)
        return summed.astype(F32) + came.astype(F32), ss + more

    def features(pair):
        yield ()
        return (yield pair)

    rounds = Rounds(weights=untied(dp.gather(after(own1, *mark))))
    sends, (ss0, *saved0) = layer_forward(in_blocks(hidden0), params[0][0], params[0][1], starts, weights0)
    rounds.add(first=first_lane(sends, ss0[0].reshape(8, -1)), grad1=features(grad1))
    weights1 = rounds.finish("weights") * 2
    mixed0, ss0 = rounds.finish("first")
    grad1 = tuple(rounds.finish("grad1"))
    r0 = inverse_gate(ss0.reshape(-1))
    hidden0_my = hidden0[0].astype(F32)
    hidden1_my = (hidden0_my + kept(r0)[:, None] * mixed0).astype(BF16)
    hidden1 = (hidden1_my, core_swap(hidden1_my))
    top_sends, (ss1, *saved1, dot1) = layer_forward(
        in_blocks(hidden1), params[1][0], params[1][1], starts, weights1, in_blocks(grad1))
    ss1, dot1 = lax.psum(jnp.stack([ss1[0], dot1[0]]), both)
    r1 = inverse_gate(ss1)

    def rms_back(dn, h, gain):
        scale = inverse_rms(h)
        pulled = dn * gain
        return scale * pulled - h * scale**3 * jnp.mean(pulled * h, axis=-1, keepdims=True), jnp.sum(dn * h * scale, axis=0)

    rows = [slice(s * LEN, (s + 1) * LEN) for s in range(2)]
    mid = [slice(s * HALF, (s + 1) * HALF) for s in range(2)]

    def backward1(s, begin):
        return layer_backward([(a, s) for a in grad1], columns(r1[rows[s]], dot1[rows[s]]), saved1, s, params[1][1], begin, weights1)

    def down(s, summed, came):
        dn = summed.astype(F32) + came.astype(F32)
        dh, gng = rms_back(dn, hidden1_my[mid[s]].astype(F32), params[1][0])
        my = (grad1[0][mid[s]].astype(F32) + dh).astype(BF16)
        return my, jnp.sum(my.astype(F32) * mixed0[mid[s]], axis=1), gng

    def both_dots(dot, other):
        return mine(jnp.concatenate([dot, other]), jnp.concatenate([other, dot]))

    def grads_of(outs, shared):
        by_kind = list(zip(*outs))
        narrow = [*by_kind[3], *shared, *by_kind[5]]
        return by_kind[2], [(0, by_kind[0]), (0, by_kind[1]), (0, narrow)]

    sends, outs = backward1(0, starts)
    back1 = [outs]
    summed_a = add(sends[0], core_swap(sends[1]))
    came_a = chip_swap(summed_a)
    sends, outs = backward1(1, after(starts, summed_a))
    back1.append(outs)
    came, came_a, *shared = lax.optimization_barrier((core_swap(sends[1]), came_a, *[core_swap(o[4]) for o in back1]))
    summed_b = add(sends[0], came)
    came_b = chip_swap(summed_b)
    my_a, dot_a, gng_a = down(0, summed_a, came_a)
    other_a, other_dot = lax.optimization_barrier((core_swap(my_a), core_swap(dot_a)))
    dot_a = both_dots(dot_a, other_dot)
    gnorms, zx = grads_of(back1, shared)
    wide1 = weight_grads([in_blocks(hidden1), in_blocks(grad1)], (True, False), params[1][0], zx + [(1, gnorms)],
                         after(slots, other_a, summed_b), dp.heights, GRADS_US)
    came_b, *wide1 = lax.optimization_barrier((came_b, *wide1))
    my_b, dot_b, gng_b = down(1, summed_b, came_b)
    gng1 = gng_a + gng_b

    def backward0(s, my, other, dot, begin):
        return layer_backward([(my, 0), (other, 0)], columns(r0[rows[s]], dot), saved0, s, params[0][1], begin, weights0)

    def top_lane():
        (came,) = yield (core_swap(after(top_sends[1], my_b)),)
        top = add(top_sends[0], came)
        passed = lax.ppermute(top, "pipe", [(0, 1)])
        yield ()
        (passed,) = yield (passed,)
        mixed = top.astype(F32) + passed.astype(F32)
        return (hidden1_my.astype(F32) + kept(r1)[:, None] * mixed).astype(BF16)

    def first_down(summed):
        passed = lax.ppermute(summed, "pipe", [(1, 0)])
        yield ()
        yield ()
        (passed,) = yield (passed,)
        dn = summed.astype(F32) + passed.astype(F32)
        dh, _ = rms_back(dn, hidden0_my, params[0][0])
        end = jnp.where(p == 0, (jnp.concatenate([my_a, my_b], axis=0).astype(F32) + dh).astype(BF16), rounds.results["top"])
        (came,) = yield (core_swap(side(end, 1 - t, 1)),)
        came, keep = came.reshape(2, HALF, part), side(end, t, 1).reshape(2, HALF, part)
        return mine(jnp.stack([keep, came], axis=1), jnp.stack([came, keep], axis=1)).reshape(1, tokens, part)

    def home(result, layer):
        pairs = [[(0, 0), (2, 1)], [(1, 0), (3, 1)]] if layer == 0 else [[(0, 2), (2, 3)], [(1, 2), (3, 3)]]
        return [lax.ppermute(result, both, pair) for pair in pairs]

    def other_half(result, layer):
        pairs = [[(2, 0), (0, 1)], [(3, 0), (1, 1)]] if layer == 0 else [[(2, 2), (0, 3)], [(3, 2), (1, 3)]]
        return [lax.ppermute(result[:, 2 * inner : 2 * inner + Q], both, pair) for pair in pairs]

    def upper_lane(pieces):
        total = yield from untied(dp.scatter(pieces, True))
        yield ()
        came = home(total, 1) + other_half(total, 1)
        yield ()
        return (yield came)

    def lower_lane(pieces, narrow):
        total = yield from dp.scatter(pieces)
        return (yield home(total, 0) + (other_half(total, 0) if narrow else []), None)

    def small(outs, gng):
        return jnp.concatenate([outs[0][6] + outs[1][6], gng.reshape(2, inner), jnp.zeros((6, inner), F32)], axis=0)

    def small_lane(parts):
        total = yield from dp.sum_all(parts)
        return (yield from all_four(total))

    rounds = Rounds(top=top_lane(), wide1=upper_lane(wide1))
    sends_a, outs_a = backward0(0, my_a, other_a, dot_a, after(starts, wide1[0]))
    rounds.add(now=once(core_swap(my_b), core_swap(dot_b), *sends_a))
    rounds.step()
    other_b, other_dot, *sends_a = rounds.results["now"]
    sends_b, outs_b = backward0(1, my_b, other_b, both_dots(dot_b, other_dot), after(starts, other_b))
    rounds.add(now=once(core_swap(sends_a[1]), *sends_b))
    rounds.step()
    came, *sends_b = rounds.results["now"]
    back0 = [outs_a, outs_b]
    summed_a = add(sends_a[0], came)
    came, *shared = lax.optimization_barrier((core_swap(sends_b[1]), *[core_swap(o[4]) for o in back0]))
    summed = jnp.concatenate([summed_a, add(sends_b[0], came)], axis=0)
    gnorms, zx = grads_of(back0, shared)
    in0 = weight_grads([in_blocks(hidden0)], (True,), params[0][0], zx, after(slots, summed), dp.heights, 14)
    gng0 = jnp.sum(summed.astype(F32) * hidden0_my * inverse_rms(hidden0_my), axis=0)
    gng1 = jnp.where(p == 0, gng1, jnp.zeros_like(gng1))
    rounds.add(now=once(summed, *in0), small=small_lane(jnp.stack([small(back0, gng0), small(back1, gng1)])))
    rounds.step()
    summed, *in0 = rounds.results["now"]
    out0 = weight_grads([[(my_a, 0), (other_a, 0), (my_b, 0), (other_b, 0)]], (False,), params[0][0], [(0, gnorms)],
                        after(slots, in0[0], *rounds.mark[:1]), dp.heights, 8)
    rounds.add(ends=first_down(summed))
    in0, out0 = in_turns(lower_lane(in0, True), lower_lane(out0, False), rounds)
    ends, sums = rounds.finish("ends"), rounds.finish("small")
    quarters = rounds.finish("wide1")
    body = 2 * inner + 2 * Q
    out0 = [jnp.where(p == 0, a, b[:, body:]) for a, b in zip(out0, quarters)]
    others = [jnp.where(p == 0, a, b).astype(F32) for a, b in zip(in0[2:], quarters[2:])]
    in0 = [jnp.where(p == 0, a, b[:, :body]) for a, b in zip(in0[:2], quarters)]

    def columns_of(first, size):
        return [a[:, first : first + size].astype(F32) for a in in0]

    g_out = jnp.concatenate(out0, axis=1).astype(F32).T
    g_zx = jnp.stack([jnp.concatenate(columns_of(k * inner, inner), axis=1) for k in range(2)], axis=1)
    g_bc = jnp.concatenate([a + b for a, b in zip(columns_of(2 * inner, Q), others)], axis=1)
    g_dt = jnp.concatenate(columns_of(2 * inner + Q, heads), axis=1)
    sums = lax.dynamic_index_in_dim(sums, p, 2, keepdims=False)
    both_p = sums.sum(axis=(0, 1))
    g_ng = both_p[16:18].reshape(1, width)
    g_cbc = both_p[8:13, inner - GW :][None]
    own = lax.dynamic_index_in_dim(sums, t, 0, keepdims=False)
    g_cx = jnp.concatenate([own[0, :5], own[1, :5]], axis=1)[None]
    g_dsk = own[:, 5].reshape(1, 2 * heads, HS).sum(axis=2)
    g_gain = own[:, 6].reshape(1, half)
    g_dtb, g_alog = (own[:, row, inner - GW : inner - GW + heads].reshape(1, 2 * heads) for row in (13, 14))
    return (ends, g_ng, g_zx[None], g_bc[None], g_dt[None], g_cx, g_cbc, g_dtb, g_alog, g_dsk, g_gain, g_out[None])


def solution(mesh):
    pipe, both, wide = ("pipe", "dp", "tensor"), ("pipe", "tensor"), P("pipe", None, "tensor")
    return jax.shard_map(
        local, mesh=mesh,
        in_specs=(P(*pipe), P("pipe", None), P("pipe", "dp", None, "tensor"), P("pipe", "dp", None), P(*pipe), wide,
                  P("pipe", None, None), P(*both), P(*both), P(*both), P(*both), P("pipe", "tensor", "dp")),
        out_specs=(P(*pipe), P("pipe", None), P("pipe", "dp", None, "tensor"), P("pipe", "dp", None), P(*pipe), wide,
                   P("pipe", None, None), P(*both), P(*both), P(*both), P(*both), P("pipe", "tensor", "dp")),
        check_vma=False,
    )
```

```python
import functools
import jax
import jax.numpy as jnp
from jax import lax
from jax.experimental import pallas as pl
from jax.experimental.pallas import tpu as pltpu
from jax.sharding import PartitionSpec as P

LEN = 512
Q = 128
GW = 256
HS = 64
EPS = 1e-05
LOG2E = 1.4426950408889634
F32 = jnp.float32
BF16 = jnp.bfloat16
NEG = -1e30
FORWARD_US = 25
BACKWARD_US = 40
GRADS_US = 20


def mm(a, b):
    return jnp.dot(a, b, preferred_element_type=F32)


def mm_nt(a, b):
    return lax.dot_general(a, b, (((1,), (1,)), ((), ())), preferred_element_type=F32)


def mm_tn(a, b):
    return lax.dot_general(a, b, (((0,), (0,)), ((), ())), preferred_element_type=F32)


def halves(a):
    high = a.astype(BF16)
    return high, (a - high.astype(F32)).astype(BF16)


def mm_split(a, b):
    high, rest = halves(a)
    return mm(high, b) + mm(rest, b)


def sigmoid(a):
    return 1.0 / (1.0 + jnp.exp2(a * (-LOG2E)))


def iota2(shape, axis):
    return lax.broadcasted_iota(jnp.int32, shape, axis)


def spread_matrix(transposed=False):
    if transposed:
        return (iota2((GW, Q), 0) // HS == iota2((GW, Q), 1)).astype(F32).astype(BF16)
    return (iota2((Q, GW), 1) // HS == iota2((Q, GW), 0)).astype(F32).astype(BF16)


def lower_ones():
    return (iota2((Q, Q), 0) >= iota2((Q, Q), 1)).astype(F32)


def shifted(ext, by):
    if by == 0:
        return ext[8:, :]
    return pltpu.roll(ext, by, 0)[8:, :]


def conv_at(pad_ref, start, taps):
    ext = pad_ref[pl.ds(pl.multiple_of(start, 8), Q + 8), :]
    out = taps[4:5, :]
    for j in range(4):
        out = out + taps[j : j + 1, :] * shifted(ext, 3 - j)
    return out


def expand(parts, spread):
    high, rest = halves(jnp.concatenate(parts, axis=0))
    out = mm(high, spread) + mm(rest, spread)
    return [out[k * Q : (k + 1) * Q] for k in range(len(parts))]


def weight_copies(starts, pieces, rest_at, bufs, sems, groups):
    wbuf, obuf, wbc, wdt = bufs
    inner = groups * GW
    zx, out, narrow = [[] for _ in range(groups)], [[] for _ in range(groups)], []
    for k in range(len(pieces) // 2):
        front, back = pieces[k], pieces[len(pieces) // 2 + k]
        here = pl.ds(pl.multiple_of(starts[k], 16), front.shape[0])
        for g in range(groups):
            for part in range(2):
                zx[g].append(pltpu.make_async_copy(
                    front.at[:, pl.ds(part * inner + g * GW, GW)], wbuf.at[g, here, pl.ds(part * GW, GW)], sems.at[k, 3 * g + part]))
            out[g].append(pltpu.make_async_copy(
                back.at[:, pl.ds(rest_at + g * GW, GW)], obuf.at[g, here, :], sems.at[k, 3 * g + 2]))
        last, at = 3 * groups, rest_at + inner
        narrow.append(pltpu.make_async_copy(back.at[:, pl.ds(at, 2 * Q)], wbc.at[here, :], sems.at[k, last]))
        narrow.append(pltpu.make_async_copy(back.at[:, pl.ds(at + 2 * Q, Q)], wdt.at[here, :], sems.at[k, last + 1]))
    return zx, out, narrow


def weight_scratch(pieces, groups, width):
    vm = pltpu.VMEM
    return [vm((groups, width, 2 * GW), BF16), vm((groups, width, GW), BF16), vm((width, 2 * Q), BF16), vm((width, Q), BF16),
            pltpu.SemaphoreType.DMA((len(pieces) // 2, 3 * groups + 2))]


def rest_column(pieces, inner):
    return 2 * inner if pieces[0].shape == pieces[len(pieces) // 2].shape else 0


def each_group(copies, act):
    for k, mine in enumerate(copies):

        @pl.when(pl.program_id(0) == k)
        def _():
            for c in mine:
                act(c)


HALF = LEN // 2
WIDE = 8 + LEN
PER = LEN // Q


def half_rows(s, which):
    return pl.ds(pl.multiple_of(s * LEN + which * HALF, HALF), HALF)


def chunk_rows(s, cc):
    return pl.ds(pl.multiple_of(s * LEN + cc * Q, Q), Q)


def steps_of(stin, dtb, rate, tri):
    pre = stin + dtb
    step = jnp.maximum(pre, 0.0) + jnp.log1p(jnp.exp(-jnp.abs(pre)))
    cumulative = jnp.dot(tri, step * rate, precision=lax.Precision.HIGHEST, preferred_element_type=F32)
    return pre, step, cumulative, cumulative - jnp.log2(step)


def fwd_kernel(n, rest_at, nseq, top, groups, unroll, starts, *refs):
    h_refs, (ng_ref, col_ref, all_ref), refs = refs[: 2 * nseq], refs[2 * nseq : 2 * nseq + 3], refs[2 * nseq + 3 :]
    cx_ref, gain_ref, dsk_ref, cbc_ref, dtb_ref, rate_ref = small_refs(col_ref, all_ref)
    if top:
        dout_refs, refs = refs[: 2 * nseq], refs[2 * nseq :]
    pieces, refs = refs[:n], refs[n:]
    p_refs, refs = refs[:2], refs[2:]
    (ss_ref, gate_ref, val_ref, y_ref, shin_ref, stin_ref, ht_ref), refs = refs[:7], refs[7:]
    if top:
        dot_ref, refs = refs[0], refs[1:]
    bufs, sems, refs = refs[:4], refs[4], refs[5:]
    wbuf, obuf, wbc_ref, wdt_ref = bufs
    (nrm_ref, vpad, csc, btsc, ssc, cum, wx, ec, cjt, gn, hst, ssum) = refs[:12]
    dsum, dgn = refs[12:] if top else (None, None)
    g = pl.program_id(0)
    core = starts[n // 2]
    sides = [(s, which) for s in range(nseq) for which in (core, 1 - core)]
    gate_copies, out_copies, narrow_copies = weight_copies(starts, pieces, rest_at, bufs, sems, groups)

    @pl.when(g == 0)
    def _():
        for c in narrow_copies:
            c.start()
        for k in range(groups):
            for c in gate_copies[k] + out_copies[k]:
                c.start()
        for (s, which), h_ref in zip(sides, h_refs):

            def norm_rows(c, carry):
                h = h_ref[pl.ds(pl.multiple_of(c * Q, Q), Q), :].astype(F32)
                scale = lax.rsqrt(jnp.mean(h * h, axis=-1, keepdims=True) + EPS)
                at = pl.multiple_of(s * LEN + which * HALF + c * Q, Q)
                nrm_ref[pl.ds(at, Q), :] = (h * scale * ng_ref[...]).astype(BF16)
                return carry

            lax.fori_loop(0, HALF // Q, norm_rows, 0, unroll=True)
        for c in narrow_copies:
            c.wait()
        ssum[...] = jnp.zeros_like(ssum)
        if top:
            dsum[...] = jnp.zeros_like(dsum)
        for s in range(nseq):
            rows = pl.ds(s * LEN, LEN)
            normed = nrm_ref[rows, :]
            shin = mm(normed, wbc_ref[...])
            shin_ref[rows, :] = shin
            vpad[pl.ds(s * WIDE, 8), :] = jnp.zeros((8, GW), F32)
            vpad[pl.ds(s * WIDE + 8, LEN), :] = shin
            stin_ref[rows, :] = mm(normed, wdt_ref[...])
        tri = lower_ones()
        taps = cbc_ref[...]

        def shared_rows(cc, carry):
            for s in range(nseq):
                c, rows = s * PER + cc, chunk_rows(s, cc)
                pre = conv_at(vpad, s * WIDE + cc * Q, taps)
                act = (pre * sigmoid(pre)).astype(BF16)
                bmat, cmat = act[:, :Q], act[:, Q:]
                bt = bmat.astype(F32).T.astype(BF16)
                btsc[c] = bt
                csc[rows, :] = cmat
                ssc[c] = mm(cmat, bt)
                _, _, cumulative, cj = steps_of(stin_ref[rows, :], dtb_ref[...], rate_ref[...], tri)
                cum[rows, :] = cumulative
                ec[rows, :] = jnp.exp2(cumulative)
                wx[rows, :] = jnp.exp2(cumulative[Q - 1 : Q, :] - cj)
                cjt[c] = cj.T[:16, :]
            return carry

        lax.fori_loop(0, PER, shared_rows, 0, unroll=unroll)

    each_group(gate_copies, lambda c: c.wait())
    each_group(out_copies, lambda c: c.wait())
    for s in range(nseq):
        rows = pl.ds(s * LEN, LEN)
        normed = nrm_ref[rows, :]
        gate_ref[rows, :] = mm(normed, wbuf[g, :, :GW]).astype(BF16)
        value = mm(normed, wbuf[g, :, GW:]).astype(BF16)
        val_ref[rows, :] = value
        vpad[pl.ds(s * WIDE, 8), :] = jnp.zeros((8, GW), F32)
        vpad[pl.ds(s * WIDE + 8, LEN), :] = value.astype(F32)
    if top:
        for (s, which), ref in zip(sides, dout_refs):
            dgn[half_rows(s, which), :] = mm(ref[...], obuf[g])
    taps = cx_ref[...]
    spread = spread_matrix()
    shift = lax.rem(Q - 4 * g, Q)
    causal = iota2((Q, Q), 0) >= iota2((Q, Q), 1)
    lane = iota2((Q, Q), 1)
    hst[...] = jnp.zeros_like(hst)

    def one(s, cc):
        c, rows = s * PER + cc, chunk_rows(s, cc)
        pre = conv_at(vpad, s * WIDE + cc * Q, taps)
        x = pre * sigmoid(pre)
        xb = x.astype(BF16)
        here = pltpu.roll(cum[rows, :], shift, 1)
        wxe, ece = expand([pltpu.roll(wx[rows, :], shift, 1), pltpu.roll(ec[rows, :], shift, 1)], spread)
        old = hst[s]
        state = old.astype(BF16)
        ht_ref[c] = state
        scores = ssc[c]
        outside = mm(csc[rows, :], state) * ece
        hst[s] = old * ece[Q - 1 : Q, :] + mm(btsc[c], (x * wxe).astype(BF16))
        parts = []
        for pair in range(GW // Q):
            mixers = []
            for half in range(2):
                i = 2 * pair + half
                cj = cjt[c, pl.ds(4 * g + i, 1), :]
                gap = jnp.where(causal, here[:, i : i + 1] - cj, NEG)
                mixers.append((scores * jnp.exp2(gap)).astype(BF16))
            x2 = xb[:, pair * Q : (pair + 1) * Q]
            zero = jnp.zeros_like(x2)
            stacked = jnp.concatenate([jnp.where(lane < HS, x2, zero), jnp.where(lane < HS, zero, x2)], axis=0)
            parts.append(mm(jnp.concatenate(mixers, axis=1), stacked))
        y = jnp.concatenate(parts, axis=1) + outside
        y_ref[rows, :] = y
        gate = gate_ref[rows, :].astype(F32)
        gated = (y + dsk_ref[...] * x) * (gate * sigmoid(gate))
        scaled = gated * gain_ref[...]
        gn[g, rows, :] = scaled.astype(BF16)
        sq = gated * gated
        ssum[rows, :] += sq[:, :Q] + sq[:, Q:]
        if top:
            prod = scaled * dgn[rows, :]
            dsum[rows, :] += prod[:, :Q] + prod[:, Q:]

    def chunk(cc, carry):
        for s in range(nseq):
            one(s, cc)
        return carry

    lax.fori_loop(0, PER, chunk, 0, unroll=unroll)

    @pl.when(g == groups - 1)
    def _():
        ones = jnp.ones((8, Q), BF16)
        high, rest = halves(ssum[...])
        ss_ref[...] = mm_nt(ones, high) + mm_nt(ones, rest)
        if top:
            high, rest = halves(dsum[...])
            dot_ref[...] = mm_nt(ones, high) + mm_nt(ones, rest)
        for i, (s, which) in enumerate(sides):
            rows = half_rows(s, which)
            total = mm_nt(gn[0, rows, :], obuf[0])
            for k in range(1, groups):
                total = total + mm_nt(gn[k, rows, :], obuf[k])
            p_refs[i % 2][pl.ds(s * HALF, HALF), :] = total.astype(BF16)


def grid_call(kernel, name, prefetch, groups, in_specs, out_specs, out_shape, scratch, args, micros):
    return pl.pallas_call(
        kernel,
        grid_spec=pltpu.PrefetchScalarGridSpec(
            num_scalar_prefetch=1, grid=(groups,), in_specs=in_specs, out_specs=out_specs, scratch_shapes=scratch),
        out_shape=out_shape,
        compiler_params=pltpu.CompilerParams(dimension_semantics=("arbitrary",), vmem_limit_bytes=60 << 20),
        cost_estimate=pl.CostEstimate(flops=int(micros * 1.15e9), bytes_accessed=20 << 20, transcendentals=0),
        name=name,
    )(prefetch, *args)


def full(shape):
    zeros = (0,) * len(shape)
    return pl.BlockSpec(shape, lambda g, *_: zeros)


def col(rows, at=0):
    return pl.BlockSpec((rows, GW), lambda g, *_: (at, g))


def row_block(rows, cols, at):
    return pl.BlockSpec((rows, cols), lambda g, *_: (at, 0))


ANYWHERE = pl.BlockSpec(memory_space=pl.ANY)


def half_specs(operands):
    return [row_block(HALF, a.shape[1], at) for a, at in operands]


def small_refs(by_group, every):
    return (by_group.at[0:5, :], by_group.at[5:6, :], by_group.at[6:7, :], every.at[8:13, 0 : 2 * Q],
            every.at[8:9, 2 * Q : 3 * Q], every.at[9:10, 2 * Q : 3 * Q])


def small_specs(small):
    return [col(8), full(small.shape)]


def layer_forward(hs, ng, small, starts, pieces, douts=(), unroll=4):
    width = hs[0][0].shape[1]
    inner = small.shape[1]
    nseq, n, top, groups = len(hs) // 2, len(pieces), len(douts) > 0, inner // GW
    rows, chunks = nseq * LEN, nseq * PER
    in_specs = half_specs(hs) + [full(ng.shape)] + small_specs(small) + half_specs(douts) + [ANYWHERE] * n
    args = [a for a, _ in hs] + [ng, small, small] + [a for a, _ in douts] + [*pieces]
    sds = jax.ShapeDtypeStruct
    out_shape = [sds((nseq * HALF, width), BF16)] * 2 + [
        sds((8, rows), F32), sds((rows, inner), BF16), sds((rows, inner), BF16), sds((rows, inner), F32),
        sds((rows, 2 * Q), F32), sds((rows, Q), F32), sds((chunks, Q, inner), BF16)]
    out_specs = [full((nseq * HALF, width))] * 2 + [
        full((8, rows)), col(rows), col(rows), col(rows), full((rows, 2 * Q)), full((rows, Q)),
        pl.BlockSpec((chunks, Q, GW), lambda g, *_: (0, 0, g))]
    if top:
        out_shape.append(sds((8, rows), F32))
        out_specs.append(full((8, rows)))
    vm = pltpu.VMEM
    scratch = weight_scratch(pieces, groups, width) + [
        vm((rows, width), BF16), vm((nseq * WIDE, GW), F32), vm((rows, Q), BF16), vm((chunks, Q, Q), BF16), vm((chunks, Q, Q), F32),
        vm((rows, Q), F32), vm((rows, Q), F32), vm((rows, Q), F32), vm((chunks, 16, Q), F32),
        vm((groups, rows, GW), BF16), vm((nseq, Q, GW), F32), vm((rows, Q), F32)]
    if top:
        scratch += [vm((rows, Q), F32), vm((rows, GW), F32)]
    out = grid_call(functools.partial(fwd_kernel, n, rest_column(pieces, inner), nseq, top, groups, unroll), "mixer_forward", starts, groups, in_specs, out_specs,
                    out_shape, scratch, args, FORWARD_US)
    return out[:2], out[2:]


def colsum(a):
    return jnp.sum(a, axis=0, keepdims=True)


def ahead(ext, by):
    if by == 0:
        return ext[:Q, :]
    return pltpu.roll(ext, Q + 8 - by, 0)[:Q, :]


def conv_back(dconv, after, taps):
    ext = jnp.concatenate([dconv, after], axis=0)
    out = taps[3:4, :] * dconv
    for j in range(3):
        out = out + taps[j : j + 1, :] * ahead(ext, 3 - j)
    return out


def bwd_kernel(n, rest_at, nseq, groups, unroll, starts, *refs):
    do_refs, refs = refs[: 2 * nseq], refs[2 * nseq :]
    (rq_rows, gate_ref, val_ref, y_ref, ht_ref, shin_ref, stin_ref), refs = refs[:7], refs[7:]
    cx_ref, gain_ref, dsk_ref, cbc_ref, dtb_ref, rate_ref = small_refs(*refs[:2])
    refs = refs[2:]
    pieces, refs = refs[:n], refs[n:]
    dn_refs, refs = refs[: 2 * nseq], refs[2 * nseq :]
    (dg_ref, dv_ref, gnorm_ref, own_ref, send_ref, ddt_ref, small_ref), refs = refs[:7], refs[7:]
    gcx_ref, tail_ref = small_ref.at[0:8, :], small_ref.at[8:16, :]
    bufs, sems, refs = refs[:4], refs[4], refs[5:]
    wbuf, obuf, wbc_ref, wdt_ref = bufs
    (vpad, spad, bsc, csc, ctsc, ssc, cjs, wx, ec, cumt, dgn, dzx, dhst, nxt, dstm, dbs, dcs, dcum, xgs, rq_ref, dsh_ref) = refs
    g = pl.program_id(0)
    core = starts[n // 2]
    sides = [(s, which) for s in range(nseq) for which in (core, 1 - core)]
    gate_copies, out_copies, narrow_copies = weight_copies(starts, pieces, rest_at, bufs, sems, groups)

    @pl.when(g == 0)
    def _():
        for k in range(groups):
            for c in out_copies[k]:
                c.start()
        for c in narrow_copies:
            c.start()
        for k in range(groups):
            for c in gate_copies[k]:
                c.start()
        for s in range(nseq):
            spad[pl.ds(s * WIDE, 8), :] = jnp.zeros((8, GW), F32)
            spad[pl.ds(s * WIDE + 8, LEN), :] = shin_ref[pl.ds(s * LEN, LEN), :]
        tri = lower_ones()
        taps = cbc_ref[...]

        def shared_rows(cc, carry):
            for s in range(nseq):
                c, rows = s * PER + cc, chunk_rows(s, cc)
                pre = conv_at(spad, s * WIDE + cc * Q, taps)
                act = (pre * sigmoid(pre)).astype(BF16)
                bmat, cmat = act[:, :Q], act[:, Q:]
                ct = cmat.astype(F32).T.astype(BF16)
                bsc[rows, :] = bmat
                csc[rows, :] = cmat
                ctsc[c] = ct
                ssc[c] = mm(bmat, ct)
                _, _, cumulative, cj = steps_of(stin_ref[rows, :], dtb_ref[...], rate_ref[...], tri)
                cjs[rows, :] = cj
                ec[rows, :] = jnp.exp2(cumulative)
                wx[rows, :] = jnp.exp2(cumulative[Q - 1 : Q, :] - cj)
                cumt[c] = cumulative.T[:16, :]
                rq_ref[rows, :] = rq_rows[:, pl.ds(pl.multiple_of(s * LEN + cc * Q, Q), Q)].T
            return carry

        lax.fori_loop(0, PER, shared_rows, 0, unroll=unroll)
        for ref in (dstm, dbs, dcs, dcum, xgs):
            ref[...] = jnp.zeros_like(ref)

    each_group(out_copies, lambda c: c.wait())
    for (s, which), ref in zip(sides, do_refs):
        dgn[half_rows(s, which), :] = mm(ref[...], obuf[g])
    for s in range(nseq):
        vpad[pl.ds(s * WIDE, 8), :] = jnp.zeros((8, GW), F32)
        vpad[pl.ds(s * WIDE + 8, LEN), :] = val_ref[pl.ds(s * LEN, LEN), :].astype(F32)
    small_ref[...] = jnp.zeros_like(small_ref)
    dhst[...] = jnp.zeros_like(dhst)
    nxt[...] = jnp.zeros_like(nxt)
    taps = cx_ref[...]
    spread = spread_matrix()
    gather = spread_matrix(True)
    to_front = lax.rem(Q - 4 * g, Q)
    causal = iota2((Q, Q), 0) <= iota2((Q, Q), 1)
    lane = iota2((Q, Q), 1)
    last_row = iota2((Q, GW), 0) == Q - 1

    def one(s, cc):
        c, rows = s * PER + cc, chunk_rows(s, cc)
        start = pl.multiple_of(s * WIDE + cc * Q, 8)
        ext = vpad[pl.ds(start, Q + 8), :]
        taken = [shifted(ext, 3 - j) for j in range(4)]
        pre = taps[4:5, :]
        for j in range(4):
            pre = pre + taps[j : j + 1, :] * taken[j]
        sx = sigmoid(pre)
        x = pre * sx
        xb = x.astype(BF16)
        gate = gate_ref[rows, :].astype(F32)
        sg = sigmoid(gate)
        silu_gate = gate * sg
        y = y_ref[rows, :]
        dsk = dsk_ref[...]
        gain = gain_ref[...]
        mixed = y + dsk * x
        gated = mixed * silu_gate
        r = rq_ref[rows, 0:1]
        q = rq_ref[rows, 1:2]
        d_norm = dgn[rows, :]
        scaled = gated * r
        gnorm_ref[rows, :] = (scaled * gain).astype(BF16)
        d_gated = (r * gain) * d_norm - gated * q
        dmix = d_gated * silu_gate
        dgate = (d_gated * mixed * (sg * (1.0 + gate * (1.0 - sg)))).astype(BF16)
        dg_ref[rows, :] = dgate
        dzx[g, rows, :GW] = dgate
        dyb = dmix.astype(BF16)
        dyf = dyb.astype(F32)
        xf = xb.astype(F32)
        wxe, ece = expand([pltpu.roll(wx[rows, :], to_front, 1), pltpu.roll(ec[rows, :], to_front, 1)], spread)
        here = pltpu.roll(cjs[rows, :], to_front, 1)
        ecl = ece[Q - 1 : Q, :]
        state = ht_ref[c]
        dh = dhst[s]
        dhb = dh.astype(BF16)
        gx_state = mm(bsc[rows, :], dhb) * wxe
        dye = (dmix * ece).astype(BF16)
        dcs[rows, :] += mm_nt(dye, state)
        dbs[rows, :] += mm_nt((x * wxe).astype(BF16), dhb)
        ends = colsum(xf * gx_state) + ecl * colsum(state.astype(F32) * dh)
        dhst[s] = dh * ecl + mm(ctsc[c], dye)
        scores = ssc[c]
        dst = jnp.zeros((Q, Q), F32)
        parts = []
        for pair in range(GW // Q):
            x2 = xb[:, pair * Q : (pair + 1) * Q]
            dy2 = dyb[:, pair * Q : (pair + 1) * Q]
            zero = jnp.zeros_like(x2)
            xs = [jnp.where(lane < HS, x2, zero), jnp.where(lane < HS, zero, x2)]
            dys = [jnp.where(lane < HS, dy2, zero), jnp.where(lane < HS, zero, dy2)]
            mixers = []
            for half in range(2):
                i = 2 * pair + half
                ci = cumt[c, pl.ds(4 * g + i, 1), :]
                decay = jnp.exp2(jnp.where(causal, ci - here[:, i : i + 1], NEG))
                mixers.append((scores * decay).astype(BF16))
                dst = dst + mm_nt(xs[half], dy2) * decay
            parts.append(mm(jnp.concatenate(mixers, axis=1), jnp.concatenate(dys, axis=0)))
        dstm[c] += dst
        gx = jnp.concatenate(parts, axis=1) + gx_state
        to_heads = lax.rem(4 * g, Q)
        xg, yg = expand([xf * gx, jnp.where(last_row, dyf * y + ends, dyf * y)], gather)
        xgs[rows, :] += pltpu.roll(xg, to_heads, 1)
        dcum[rows, :] += pltpu.roll(yg - xg, to_heads, 1)
        dx = gx + dsk * dmix
        dconv = dx * (sx * (1.0 + pre * (1.0 - sx)))
        dvalue = conv_back(dconv, nxt[s], taps).astype(BF16)
        nxt[s] = dconv[:8, :]
        dv_ref[rows, :] = dvalue
        dzx[g, rows, GW:] = dvalue
        sums = [colsum(dconv * taken[j]) for j in range(4)]
        sums += [colsum(dconv), colsum(dmix * x), colsum(d_norm * scaled), jnp.zeros((1, GW), F32)]
        gcx_ref[...] += jnp.concatenate(sums, axis=0)

    def chunk(back, carry):
        for s in range(nseq):
            one(s, PER - 1 - back)
        return carry

    lax.fori_loop(0, PER, chunk, 0, unroll=unroll)

    @pl.when(g == groups - 1)
    def _():
        upper = (iota2((Q, Q), 0) <= iota2((Q, Q), 1)).astype(F32)
        taps = cbc_ref[...]
        nxt[...] = jnp.zeros_like(nxt)

        def shared_back(s, cc):
            c, rows = s * PER + cc, chunk_rows(s, cc)
            start = pl.multiple_of(s * WIDE + cc * Q, 8)
            ext = spad[pl.ds(start, Q + 8), :]
            taken = [shifted(ext, 3 - j) for j in range(4)]
            pre = taps[4:5, :]
            for j in range(4):
                pre = pre + taps[j : j + 1, :] * taken[j]
            sx = sigmoid(pre)
            dst = dstm[c]
            d_b = dbs[rows, :] + mm(dst.astype(BF16), csc[rows, :])
            d_c = dcs[rows, :] + mm(dst.T.astype(BF16), bsc[rows, :])
            dconv = jnp.concatenate([d_b, d_c], axis=1) * (sx * (1.0 + pre * (1.0 - sx)))
            back = conv_back(dconv, nxt[s], taps).astype(BF16)
            dsh_ref[rows, :] = back
            first = core == 0
            own_ref[rows, :] = jnp.where(first, back[:, :Q], back[:, Q:])
            send_ref[rows, :] = jnp.where(first, back[:, Q:], back[:, :Q])
            nxt[s] = dconv[:8, :]
            sums = [colsum(dconv * taken[j]) for j in range(4)] + [colsum(dconv)]
            da = jnp.dot(upper, dcum[rows, :], precision=lax.Precision.HIGHEST, preferred_element_type=F32)
            pre = stin_ref[rows, :] + dtb_ref[...]
            step = jnp.maximum(pre, 0.0) + jnp.log1p(jnp.exp(-jnp.abs(pre)))
            sig = sigmoid(pre)
            rate = rate_ref[...] * (1.0 / LOG2E)
            dpre = da * rate * sig + xgs[rows, :] * (sig / jnp.maximum(step, 1e-37))
            ddt_ref[rows, :] = dpre.astype(BF16)
            wide = jnp.zeros((1, GW - Q), F32)
            sums += [jnp.concatenate([a, wide], axis=1) for a in (colsum(dpre), colsum(step * da) * rate)]
            tail_ref[...] += jnp.concatenate(sums + [jnp.zeros((1, GW), F32)], axis=0)

        def back_rows(back, carry):
            for s in range(nseq):
                shared_back(s, PER - 1 - back)
            return carry

        lax.fori_loop(0, PER, back_rows, 0, unroll=unroll)
        for c in narrow_copies:
            c.wait()
        for k in range(groups):
            for c in gate_copies[k]:
                c.wait()
        for (s, which), ref in zip(sides, dn_refs):
            rows = half_rows(s, which)
            total = mm_nt(dsh_ref[rows, :], wbc_ref[...]) + mm_nt(ddt_ref[rows, :], wdt_ref[...])
            for k in range(groups):
                total = total + mm_nt(dzx[k, rows, :], wbuf[k])
            ref[...] = total.astype(BF16)


def layer_backward(douts, rq, saved, at, small, starts, pieces, unroll=4):
    gate, value, y, shin, stin, ht = saved
    width = douts[0][0].shape[1]
    inner = small.shape[1]
    nseq, n, groups = len(douts) // 2, len(pieces), inner // GW
    rows, chunks, at = nseq * LEN, nseq * PER, at // nseq
    in_specs = half_specs(douts) + [
        full(rq.shape), col(rows, at), col(rows, at), col(rows, at),
        pl.BlockSpec((chunks, Q, GW), lambda g, *_: (at, 0, g)), row_block(rows, 2 * Q, at), row_block(rows, Q, at)]
    in_specs += small_specs(small) + [ANYWHERE] * n
    args = [a for a, _ in douts] + [rq, gate, value, y, ht, shin, stin, small, small, *pieces]
    sds = jax.ShapeDtypeStruct
    out_shape = [sds((HALF, width), BF16)] * (2 * nseq) + [sds((rows, inner), BF16)] * 3 + [
        sds((rows, Q), BF16), sds((rows, Q), BF16), sds((rows, Q), BF16), sds((16, inner), F32)]
    out_specs = [full((HALF, width))] * (2 * nseq) + [col(rows)] * 3 + [full((rows, Q))] * 3 + [col(16)]
    vm = pltpu.VMEM
    scratch = weight_scratch(pieces, groups, width) + [
        vm((nseq * WIDE, GW), F32), vm((nseq * WIDE, GW), F32),
        vm((rows, Q), BF16), vm((rows, Q), BF16), vm((chunks, Q, Q), BF16), vm((chunks, Q, Q), F32),
        vm((rows, Q), F32), vm((rows, Q), F32), vm((rows, Q), F32), vm((chunks, 16, Q), F32),
        vm((rows, GW), F32), vm((groups, rows, 2 * GW), BF16), vm((nseq, Q, GW), F32), vm((nseq, 8, GW), F32),
        vm((chunks, Q, Q), F32), vm((rows, Q), F32), vm((rows, Q), F32), vm((rows, Q), F32), vm((rows, Q), F32),
        vm((rows, 8), F32), vm((rows, 2 * Q), BF16)]
    out = grid_call(functools.partial(bwd_kernel, n, rest_column(pieces, inner), nseq, groups, unroll), "mixer_backward", starts, groups, in_specs, out_specs,
                    out_shape, scratch, args, BACKWARD_US * nseq / 2)
    return out[: 2 * nseq], out[2 * nseq :]


def grad_kernel(steps, norms, starts, *refs):
    gain_ref, refs = refs[0], refs[1:]
    lhs, refs = refs[: 4 * len(norms)], refs[4 * len(norms) :]
    outs, (turned, whole) = refs[:-2], refs[-2:]
    g = pl.program_id(0)

    def turn(halves_of, norm):
        core = starts[starts.shape[0] - 1]
        for k, ref in enumerate(halves_of):
            base = k // 2 * LEN + (core if k % 2 == 0 else 1 - core) * HALF
            here = pl.ds(pl.multiple_of(base, HALF), HALF)
            if norm:
                h = ref[...].astype(F32)
                scale = lax.rsqrt(jnp.mean(h * h, axis=-1, keepdims=True) + EPS)
            for j in range(turned.shape[0] // GW):
                cols = pl.ds(j * GW, GW)
                part = ref[:, cols]
                if norm:
                    part = (part.astype(F32) * scale * gain_ref[:, cols]).astype(BF16)
                turned[cols, here] = part.T

    first, ready = 0, None
    for source, count, width in steps:
        rhs, outs = outs[:width], outs[width:]
        if source != ready:
            pl.when(g == first)(functools.partial(turn, lhs[4 * source : 4 * source + 4], norms[source]))
            ready = source

        @pl.when((g >= first) & (g < first + count))
        def _():
            both = jnp.concatenate([ref[...] for ref in rhs[:2]], axis=0)
            if width == 6:
                came, steps_in = (jnp.concatenate([ref[...] for ref in rhs[k : k + 2]], axis=0) for k in (2, 4))
                both = jnp.concatenate([(both.astype(F32) + came.astype(F32)).astype(BF16), steps_in], axis=1)
            whole[...] = mm(turned[...], both).astype(BF16)

        first += count
    for k, out in enumerate(outs):
        out[...] = whole[pl.ds(pl.multiple_of(starts[k], 16), out.shape[0]), :]


def weight_grads(lhs, norms, gain, rhs, starts, heights, micros):
    width = gain.shape[1]
    steps = [(source, max(arrays[0].shape[1] // GW, 1), len(arrays)) for source, arrays in rhs]
    total = sum(count for _, count, _ in steps)
    flat = [operand for source in lhs for operand in source]
    specs, first = [full(gain.shape)] + half_specs(flat), 0
    args = [gain] + [a for a, _ in flat] + [a for _, arrays in rhs for a in arrays]
    for (_, arrays), (_, count, _) in zip(rhs, steps):
        for a in arrays:
            specs.append(pl.BlockSpec(
                (LEN, min(GW, a.shape[1])), lambda g, *_, first=first, count=count: (0, jnp.clip(g - first, 0, count - 1))))
        first += count
    return grid_call(functools.partial(grad_kernel, steps, norms), "weight_grads", starts, total, specs,
                     [col(h) for h in heights], [jax.ShapeDtypeStruct((h, total * GW), BF16) for h in heights],
                     [pltpu.VMEM((width, 2 * LEN), BF16), pltpu.VMEM((width, GW), BF16)], args, micros)


RING = (0, 1, 3, 2)
SWAP = [(0, 1), (1, 0)]


def add(a, b):
    return (a.astype(F32) + b.astype(F32)).astype(BF16)


def after(a, *others):
    return lax.optimization_barrier((a, *others))[0]


class Rounds:
    def __init__(self, **lanes):
        self.lanes, self.results, self.wanted, self.mark = {}, {}, {}, ()
        self.add(**lanes)

    def add(self, **lanes):
        for name, lane in lanes.items():
            self.results.pop(name, None)
            self.lanes[name] = lane
            self._go(name, None)

    def _go(self, name, values):
        try:
            self.wanted[name] = list(self.lanes[name].send(values))
        except StopIteration as stop:
            self.results[name] = stop.value
            del self.lanes[name]
            self.wanted.pop(name, None)

    def step(self, count=1, others=()):
        for _ in range(count):
            flat, tree = jax.tree.flatten(self.wanted)
            if flat or others:
                flat = lax.optimization_barrier((*flat, *others))
                flat, others = flat[: tree.num_leaves], flat[tree.num_leaves :]
                self.mark = flat or others
            for name, values in jax.tree.unflatten(tree, flat).items():
                self._go(name, values)
        return others

    def finish(self, name):
        while name not in self.results:
            self.step()
        return self.results[name]


def untied(lane):
    values = None
    while True:
        try:
            arrays, _ = lane.send(values)
        except StopIteration as stop:
            return stop.value
        values = yield arrays


def in_turns(first, second, background):
    lanes, results, tie = [first, second], [None, None], ()
    wants = [next(lane) for lane in lanes]

    def send(i, values):
        try:
            wants[i] = lanes[i].send(values)
            return (wants[i][1],) if wants[i][1] is not None else ()
        except StopIteration as stop:
            results[i], lanes[i] = stop.value, None
            return ()

    while lanes != [None, None]:
        for i in range(2):
            if lanes[i] is None or (i == 0 and wants[0][1] is None):
                continue
            arrays = tuple(wants[i][0])
            if i == 0:
                tie = send(0, lax.optimization_barrier(arrays + tie)[: len(arrays)])
                continue
            ending = tuple(wants[0][0]) if lanes[0] is not None and wants[0][1] is None else ()
            got = background.step(1, arrays + ending + tie)
            tie = send(1, got[: len(arrays)])
            if ending:
                send(0, got[len(arrays) : len(arrays) + len(ending)])
    return results


def place_table(rows):
    table = [[row + [core] for core in range(2)] for row in rows]
    table = jnp.array(table, jnp.int32)
    where = (lax.axis_index("dp"), lax.axis_index("tensor"), 0)
    return lax.dynamic_slice(table, where, (1, 1, table.shape[2])).reshape(-1)


class Ring:
    def __init__(self, height):
        follow = {RING[i]: RING[(i + 1) % 4] for i in range(4)}
        self.along = [(z * 2 + x, follow[z] * 2 + x) for z in range(4) for x in range(2)]
        self.cross = [(i, i ^ 1) for i in range(8)]
        self.heights = [height] * 8
        slots, pieces = [], []
        for z in range(4):
            for x in range(2):
                across = [RING[(RING.index(z) - k) % 4] * 2 for k in range(4)]
                slots.append([(a + x) * height for a in across] + [(a + 1 - x) * height for a in across])
                pieces.append(slots[-1] + [slots[-1][7] + height // 2])
        self.slots, self.pieces = place_table(slots), place_table(pieces)

    def z(self, a):
        return lax.ppermute(a, "dp", self.along)

    def x(self, a):
        return lax.ppermute(a, "dp", self.cross)

    def gather(self, own):
        half = own.shape[0] // 2
        mine, theirs = [own], []
        for k in range(3):
            along, across = yield (self.z(mine[k]), self.x(mine[k])), mine[k]
            mine.append(along)
            theirs.append(across)
        last = yield (self.x(mine[3][:half]), self.z(theirs[2][half:])), theirs[2]
        return mine + theirs + list(last)

    def scatter(self, pieces, plain=False):
        mine, theirs = pieces[:4], list(pieces[4:])
        half = mine[0].shape[0] // 2
        if plain:
            (came,) = yield (self.x(theirs[1]),), theirs[1]
            total = add(mine[1], came)
            for k in (2, 3, 0):
                came, passed = yield (self.x(after(theirs[k], came)), self.z(total)), total
                total = (mine[k].astype(F32) + came.astype(F32) + passed.astype(F32)).astype(BF16)
            return total
        came, passed = yield (self.x(theirs[1][:half]), self.z(theirs[1][half:])), theirs[1]
        theirs[2] = jnp.concatenate([theirs[2][:half], add(theirs[2][half:], passed)], axis=0)
        total = jnp.concatenate([add(mine[1][:half], came), mine[1][half:]], axis=0)
        for k in (2, 3, 0):
            came, passed = yield (self.x(after(theirs[k], came)), self.z(total)), total
            total = (mine[k].astype(F32) + came.astype(F32) + passed.astype(F32)).astype(BF16)
        return total

    def sum_all(self, a):
        for bit in (1, 2, 4):
            (came,) = yield (lax.ppermute(a, "dp", [(i, i ^ bit) for i in range(8)]),)
            a = a + came
        return a


class Whole:
    def __init__(self, height):
        count = lax.axis_size("dp")
        self.heights = [height * count]
        self.slots = self.pieces = place_table([[0]] * count)

    def gather(self, own):
        return list((yield [lax.all_gather(own, "dp", axis=0, tiled=True)], own))

    def scatter(self, pieces, plain=False):
        return (yield [lax.psum_scatter(pieces[0], "dp", scatter_dimension=0, tiled=True)], pieces[0])[0]

    def sum_all(self, a):
        return (yield [lax.psum(a, "dp")])[0]


def inverse_rms(h):
    return lax.rsqrt(jnp.mean(h * h, axis=-1, keepdims=True) + EPS)


def lanes(row, count=Q):
    return jnp.pad(row, ((0, 0), (0, count - row.shape[1])))


def local(boundary, norm_gain, in_zx, in_bc, in_dt, conv_x, conv_bc, dt_bias, a_log, d_skip, gate_gain, out_w):
    p, t = lax.axis_index("pipe"), lax.axis_index("tensor")
    height = in_zx.shape[1]
    dp = (Ring if lax.axis_size("dp") == 8 else Whole)(height)
    tokens, part = boundary.shape[1:]
    width = 2 * part
    half = gate_gain.shape[1]
    inner = half // 2
    full_inner = 2 * half
    heads = dt_bias.shape[1] // 2
    both = ("pipe", "tensor")

    def mine(first, second):
        return jnp.where(t == 0, first, second)

    def core_swap(a):
        return lax.ppermute(a, "tensor", SWAP)

    def chip_swap(a):
        return lax.ppermute(a, "pipe", SWAP)

    def side(a, which, axis):
        size = a.shape[axis] // 2
        return lax.dynamic_slice_in_dim(a, which * size, size, axis)

    def all_four(a):
        (b,) = yield (chip_swap(a),)
        two = jnp.where(p == 0, jnp.stack([a, b]), jnp.stack([b, a]))
        (four,) = yield (core_swap(two),)
        return mine(jnp.stack([two, four], axis=1), jnp.stack([four, two], axis=1))

    turned = out_w[0].T
    sources = []
    for q in range(2):
        cols = slice(q * inner, (q + 1) * inner)
        steps = lanes(in_dt[0][:, q * heads : (q + 1) * heads])
        sources.append((jnp.concatenate([in_zx[0, :, 0, cols], in_zx[0, :, 1, cols]], axis=1),
                        jnp.concatenate([turned[:, cols], in_bc[0], steps], axis=1)))
    routes = [[[(0, 0), (1, 2)], [(0, 1), (1, 3)]], [[(2, 0), (3, 2)], [(2, 1), (3, 3)]]]

    def owned(layer, parts):
        came = [[lax.ppermute(a, both, r) for a in quarter] for quarter, r in zip(parts, routes[layer])]
        return [mine(*pair) for pair in zip(*came)]

    own0 = owned(0, sources)
    (own1,) = owned(1, [[jnp.concatenate(quarter, axis=1)] for quarter in sources])

    def packed(q):
        cols, own = slice(q * inner, (q + 1) * inner), slice(q * heads, (q + 1) * heads)
        steps = [dt_bias[:, own], -jnp.exp(a_log[:, own]) * LOG2E]
        steps = jnp.concatenate([jnp.pad(a, ((0, 0), (0, Q - heads))) for a in steps] + [jnp.zeros((3, Q), F32)], axis=0)
        shared = jnp.concatenate([conv_bc[0], steps], axis=1)
        shared = jnp.concatenate([shared, jnp.zeros((5, inner - 3 * Q), F32)], axis=1)
        top = [conv_x[0][:, cols], gate_gain[:, cols], jnp.repeat(d_skip[:, own], HS, axis=1), jnp.zeros((1, inner), F32)]
        return jnp.concatenate([*top, shared, jnp.zeros((1, inner), F32), norm_gain.reshape(2, inner)], axis=0)

    one = jnp.stack([packed(0), packed(1)])

    def ends_lane(here):
        there = chip_swap(here)
        yield ()
        yield ()
        (there,) = yield (there,)
        ours = [jnp.where(p == 0, here, there), jnp.where(p == 0, there, here)]
        others = yield [core_swap(a) for a in ours]

        def rows(a, b, which):
            left, right = (c.reshape(2, 2, HALF, part) for c in (a, b))
            left, right = (lax.dynamic_index_in_dim(c, which, 1, keepdims=False).reshape(2 * HALF, part) for c in (left, right))
            return mine(jnp.concatenate([left, right], axis=1), jnp.concatenate([right, left], axis=1))

        return [(rows(a, b, t), rows(a, b, 1 - t)) for a, b in zip(ours, others)]

    def once(*arrays):
        return (yield arrays)

    one, here, own0[0] = lax.optimization_barrier((one, boundary[0], own0[0]))
    rounds = Rounds(own1=once(own1), params=all_four(one), ends=ends_lane(here))
    front, back = in_turns(dp.gather(own0[0]), dp.gather(own0[1]), rounds)
    weights0, mark = front + back, back[3 % len(back) :][:4]
    (own1,) = rounds.finish("own1")
    params = rounds.finish("params")
    hidden0, grad1 = rounds.finish("ends")

    def layer_params(layer):
        mine = lax.dynamic_slice(params, (layer, p, t, 0, 0), (1, 1, 1, 16, inner))[0, 0, 0]
        return mine[14:].reshape(1, width), mine

    params = [layer_params(0), layer_params(1)]

    starts, slots = dp.pieces, dp.slots

    def over_cores(my, other):
        return add(my, core_swap(other))

    def in_blocks(pair):
        return [(a, s) for s in range(2) for a in pair]

    def inverse_gate(squares):
        return lax.rsqrt(squares / full_inner + EPS)

    def columns(r, dot):
        return jnp.pad(jnp.stack([r, r**3 * dot / full_inner]), ((0, 6), (0, 0)))

    def kept(r):
        return lax.dynamic_index_in_dim(r.reshape(2, 2, HALF), t, 1, keepdims=False).reshape(-1)

    def features(pair):
        yield ()
        return (yield pair)

    rows = [slice(s * LEN, (s + 1) * LEN) for s in range(2)]
    mid = [slice(s * HALF, (s + 1) * HALF) for s in range(2)]

    def forward0(s, begin):
        (keep, send), (ss, *saved) = layer_forward([(a, s) for a in hidden0], params[0][0], params[0][1], begin, weights0)
        return keep, send, ss[0], saved

    rounds = Rounds(weights=untied(dp.gather(after(own1, *mark))))
    keep, send, ss_a, saved_a = forward0(0, starts)
    rounds.add(now=once(keep, send, ss_a))
    rounds.step()
    keep, send, ss_a = rounds.results["now"]
    summed = [add(keep, core_swap(send))]
    passed = [chip_swap(summed[0])]
    keep, send, ss_b, saved_b = forward0(1, after(starts, summed[0]))
    rounds.add(now=once(keep, send, ss_b, passed[0]), grad1=features(grad1))
    rounds.step()
    keep, send, ss_b, passed[0] = rounds.results["now"]
    saved0 = [saved_a, saved_b]
    summed.append(add(keep, core_swap(send)))
    passed.append(chip_swap(summed[1]))
    ss0 = jnp.concatenate([ss_a, ss_b]).reshape(8, -1)
    ss0 = ss0 + chip_swap(ss0)
    ss0 = ss0 + core_swap(ss0)
    rounds.step()
    rounds.add(now=once(passed[1], ss0))
    weights1 = rounds.finish("weights") * 2
    passed[1], ss0 = rounds.finish("now")
    grad1 = tuple(rounds.finish("grad1"))
    r0 = inverse_gate(ss0.reshape(-1))
    mixed0 = [a.astype(F32) + b.astype(F32) for a, b in zip(summed, passed)]
    hidden0_my = hidden0[0].astype(F32)
    hidden1_my = [(hidden0_my[mid[s]] + kept(r0)[mid[s]][:, None] * mixed0[s]).astype(BF16) for s in range(2)]
    hidden1 = [(a, 0) for my in hidden1_my for a in (my, core_swap(my))]
    top_sends, (ss1, *saved1, dot1) = layer_forward(hidden1, params[1][0], params[1][1], starts, weights1, in_blocks(grad1))
    ss1, dot1 = lax.psum(jnp.stack([ss1[0], dot1[0]]), both)
    r1 = inverse_gate(ss1)

    def rms_back(dn, h, gain):
        scale = inverse_rms(h)
        pulled = dn * gain
        return scale * pulled - h * scale**3 * jnp.mean(pulled * h, axis=-1, keepdims=True), jnp.sum(dn * h * scale, axis=0)

    def backward1(s, begin):
        return layer_backward([(a, s) for a in grad1], columns(r1[rows[s]], dot1[rows[s]]), saved1, s, params[1][1], begin, weights1)

    def down(s, summed, came):
        dn = summed.astype(F32) + came.astype(F32)
        dh, gng = rms_back(dn, hidden1_my[s].astype(F32), params[1][0])
        my = (grad1[0][mid[s]].astype(F32) + dh).astype(BF16)
        return my, jnp.sum(my.astype(F32) * mixed0[s], axis=1), gng

    def both_dots(dot, other):
        return mine(jnp.concatenate([dot, other]), jnp.concatenate([other, dot]))

    def grads_of(outs, shared):
        by_kind = list(zip(*outs))
        narrow = [*by_kind[3], *shared, *by_kind[5]]
        return by_kind[2], [(0, by_kind[0]), (0, by_kind[1]), (0, narrow)]

    sends, outs = backward1(0, starts)
    back1 = [outs]
    summed_a = add(sends[0], core_swap(sends[1]))
    came_a = chip_swap(summed_a)
    shared_a = core_swap(after(outs[4], summed_a))
    sends, outs = backward1(1, after(starts, shared_a))
    back1.append(outs)
    came, came_a, shared_b = lax.optimization_barrier((core_swap(sends[1]), came_a, core_swap(outs[4])))
    shared = [shared_a, shared_b]
    summed_b = add(sends[0], came)
    came_b = chip_swap(summed_b)
    my_a, dot_a, gng_a = down(0, summed_a, came_a)
    other_a, other_dot = lax.optimization_barrier((core_swap(my_a), core_swap(dot_a)))
    dot_a = both_dots(dot_a, other_dot)
    gnorms, zx = grads_of(back1, shared)
    wide1 = weight_grads([hidden1, in_blocks(grad1)], (True, False), params[1][0], zx + [(1, gnorms)],
                         after(slots, other_a, summed_b), dp.heights, GRADS_US)
    came_b, *wide1 = lax.optimization_barrier((came_b, *wide1))
    my_b, dot_b, gng_b = down(1, summed_b, came_b)
    gng1 = gng_a + gng_b

    def backward0(s, my, other, dot, begin):
        return layer_backward([(my, 0), (other, 0)], columns(r0[rows[s]], dot), saved0[s], 0, params[0][1], begin, weights0)

    def top_lane():
        (came,) = yield (core_swap(after(top_sends[1], my_b)),)
        top = add(top_sends[0], came)
        passed = lax.ppermute(top, "pipe", [(0, 1)])
        yield ()
        (passed,) = yield (passed,)
        mixed = top.astype(F32) + passed.astype(F32)
        return (jnp.concatenate(hidden1_my, axis=0).astype(F32) + kept(r1)[:, None] * mixed).astype(BF16)

    def first_down(summed):
        passed = lax.ppermute(summed, "pipe", [(1, 0)])
        yield ()
        yield ()
        (passed,) = yield (passed,)
        dn = summed.astype(F32) + passed.astype(F32)
        dh, _ = rms_back(dn, hidden0_my, params[0][0])
        end = jnp.where(p == 0, (jnp.concatenate([my_a, my_b], axis=0).astype(F32) + dh).astype(BF16), rounds.results["top"])
        (came,) = yield (core_swap(side(end, 1 - t, 1)),)
        came, keep = came.reshape(2, HALF, part), side(end, t, 1).reshape(2, HALF, part)
        return mine(jnp.stack([keep, came], axis=1), jnp.stack([came, keep], axis=1)).reshape(1, tokens, part)

    def home(result, layer):
        pairs = [[(0, 0), (2, 1)], [(1, 0), (3, 1)]] if layer == 0 else [[(0, 2), (2, 3)], [(1, 2), (3, 3)]]
        return [lax.ppermute(result, both, pair) for pair in pairs]

    def other_half(result, layer):
        pairs = [[(2, 0), (0, 1)], [(3, 0), (1, 1)]] if layer == 0 else [[(2, 2), (0, 3)], [(3, 2), (1, 3)]]
        return [lax.ppermute(result[:, 2 * inner : 2 * inner + Q], both, pair) for pair in pairs]

    def upper_lane(pieces):
        total = yield from untied(dp.scatter(pieces, True))
        yield ()
        came = home(total, 1) + other_half(total, 1)
        yield ()
        return (yield came)

    def lower_lane(pieces, narrow):
        total = yield from dp.scatter(pieces)
        return (yield home(total, 0) + (other_half(total, 0) if narrow else []), None)

    def small(outs, gng):
        return jnp.concatenate([outs[0][6] + outs[1][6], gng.reshape(2, inner), jnp.zeros((6, inner), F32)], axis=0)

    def small_lane(parts):
        total = yield from dp.sum_all(parts)
        return (yield from all_four(total))

    rounds = Rounds(top=top_lane(), wide1=upper_lane(wide1))
    sends_a, outs_a = backward0(0, my_a, other_a, dot_a, after(starts, wide1[0]))
    rounds.add(now=once(core_swap(my_b), core_swap(dot_b), *sends_a))
    rounds.step()
    other_b, other_dot, *sends_a = rounds.results["now"]
    sends_b, outs_b = backward0(1, my_b, other_b, both_dots(dot_b, other_dot), after(starts, other_b))
    rounds.add(now=once(core_swap(sends_a[1]), *sends_b))
    rounds.step()
    came, *sends_b = rounds.results["now"]
    back0 = [outs_a, outs_b]
    summed_a = add(sends_a[0], came)
    came, *shared = lax.optimization_barrier((core_swap(sends_b[1]), *[core_swap(o[4]) for o in back0]))
    summed = jnp.concatenate([summed_a, add(sends_b[0], came)], axis=0)
    gnorms, zx = grads_of(back0, shared)
    in0 = weight_grads([in_blocks(hidden0)], (True,), params[0][0], zx, after(slots, summed), dp.heights, 14)
    gng0 = jnp.sum(summed.astype(F32) * hidden0_my * inverse_rms(hidden0_my), axis=0)
    gng1 = jnp.where(p == 0, gng1, jnp.zeros_like(gng1))
    gng1 = jnp.where(p == 0, gng1, jnp.zeros_like(gng1))
    out0 = weight_grads([[(my_a, 0), (other_a, 0), (my_b, 0), (other_b, 0)]], (False,), params[0][0], [(0, gnorms)],
                        after(slots, in0[0]), dp.heights, 8)
    rounds.add(now=once(summed, *in0, *out0))
    rounds.step()
    summed, *wide0 = rounds.results["now"]
    in0, out0 = wide0[: len(in0)], wide0[len(in0) :]
    rounds.add(ends=first_down(summed), small=small_lane(jnp.stack([small(back0, gng0), small(back1, gng1)])))
    out0, in0 = in_turns(lower_lane(out0, False), lower_lane(in0, True), rounds)
    ends, sums = rounds.finish("ends"), rounds.finish("small")
    quarters = rounds.finish("wide1")
    body = 2 * inner + 2 * Q
    out0 = [jnp.where(p == 0, a, b[:, body:]) for a, b in zip(out0, quarters)]
    others = [jnp.where(p == 0, a, b).astype(F32) for a, b in zip(in0[2:], quarters[2:])]
    in0 = [jnp.where(p == 0, a, b[:, :body]) for a, b in zip(in0[:2], quarters)]

    def columns_of(first, size):
        return [a[:, first : first + size].astype(F32) for a in in0]

    g_out = jnp.concatenate(out0, axis=1).astype(F32).T
    g_zx = jnp.stack([jnp.concatenate(columns_of(k * inner, inner), axis=1) for k in range(2)], axis=1)
    g_bc = jnp.concatenate([a + b for a, b in zip(columns_of(2 * inner, Q), others)], axis=1)
    g_dt = jnp.concatenate(columns_of(2 * inner + Q, heads), axis=1)
    sums = lax.dynamic_index_in_dim(sums, p, 2, keepdims=False)
    both_p = sums.sum(axis=(0, 1))
    g_ng = both_p[16:18].reshape(1, width)
    g_cbc = both_p[8:13, inner - GW :][None]
    own = lax.dynamic_index_in_dim(sums, t, 0, keepdims=False)
    g_cx = jnp.concatenate([own[0, :5], own[1, :5]], axis=1)[None]
    g_dsk = own[:, 5].reshape(1, 2 * heads, HS).sum(axis=2)
    g_gain = own[:, 6].reshape(1, half)
    g_dtb, g_alog = (own[:, row, inner - GW : inner - GW + heads].reshape(1, 2 * heads) for row in (13, 14))
    return (ends, g_ng, g_zx[None], g_bc[None], g_dt[None], g_cx, g_cbc, g_dtb, g_alog, g_dsk, g_gain, g_out[None])


def solution(mesh):
    pipe, both, wide = ("pipe", "dp", "tensor"), ("pipe", "tensor"), P("pipe", None, "tensor")
    return jax.shard_map(
        local, mesh=mesh,
        in_specs=(P(*pipe), P("pipe", None), P("pipe", "dp", None, "tensor"), P("pipe", "dp", None), P(*pipe), wide,
                  P("pipe", None, None), P(*both), P(*both), P(*both), P(*both), P("pipe", "tensor", "dp")),
        out_specs=(P(*pipe), P("pipe", None), P("pipe", "dp", None, "tensor"), P("pipe", "dp", None), P(*pipe), wide,
                   P("pipe", None, None), P(*both), P(*both), P(*both), P(*both), P("pipe", "tensor", "dp")),
        check_vma=False,
    )
```
